32 devices in a mesh: fsdp: 8 (over z, y), seq: 4 (over x, core).
Axes of the slice: x: 2, y: 2, z: 4, core: 2. Of those that a mesh axis runs over, the one named last changes fastest.
Arguments:
- layer_input: bfloat16 [4096, 2048], P(('fsdp', 'seq')), may hold values from -6 to 6
- segment_ids: int32 [8, 512], P('fsdp'), may hold values from 0 to 7, as said below
- positions: int32 [4096], P('fsdp'), may hold values from 0 to 766, as said below
- ln1_gain: bfloat16 [2048], P(('fsdp', 'seq')), may hold values from 0.5 to 1.5
- ln1_bias: bfloat16 [2048], P(('fsdp', 'seq')), may hold values from -4 to 4
- qkv_weight: bfloat16 [2048, 6144], P(('fsdp', 'seq')), may hold values from -0.125 to 0.125
- qkv_bias: bfloat16 [6144], P(('fsdp', 'seq')), may hold values from -6 to 6
- out_weight: bfloat16 [2048, 2048], P(('fsdp', 'seq')), may hold values from -0.75 to 0.75
- ln2_gain: bfloat16 [2048], P(('fsdp', 'seq')), may hold values from 0.5 to 1.5
- ln2_bias: bfloat16 [2048], P(('fsdp', 'seq')), may hold values from -4 to 4
- gate_weight: bfloat16 [2048, 5632], P(('fsdp', 'seq')), may hold values from -0.125 to 0.125
- up_weight: bfloat16 [2048, 5632], P(('fsdp', 'seq')), may hold values from -0.125 to 0.125
- down_weight: bfloat16 [2048, 5632], P(('fsdp', 'seq')), may hold values from -0.078125 to 0.078125
- cotangent: bfloat16 [4096, 2048], P(('fsdp', 'seq')), may hold values from -6 to 6
Outputs:
- layer_output: bfloat16 [4096, 2048], P(('fsdp', 'seq'))
- input_grad: float32 [4096, 2048], P(('fsdp', 'seq'))
- ln1_gain_grad: float32 [2048], P(('fsdp', 'seq'))
- ln1_bias_grad: float32 [2048], P(('fsdp', 'seq'))
- qkv_weight_grad: float32 [2048, 6144], P(('fsdp', 'seq'))
- qkv_bias_grad: float32 [6144], P(('fsdp', 'seq'))
- out_weight_grad: float32 [2048, 2048], P(('fsdp', 'seq'))
- ln2_gain_grad: float32 [2048], P(('fsdp', 'seq'))
- ln2_bias_grad: float32 [2048], P(('fsdp', 'seq'))
- gate_weight_grad: float32 [2048, 5632], P(('fsdp', 'seq'))
- up_weight_grad: float32 [2048, 5632], P(('fsdp', 'seq'))
- down_weight_grad: float32 [2048, 5632], P(('fsdp', 'seq'))
The draws below stay inside these ranges and needn't reach their ends.
Inputs may be any that keep to these rules, and one draw needn't show every extreme that they name: `segment_ids`: segment ids never fall along a sequence; each document holds 64 to 256 tokens, the first and last of a sequence may be cut. `positions`: A token's position counts from its document's first token, which for a sequence's first document may lie up to 511 tokens before the sequence.
All inputs are finite; a program needn't handle non-finite values.
Results may differ from the reference program's by a relative error of at most 0.012.
Values may be sent and summed in bfloat16 or wider, within the bound.
No kernel may reach another device: no remote copies, remote signals or barrier semaphores. Data moves between devices by JAX's collectives and lax.ppermute only.
A program may use at most 256 MiB of HBM per device.

```python
import jax
import jax.numpy as jnp
from jax import lax

D = 2048
HEADS = 32
HEAD_DIM = 64
FF = 5632
SEQ_LEN = 512
SEQS = 8
TOKENS = 4096


def document_layout(key):
    inner = jax.random.fold_in(key, 11)
    key_len, key_first = jax.random.split(inner)
    lengths = jax.random.randint(key_len, (SEQS, 16), SEQ_LEN // 8, SEQ_LEN // 2 + 1)
    first = jax.random.randint(key_first, (SEQS, 1), 0, SEQ_LEN)
    seq_row = jnp.arange(SEQS)[:, None]
    doc_col = jnp.arange(16)[None, :]
    lengths = jnp.where(seq_row == SEQS - 1, SEQ_LEN // 8, lengths)
    lengths = jnp.where((seq_row == 0) & (doc_col == 0), SEQ_LEN // 2, lengths)
    first = jnp.where(seq_row == 0, SEQ_LEN - 1, first)
    ends = jnp.cumsum(lengths, axis=1)
    index = jnp.arange(SEQ_LEN)
    segment = jnp.sum((ends[:, None, :] <= index[None, :, None]).astype(jnp.int32), axis=-1)
    starts = jnp.concatenate([-first, ends], axis=1)
    begin = jnp.take_along_axis(starts, segment, axis=1)
    return (segment.astype(jnp.int32), (index[None, :] - begin).astype(jnp.int32))


def draw_segment_ids(key, part):
    return document_layout(key)[0]


def draw_positions(key, part):
    return document_layout(key)[1].reshape(TOKENS)


def raised(entries, stream_key, source, target, blocks, factor):
    def block_of(position):
        return (jnp.arange(entries.shape[position]) // (entries.shape[position] // blocks)).reshape((-1,) + (1,) * (entries.ndim - 1 - position))

    first = jax.random.permutation(stream_key, blocks)[block_of(target)]
    second = (block_of(target) + blocks // 2) % blocks
    return jnp.where((block_of(source) == first) | (block_of(source) == second), factor * entries, entries)


def level_of(rng, dims, cuts, low, high):
    def one(position, parts):
        draws = jax.random.uniform(jax.random.fold_in(jax.random.fold_in(rng, 6), position), (parts,), jnp.float32, low / len(cuts), high / len(cuts))
        return jnp.repeat(jnp.exp(draws), dims[position] // parts).reshape((-1,) + (1,) * (len(dims) - position - 1))

    factor_of = one(*cuts[0])
    for cut in cuts[1:]:
        factor_of = factor_of * one(*cut)
    return factor_of


def normal_values(stream_key, dims, scale, limit, cuts=(), dtype=jnp.bfloat16):
    factor_of = level_of(stream_key, dims, cuts, -0.22, 0.18) if cuts else 1.0
    values = jax.random.normal(stream_key, dims, jnp.float32) * scale * factor_of
    return jnp.minimum(jnp.maximum(values, -limit), limit).astype(dtype)


def noise_with(key, shape, width, reach, shards, heavy, kind=jnp.bfloat16):
    array = width * jax.random.normal(key, shape, jnp.float32)
    if shards:
        array = array * level_of(key, shape, shards, -0.22, 0.18)
    return jnp.clip(raised(array, jax.random.fold_in(key, 3), *heavy), -reach, reach).astype(kind)


def setup_inputs(seed: int = 0) -> dict:
    key_of = jax.random.split(jax.random.key(seed), 15)
    return {
        "layer_input": normal_values(key_of[0], (TOKENS, D), 1.0, 6.0, ((0, 32),)),
        "segment_ids": draw_segment_ids(jax.random.fold_in(key_of[14], 71), 0),
        "positions": draw_positions(jax.random.fold_in(key_of[14], 71), 0),
        "ln1_gain": jnp.clip(1.0 + 0.1 * jax.random.normal(key_of[3], (D,), jnp.float32), 0.5, 1.5).astype(jnp.bfloat16),
        "ln1_bias": normal_values(key_of[4], (D,), 0.3, 4.0, ((0, 32),)),
        "qkv_weight": normal_values(key_of[5], (D, 3 * D), D ** -0.5, 0.125, ((0, 32),)),
        "qkv_bias": normal_values(key_of[6], (3 * D,), 0.5, 6.0, ((0, 32),)),
        "out_weight": normal_values(key_of[7], (D, D), (D // 32) ** -0.5, 0.75, ((0, 32),)),
        "ln2_gain": jnp.clip(1.0 + 0.1 * jax.random.normal(key_of[8], (D,), jnp.float32), 0.5, 1.5).astype(jnp.bfloat16),
        "ln2_bias": normal_values(key_of[9], (D,), 0.3, 4.0, ((0, 32),)),
        "gate_weight": normal_values(key_of[10], (D, FF), D ** -0.5, 0.125, ((0, 32),)),
        "up_weight": normal_values(key_of[11], (D, FF), D ** -0.5, 0.125, ((0, 32),)),
        "down_weight": normal_values(key_of[12], (D, FF), FF ** -0.5, 0.078125, ((0, 32),)),
        "cotangent": noise_with(key_of[13], (TOKENS, D), 1.0, 6.0, ((0, 32),), (0, 1, 32, 2.75)),
    }


@jax.custom_vjp
def low(v):
    return lax.optimization_barrier(v.astype(jnp.bfloat16)).astype(jnp.float32)

@jax.custom_vjp
def low_back(v):
    return v

def low_keep(v):
    return (low(v), None)

def low_pass(kept, grad):
    return (grad,)

def back_keep(v):
    return (v, None)

def back_low(kept, grad):
    return (low(grad),)
low.defvjp(low_keep, low_pass)
low_back.defvjp(back_keep, back_low)

def matmul(left, right):
    return jnp.dot(left, right, precision=lax.Precision.HIGHEST)

def layer_norm(values, gain, shift):
    center = lax.optimization_barrier(jnp.mean(values, axis=-1, keepdims=True))
    centered = values - center
    spread = lax.optimization_barrier(jnp.mean(centered * centered, axis=-1, keepdims=True))
    return centered * lax.rsqrt(spread + 1e-05) * gain + shift

def rotary_tables(spots):
    inverse = 10000.0 ** (-jnp.arange(8).astype(jnp.float32) / 8.0)
    angle = spots.astype(jnp.float32)[:, None] * inverse[None, :]
    return (jnp.cos(angle), jnp.sin(angle))

def rotate(heads_view, cosine, sine):
    first = heads_view[..., :8]
    second = heads_view[..., 8:16]
    rest = heads_view[..., 16:]
    cos_part = cosine[:, None, :]
    sin_part = sine[:, None, :]
    return jnp.concatenate([first * cos_part - second * sin_part, second * cos_part + first * sin_part, rest], axis=-1)

def one_sequence(params, inputs):
    ln1_g, ln1_b, w_qkv, b_qkv, w_out, ln2_g, ln2_b, w_gate, w_up, w_down = params
    rows, segment, spots = inputs
    length = rows.shape[0]
    normed = low(layer_norm(rows, ln1_g, ln1_b))
    mixed = low_back(matmul(normed, w_qkv) + b_qkv)
    cosine, sine = rotary_tables(spots)
    query = low(rotate(mixed[:, :D].reshape(length, HEADS, HEAD_DIM), cosine, sine))
    keys = low(rotate(mixed[:, D:2 * D].reshape(length, HEADS, HEAD_DIM), cosine, sine))
    values = low(mixed[:, 2 * D:].reshape(length, HEADS, HEAD_DIM))
    scores = low_back(jnp.einsum('qhd,khd->hqk', query, keys, precision=lax.Precision.HIGHEST) * 0.125)
    index = jnp.arange(length)
    allowed = (segment[:, None] == segment[None, :]) & (index[None, :] <= index[:, None])
    scores = jnp.where(allowed[None], scores, -1e+30)
    probs = low(jax.nn.softmax(scores, axis=-1))
    attended = jnp.einsum('hqk,khd->qhd', probs, values, precision=lax.Precision.HIGHEST).reshape(length, D)
    attended = low(low_back(attended))
    hidden = rows + low_back(matmul(attended, w_out.T))
    normed2 = low(layer_norm(hidden, ln2_g, ln2_b))
    gate = low_back(matmul(normed2, w_gate))
    up = low_back(matmul(normed2, w_up))
    inner = low(jax.nn.silu(gate) * up)
    return hidden + matmul(inner, w_down.T)

def reference(layer_input, segment_ids, positions, ln1_gain, ln1_bias, qkv_weight, qkv_bias, out_weight, ln2_gain, ln2_bias, gate_weight, up_weight, down_weight, cotangent):
    params = (ln1_gain.astype(jnp.float32), ln1_bias.astype(jnp.float32), qkv_weight.astype(jnp.float32), qkv_bias.astype(jnp.float32), out_weight.astype(jnp.float32), ln2_gain.astype(jnp.float32), ln2_bias.astype(jnp.float32), gate_weight.astype(jnp.float32), up_weight.astype(jnp.float32), down_weight.astype(jnp.float32))
    rows = layer_input.astype(jnp.float32).reshape(SEQS, SEQ_LEN, D)
    spots = positions.reshape(SEQS, SEQ_LEN)
    step = jax.checkpoint(one_sequence)

    def forward(all_rows, weights):
        return lax.map(lambda inputs: step(weights, inputs), (all_rows, segment_ids, spots))
    result, pullback = jax.vjp(forward, rows, params)
    row_grad, grads = pullback(cotangent.astype(jnp.float32).reshape(SEQS, SEQ_LEN, D))
    g_ln1, b_ln1, g_qkv, g_bias, g_out, g_ln2, b_ln2, g_gate, g_up, g_down = grads
    return (result.reshape(TOKENS, D).astype(jnp.bfloat16), row_grad.reshape(TOKENS, D), g_ln1, b_ln1, g_qkv, g_bias, g_out, g_ln2, b_ln2, g_gate, g_up, g_down)
```

```python
import jax
import jax.numpy as jnp
from jax import lax
from jax.sharding import PartitionSpec as P

HEADS = 32
HEAD_DIM = 64
AXES = ("fsdp", "seq")
F32 = jnp.float32
BF16 = jnp.bfloat16


def layer_norm(values, gain, shift):
    center = jnp.mean(values, axis=-1, keepdims=True)
    centered = values - center
    spread = jnp.mean(centered * centered, axis=-1, keepdims=True)
    return centered * lax.rsqrt(spread + 1e-05) * gain + shift


def norm_back(values, gain, grad):
    center = jnp.mean(values, axis=-1, keepdims=True)
    centered = values - center
    scale = lax.rsqrt(jnp.mean(centered * centered, axis=-1, keepdims=True) + 1e-05)
    hat = centered * scale
    lifted = grad * gain
    inner = jnp.mean(lifted * hat, axis=-1, keepdims=True)
    pulled = scale * (lifted - jnp.mean(lifted, axis=-1, keepdims=True) - hat * inner)
    return pulled, jnp.sum(grad * hat, axis=0), jnp.sum(grad, axis=0)


def rotary_tables(spots):
    inverse = 10000.0 ** (-jnp.arange(8).astype(F32) / 8.0)
    angle = spots.astype(F32)[..., None] * inverse
    return jnp.cos(angle), jnp.sin(angle)


def rotate(view, cosine, sine):
    first = view[..., :8]
    second = view[..., 8:16]
    rest = view[..., 16:]
    return jnp.concatenate(
        [first * cosine - second * sine, second * cosine + first * sine, rest], axis=-1
    )


def dot_rows(left, right, kind=F32):
    return lax.dot_general(
        left, right, (((0,), (0,)), ((), ())), preferred_element_type=F32
    ).astype(kind)


def dot_cols(left, right, kind=F32):
    return lax.dot_general(
        left, right, (((1,), (1,)), ((), ())), preferred_element_type=F32
    ).astype(kind)


def dot(left, right):
    return jnp.dot(left, right, preferred_element_type=F32)


class Places:
    def __init__(self):
        self.fsdp = lax.axis_size("fsdp")
        self.seq = lax.axis_size("seq")
        self.count = self.fsdp * self.seq
        self.outer = self.fsdp // 4
        spot = lax.axis_index("fsdp")
        side = lax.axis_index("seq")
        self.a = spot // 4
        self.b = (spot // 2) % 2
        self.e = spot % 2
        self.x = side // 2
        self.c = side % 2

    def flip(self, values, c=0, x=0, e=0, b=0):
        mask = c + 2 * x + self.seq * (e + 2 * b)
        return lax.ppermute(values, AXES, [(i, i ^ mask) for i in range(self.count)])

    def shift(self, values, steps):
        stride = 4 * self.seq
        return lax.ppermute(
            values, AXES, [((i + steps * stride) % self.count, i) for i in range(self.count)]
        )

    def push(self, values, steps):
        stride = 4 * self.seq
        return lax.ppermute(
            values, AXES, [(i, (i + steps * stride) % self.count) for i in range(self.count)]
        )


def pick(bit, first, second):
    return jnp.where(bit == 0, first, second)


def joined(bit, own, other, axis):
    return pick(
        bit, jnp.concatenate([own, other], axis=axis), jnp.concatenate([other, own], axis=axis)
    )


def to_relative(at, values):
    width = values.shape[-1] // (at.outer * 4)
    parts = []
    for i in range(at.outer):
        for j in range(2):
            for k in range(2):
                spot = (((at.a + i) % at.outer) * 2 + k) * 2 + (at.e ^ j)
                parts.append(
                    lax.dynamic_slice_in_dim(values, spot * width, width, values.ndim - 1)
                )
    return jnp.concatenate(parts, axis=-1)


def to_absolute(at, values):
    width = values.shape[-1] // (at.outer * 4)
    parts = []
    for i in range(at.outer):
        for k in range(2):
            for j in range(2):
                spot = (((i - at.a) % at.outer) * 2 + (at.e ^ j)) * 2 + k
                parts.append(
                    lax.dynamic_slice_in_dim(values, spot * width, width, values.ndim - 1)
                )
    return jnp.concatenate(parts, axis=-1)


def gather_tokens(at, values):
    near = [
        values,
        at.flip(values, x=1),
        at.flip(values, b=1),
        at.flip(values, x=1, b=1),
    ]
    return jnp.concatenate(near + [at.flip(v, c=1) for v in near], axis=0)


def sum_tokens(at, own, other):
    total = own + at.flip(other, c=1).astype(F32)
    rows = total.shape[0] // 4
    far = total[rows:].astype(BF16)
    out = total[:rows]
    out = out + at.flip(far[:rows], x=1).astype(F32)
    out = out + at.flip(far[rows : 2 * rows], b=1).astype(F32)
    out = out + at.flip(far[2 * rows :], x=1, b=1).astype(F32)
    return out


def fetch(at, weights, parts):
    pieces = []
    for w, n in zip(weights, parts):
        width = w.shape[1] // (8 * n)
        for p in range(n):
            pieces.append(
                [w[:, (p * 8 + j) * width : (p * 8 + j + 1) * width] for j in range(8)]
            )
    def half(side):
        return jnp.concatenate(
            [
                pick(side, piece[2 * g], piece[2 * g + 1])
                for g in range(4)
                for piece in pieces
            ],
            axis=1,
        )

    block = joined(at.c, half(at.c), at.flip(half(1 - at.c), c=1), 0)
    wide = block.shape[1] // 4
    quarter = [block[:, i * wide : (i + 1) * wide] for i in range(4)]
    def side_of(side):
        return jnp.concatenate(
            [pick(side, quarter[0], quarter[1]), pick(side, quarter[2], quarter[3])], axis=1
        )

    block = joined(at.x, side_of(at.x), at.flip(side_of(1 - at.x), x=1), 0)
    low, high = block[:, :wide], block[:, wide:]
    block = joined(at.b, pick(at.b, low, high), at.flip(pick(at.b, high, low), b=1), 0)
    blocks = []
    for i in range(at.outer):
        here = block if i == 0 else at.shift(block, i)
        blocks.append(here)
        blocks.append(at.flip(here, e=1))
    return blocks


def deliver(at, make, parts):
    outer = at.outer
    sent = [at.flip(make(2 * i + 1, BF16), e=1) for i in range(outer)]
    total = None
    for i in list(range(1, outer)) + [0]:
        here = make(2 * i, F32) + sent[i].astype(F32)
        if i:
            here = at.push(here.astype(BF16), i).astype(F32)
        total = here if total is None else total + here
    block = total.astype(BF16)
    rows = block.shape[0] // 2
    low, high = block[:rows], block[rows:]
    block = joined(at.b, pick(at.b, low, high), at.flip(pick(at.b, high, low), b=1), 1)
    rows = rows // 2
    low, high = block[:rows], block[rows:]
    own, other = pick(at.x, low, high), at.flip(pick(at.x, high, low), x=1)
    wide = own.shape[1] // 2
    block = jnp.concatenate(
        [
            joined(at.x, own[:, :wide], other[:, :wide], 1),
            joined(at.x, own[:, wide:], other[:, wide:], 1),
        ],
        axis=1,
    )
    rows = rows // 2
    low, high = block[:rows], block[rows:]
    own, other = pick(at.c, low, high), at.flip(pick(at.c, high, low), c=1)
    width = wide // parts
    outs = []
    for p in range(parts):
        cols = []
        for g in range(4):
            at_col = (g * parts + p) * width
            cols.append(
                joined(
                    at.c,
                    own[:, at_col : at_col + width].astype(F32),
                    other[:, at_col : at_col + width].astype(F32),
                    1,
                )
            )
        outs.append(jnp.concatenate(cols, axis=1))
    return outs


def fetch_small(at, values):
    block = values[None]
    block = joined(at.c, block, at.flip(block, c=1), 0)
    block = joined(at.x, block, at.flip(block, x=1), 0)
    block = joined(at.b, block, at.flip(block, b=1), 0)
    whole = jnp.stack([block] + [at.shift(block, i) for i in range(1, at.outer)])
    return jnp.stack([whole, at.flip(whole, e=1)], axis=1)


def deliver_small(at, values):
    whole = values[:, 0] + at.flip(values[:, 1], e=1)
    block = whole[0]
    for i in range(1, at.outer):
        block = block + at.push(whole[i], i)
    for bit, name in ((at.b, "b"), (at.x, "x"), (at.c, "c")):
        rows = block.shape[0] // 2
        low, high = block[:rows], block[rows:]
        block = pick(bit, low, high) + at.flip(pick(bit, high, low), **{name: 1})
    return block[0]


def order_tokens(at, values):
    seqs, length = values.shape
    view = values.reshape(seqs, 2, 2, length // 4)
    view = pick(at.x, view, view[:, ::-1])
    view = pick(at.c, view, view[:, :, ::-1])
    return jnp.swapaxes(view, 1, 2).reshape(seqs, length)


def body(
    layer_input,
    segment_ids,
    positions,
    ln1_gain,
    ln1_bias,
    qkv_weight,
    qkv_bias,
    out_weight,
    ln2_gain,
    ln2_bias,
    gate_weight,
    up_weight,
    down_weight,
    cotangent,
):
    at = Places()
    width = layer_input.shape[1]
    rows = qkv_weight.shape[0]
    bias_rows = qkv_bias.shape[0]
    length = segment_ids.shape[1]
    heads_here = HEADS // 8
    part = width // 8
    units = gate_weight.shape[1] // 8
    step = width // (2 * at.outer)
    slot = at.b * 4 + at.x * 2 + at.c

    inputs_low = to_relative(at, layer_input)
    inputs = inputs_low.astype(F32)
    inputs_all = gather_tokens(at, inputs_low)
    qkv_blocks = fetch(at, [qkv_weight], [3])
    small = fetch_small(
        at, jnp.concatenate([qkv_bias, ln1_gain, ln1_bias, ln2_gain, ln2_bias])
    )
    spots = jnp.concatenate([segment_ids, positions[None]], axis=0)
    spots = jnp.stack([spots, at.flip(spots, b=1)])
    segments = order_tokens(at, spots[:, 0])
    places = order_tokens(at, spots[:, 1])
    index = order_tokens(at, jnp.arange(length)[None])[0]

    def vector(i):
        start = bias_rows + i * rows
        return small[..., start : start + rows].reshape(width).astype(F32)

    gain_one, shift_one, gain_two, shift_two = (vector(i) for i in range(4))
    bias = small[..., :bias_rows]
    bias = pick(at.e, bias, bias[:, ::-1])
    bias = jnp.roll(bias, at.a, axis=0)
    bias = bias.reshape(at.outer, 2, 2, 4, bias_rows).swapaxes(1, 2).reshape(3, 8, part)
    bias = lax.dynamic_index_in_dim(bias, slot, 1, keepdims=False).reshape(3 * part).astype(F32)

    def cut(values, i):
        return values[:, i * step : (i + 1) * step]

    def contract(values, blocks):
        total = dot(cut(values, 0), blocks[0])
        for i in range(1, len(blocks)):
            total = total + dot(cut(values, i), blocks[i])
        return total

    def expand(values, blocks):
        half = values.shape[0] // 2
        other = jnp.concatenate([dot_cols(values[half:], w, BF16) for w in blocks], axis=1)
        own = jnp.concatenate([dot_cols(values[:half], w) for w in blocks], axis=1)
        return sum_tokens(at, own, other)

    def by_sequence(values, n):
        view = values.reshape(2, 2, length // 2, n, HEAD_DIM)
        return view.transpose(1, 3, 0, 2, 4).reshape(2, n, length, HEAD_DIM)

    def by_token(values):
        n = values.shape[1]
        view = values.reshape(2, n, 2, length // 2, HEAD_DIM)
        return view.transpose(2, 0, 3, 1, 4).reshape(2 * length, n * HEAD_DIM)

    normed_all = layer_norm(inputs_all.astype(F32), gain_one, shift_one).astype(BF16)
    mixed = contract(normed_all, qkv_blocks) + bias
    cosine, sine = rotary_tables(places)
    cosine, sine = cosine[:, None], sine[:, None]
    query = rotate(by_sequence(mixed[:, :part], heads_here), cosine, sine).astype(BF16)
    key = rotate(by_sequence(mixed[:, part : 2 * part], heads_here), cosine, sine).astype(BF16)
    value = by_sequence(mixed[:, 2 * part :], heads_here).astype(BF16)
    allowed = (segments[:, :, None] == segments[:, None, :]) & (
        index[None, None, :] <= index[None, :, None]
    )
    scores = jnp.einsum("bhtd,bhld->bhtl", query, key, preferred_element_type=F32) * 0.125
    scores = jnp.where(allowed[:, None], scores, -1e30)
    top = jnp.max(scores, axis=-1, keepdims=True)
    expo = jnp.exp(scores - top)
    total = jnp.sum(expo, axis=-1, keepdims=True)
    probs = expo / total
    probs_low = probs.astype(BF16)
    attended = by_token(
        jnp.einsum("bhtl,bhld->bhtd", probs_low, value, preferred_element_type=F32)
    ).astype(BF16)

    out_blocks = fetch(at, [out_weight], [1])
    hidden = inputs + expand(attended, out_blocks)
    normed2 = layer_norm(hidden, gain_two, shift_two).astype(BF16)
    normed2_all = gather_tokens(at, normed2)
    pair_blocks = fetch(at, [gate_weight, up_weight], [1, 1])
    cotangent_low = to_relative(at, cotangent)
    cotangent_all = gather_tokens(at, cotangent_low)
    down_blocks = fetch(at, [down_weight], [1])

    gate_up = contract(normed2_all, pair_blocks)
    gate = gate_up[:, :units]
    up = gate_up[:, units:]
    sigmoid = 1.0 / (1.0 + jnp.exp(-gate))
    silu = gate * sigmoid
    inner = (silu * up).astype(BF16)
    down_grads = deliver(
        at, lambda i, kind: dot_rows(cut(cotangent_all, i), inner, kind), 1
    )
    inner_grad = contract(cotangent_all, down_blocks)
    gate_grad = inner_grad * up * sigmoid * (1.0 + gate * (1.0 - sigmoid))
    up_grad = inner_grad * silu
    pair_low = jnp.concatenate([gate_grad.astype(BF16), up_grad.astype(BF16)], axis=1)
    normed2_grad = expand(pair_low, pair_blocks)
    pair_grads = deliver(
        at, lambda i, kind: dot_rows(cut(normed2_all, i), pair_low, kind), 2
    )
    result = to_absolute(at, hidden + expand(inner, down_blocks))

    hidden_part, gain_two_grad, shift_two_grad = norm_back(hidden, gain_two, normed2_grad)
    hidden_grad = cotangent_low.astype(F32) + hidden_part
    branch_all = gather_tokens(at, hidden_grad.astype(BF16))
    attended_grad = by_sequence(contract(branch_all, out_blocks), heads_here).astype(BF16)
    out_grads = deliver(
        at, lambda i, kind: dot_rows(cut(branch_all, i), attended, kind), 1
    )
    value_grad = jnp.einsum(
        "bhtl,bhtd->bhld", probs_low, attended_grad, preferred_element_type=F32
    )
    probs_grad = jnp.einsum(
        "bhtd,bhld->bhtl", attended_grad, value, preferred_element_type=F32
    )
    center = jnp.sum(probs * probs_grad, axis=-1, keepdims=True)
    scores_low = (probs * (probs_grad - center)).astype(BF16)
    query_grad = (
        jnp.einsum("bhtl,bhld->bhtd", scores_low, key, preferred_element_type=F32) * 0.125
    )
    key_grad = (
        jnp.einsum("bhtl,bhtd->bhld", scores_low, query, preferred_element_type=F32) * 0.125
    )
    mixed_low = jnp.concatenate(
        [
            by_token(rotate(query_grad, cosine, -sine)),
            by_token(rotate(key_grad, cosine, -sine)),
            by_token(value_grad),
        ],
        axis=1,
    ).astype(BF16)
    qkv_grads = deliver(
        at, lambda i, kind: dot_rows(cut(normed_all, i), mixed_low, kind), 3
    )
    normed_grad = expand(mixed_low, qkv_blocks)
    input_part, gain_one_grad, shift_one_grad = norm_back(inputs, gain_one, normed_grad)
    input_grad = to_absolute(at, hidden_grad + input_part)

    bias_part = jnp.sum(mixed_low.astype(F32), axis=0).reshape(3, 1, part)
    own_slot = (jnp.arange(8) == slot).astype(F32)[None, :, None]
    bias_whole = (bias_part * own_slot).reshape(at.outer, 2, 2, 4, bias_rows).swapaxes(1, 2)
    bias_whole = jnp.roll(bias_whole, -at.a, axis=0)
    bias_whole = pick(at.e, bias_whole, bias_whole[:, ::-1]).reshape(at.outer, 2, 8, bias_rows)
    grads = [
        v.reshape(at.outer, 2, 8, rows)
        for v in (gain_one_grad, shift_one_grad, gain_two_grad, shift_two_grad)
    ]
    shares = deliver_small(at, jnp.concatenate([bias_whole] + grads, axis=-1))

    def share(i):
        return shares[bias_rows + i * rows : bias_rows + (i + 1) * rows]

    return (
        result.astype(BF16),
        input_grad,
        share(0),
        share(1),
        jnp.concatenate(qkv_grads, axis=1),
        shares[:bias_rows],
        out_grads[0],
        share(2),
        share(3),
        pair_grads[0],
        pair_grads[1],
        down_grads[0],
    )


def solution(mesh):
    both = ("fsdp", "seq")
    wide = P(both, None)
    flat = P(both)
    return jax.shard_map(
        body,
        mesh=mesh,
        in_specs=(
            wide, P("fsdp", None), P("fsdp"), flat, flat, wide, flat,
            wide, flat, flat, wide, wide, wide, wide,
        ),
        out_specs=(wide, wide, flat, flat, wide, flat, wide, flat, flat, wide, wide, wide),
        check_vma=False,
    )
```

```python
import functools
import math

import jax
import jax.numpy as jnp
from jax import lax
from jax.experimental import pallas as pl
from jax.experimental.pallas import tpu as pltpu
from jax.sharding import PartitionSpec as P

HEADS = 32
HEAD_DIM = 64
AXES = ("fsdp", "seq")
F32 = jnp.float32
BF16 = jnp.bfloat16


def layer_norm(values, gain, shift):
    center = jnp.mean(values, axis=-1, keepdims=True)
    centered = values - center
    spread = jnp.mean(centered * centered, axis=-1, keepdims=True)
    return centered * lax.rsqrt(spread + 1e-05) * gain + shift


def norm_back(values, gain, grad):
    center = jnp.mean(values, axis=-1, keepdims=True)
    centered = values - center
    scale = lax.rsqrt(jnp.mean(centered * centered, axis=-1, keepdims=True) + 1e-05)
    hat = centered * scale
    lifted = grad * gain
    inner = jnp.mean(lifted * hat, axis=-1, keepdims=True)
    pulled = scale * (lifted - jnp.mean(lifted, axis=-1, keepdims=True) - hat * inner)
    return pulled, jnp.sum(grad * hat, axis=0), jnp.sum(grad, axis=0)


def rotary_tables(spots):
    inverse = 10000.0 ** (-jnp.arange(8).astype(F32) / 8.0)
    angle = spots.astype(F32)[..., None] * inverse
    return jnp.cos(angle), jnp.sin(angle)


def rotate(view, cosine, sine):
    first = view[..., :8]
    second = view[..., 8:16]
    rest = view[..., 16:]
    return jnp.concatenate(
        [first * cosine - second * sine, second * cosine + first * sine, rest], axis=-1
    )


def dot_rows(left, right, kind=F32):
    return lax.dot_general(
        left, right, (((0,), (0,)), ((), ())), preferred_element_type=F32
    ).astype(kind)


def dot_cols(left, right, kind=F32):
    return lax.dot_general(
        left, right, (((1,), (1,)), ((), ())), preferred_element_type=F32
    ).astype(kind)


def dot(left, right):
    return jnp.dot(left, right, preferred_element_type=F32)


class Places:
    def __init__(self):
        self.fsdp = lax.axis_size("fsdp")
        self.seq = lax.axis_size("seq")
        self.count = self.fsdp * self.seq
        self.outer = self.fsdp // 4
        spot = lax.axis_index("fsdp")
        side = lax.axis_index("seq")
        self.a = spot // 4
        self.b = (spot // 2) % 2
        self.e = spot % 2
        self.x = side // 2
        self.c = side % 2
        self.slot = jnp.reshape(self.b * 4 + side, (1,)).astype(jnp.int32)

    def flip(self, values, c=0, x=0, e=0, b=0):
        mask = c + 2 * x + self.seq * (e + 2 * b)
        return lax.ppermute(values, AXES, [(i, i ^ mask) for i in range(self.count)])

    def shift(self, values, steps):
        stride = 4 * self.seq
        return lax.ppermute(
            values, AXES, [((i + steps * stride) % self.count, i) for i in range(self.count)]
        )

    def push(self, values, steps):
        stride = 4 * self.seq
        return lax.ppermute(
            values, AXES, [(i, (i + steps * stride) % self.count) for i in range(self.count)]
        )


def pick(bit, first, second):
    return jnp.where(bit == 0, first, second)


def joined(bit, own, other, axis):
    return pick(
        bit, jnp.concatenate([own, other], axis=axis), jnp.concatenate([other, own], axis=axis)
    )


def order_kernel(width, spots_ref, *refs):
    half = len(refs) // 2
    for ref, out in zip(refs[:half], refs[half:]):
        for i in range(ref.shape[1] // width):
            start = pl.multiple_of(spots_ref[i] * width, 128)
            out[:, i * width : (i + 1) * width] = ref[:, pl.ds(start, width)]


def reorder(spots, arrays):
    width = arrays[0].shape[1] // len(spots)
    if width % 128:
        return [
            jnp.concatenate(
                [lax.dynamic_slice_in_dim(v, spot * width, width, 1) for spot in spots], axis=1
            )
            for v in arrays
        ]
    order = jnp.stack(spots).astype(jnp.int32)
    outs = [(v.shape, v.dtype) for v in arrays]
    return call(functools.partial(order_kernel, width), outs, order, *arrays)


def to_relative(at, *arrays):
    spots = [
        (((at.a + i) % at.outer) * 2 + k) * 2 + (at.e ^ j)
        for i in range(at.outer)
        for j in range(2)
        for k in range(2)
    ]
    return reorder(spots, arrays)


def to_absolute(at, *arrays):
    spots = [
        (((i - at.a) % at.outer) * 2 + (at.e ^ j)) * 2 + k
        for i in range(at.outer)
        for k in range(2)
        for j in range(2)
    ]
    return reorder(spots, arrays)


def gather_tokens(at, values):
    near = [
        values,
        at.flip(values, x=1),
        at.flip(values, b=1),
        at.flip(values, x=1, b=1),
    ]
    return jnp.concatenate(near + [at.flip(v, c=1) for v in near], axis=0)


def sum_tokens(at, own, other):
    total = own + at.flip(other, c=1).astype(F32)
    rows = total.shape[0] // 4
    far = total[rows:].astype(BF16)
    out = total[:rows]
    out = out + at.flip(far[:rows], x=1).astype(F32)
    out = out + at.flip(far[rows : 2 * rows], b=1).astype(F32)
    out = out + at.flip(far[2 * rows :], x=1, b=1).astype(F32)
    return out


def call(kernel, outs, *args, flops=0):
    size = sum(v.size * v.dtype.itemsize for v in args)
    size += sum(math.prod(shape) * jnp.dtype(kind).itemsize for shape, kind in outs)
    specs = [
        pl.BlockSpec(memory_space=pltpu.SMEM if v.dtype == jnp.int32 else pltpu.VMEM)
        for v in args
    ]
    return pl.pallas_call(
        kernel,
        out_shape=[jax.ShapeDtypeStruct(shape, kind) for shape, kind in outs],
        in_specs=specs,
        out_specs=[pl.BlockSpec(memory_space=pltpu.VMEM)] * len(outs),
        compiler_params=pltpu.CompilerParams(vmem_limit_bytes=2 * size + 8 * 2**20),
        cost_estimate=pl.CostEstimate(flops=flops, bytes_accessed=size, transcendentals=0),
    )(*args)


def block_at(ref, part, spot, width):
    return ref[:, pl.ds(pl.multiple_of((part * 8 + spot) * width, 128), width)]


def cut_kernel(parts, slot_ref, *refs):
    slot = slot_ref[0]
    weights, pieces = refs[: len(parts)], refs[len(parts) :]
    col = 0
    for ref, count in zip(weights, parts):
        width = ref.shape[1] // (8 * count)
        for p in range(count):
            if width % 128 == 0:
                for d in range(8):
                    pieces[d][:, col : col + width] = block_at(ref, p, slot ^ d, width)
            else:
                for d in range(0, 8, 2):
                    spot = slot ^ d
                    start = (p * 4 + spot // 2) * 2 * width
                    both = ref[:, pl.ds(pl.multiple_of(start, 128), 2 * width)]
                    even = spot % 2 == 0
                    low, high = both[:, :width], both[:, width:]
                    pieces[d][:, col : col + width] = jnp.where(even, low, high)
                    pieces[d + 1][:, col : col + width] = jnp.where(even, high, low)
            col += width


def place_kernel(slot_ref, *refs):
    slot = slot_ref[0]
    pieces, outs = refs[:8], refs[8:]
    rows = pieces[0].shape[0]
    for d in range(8):
        start = pl.multiple_of((slot ^ d) * rows, rows)
        col = 0
        for out in outs:
            out[pl.ds(start, rows), :] = pieces[d][:, col : col + out.shape[1]]
            col += out.shape[1]


def sum_cut_kernel(count, slot_ref, *refs):
    slot = slot_ref[0]
    terms, pieces = refs[:count], refs[count:]
    rows = pieces[0].shape[0]
    for d in range(8):
        span = pl.ds(pl.multiple_of((slot ^ d) * rows, rows), rows)
        total = terms[0][span, :].astype(F32)
        for term in terms[1:]:
            total = total + term[span, :].astype(F32)
        pieces[d][...] = total.astype(BF16)


def spread_kernel(counts, slot_ref, *refs):
    slot = slot_ref[0]
    pieces, outs = refs[:8], refs[8:]
    col = 0
    for out, count in zip(outs, counts):
        width = out.shape[1] // (8 * count)
        for p in range(count):
            if width % 128 == 0:
                for d in range(8):
                    start = pl.multiple_of((p * 8 + (slot ^ d)) * width, 128)
                    out[:, pl.ds(start, width)] = pieces[d][:, col : col + width].astype(F32)
            else:
                for d in range(0, 8, 2):
                    spot = slot ^ d
                    even = spot % 2 == 0
                    one = pieces[d][:, col : col + width].astype(F32)
                    two = pieces[d + 1][:, col : col + width].astype(F32)
                    both = jnp.concatenate(
                        [jnp.where(even, one, two), jnp.where(even, two, one)], axis=1
                    )
                    start = pl.multiple_of((p * 4 + spot // 2) * 2 * width, 128)
                    out[:, pl.ds(start, 2 * width)] = both
            col += width


def exchange(at, pieces):
    return [pieces[0]] + [
        at.flip(pieces[d], b=d // 4, x=(d // 2) % 2, c=d % 2) for d in range(1, 8)
    ]


def fetch_group(at, weights, parts, splits):
    rows = weights[0].shape[0]
    wide = sum(w.shape[1] for w in weights) // 8
    pieces = call(
        functools.partial(cut_kernel, parts),
        [((rows, wide), BF16)] * 8,
        at.slot,
        *weights,
    )
    return call(
        place_kernel, [((8 * rows, n), BF16) for n in splits], at.slot, *exchange(at, pieces)
    )


def fetch_blocks(at, block):
    blocks = []
    for i in range(at.outer):
        here = block if i == 0 else at.shift(block, i)
        blocks.append(here)
        blocks.append(at.flip(here, e=1))
    return blocks


def deliver(at, make, counts, widths):
    outer = at.outer
    sent = [at.flip(make(2 * i + 1, BF16), e=1) for i in range(outer)]
    terms = []
    for i in range(1, outer):
        here = make(2 * i, F32) + sent[i].astype(F32)
        terms.append(at.push(here.astype(BF16), i))
    terms = [make(0, F32), sent[0]] + terms
    rows = terms[0].shape[0] // 8
    pieces = call(
        functools.partial(sum_cut_kernel, len(terms)),
        [((rows, terms[0].shape[1]), BF16)] * 8,
        at.slot,
        *terms,
    )
    return call(
        functools.partial(spread_kernel, counts),
        [((rows, n), F32) for n in widths],
        at.slot,
        *exchange(at, pieces),
    )


def fetch_small(at, values):
    block = values[None]
    block = joined(at.c, block, at.flip(block, c=1), 0)
    block = joined(at.x, block, at.flip(block, x=1), 0)
    block = joined(at.b, block, at.flip(block, b=1), 0)
    whole = jnp.stack([block] + [at.shift(block, i) for i in range(1, at.outer)])
    return jnp.stack([whole, at.flip(whole, e=1)], axis=1)


def deliver_small(at, values):
    whole = values[:, 0] + at.flip(values[:, 1], e=1)
    block = whole[0]
    for i in range(1, at.outer):
        block = block + at.push(whole[i], i)
    for bit, name in ((at.b, "b"), (at.x, "x"), (at.c, "c")):
        rows = block.shape[0] // 2
        low, high = block[:rows], block[rows:]
        block = pick(bit, low, high) + at.flip(pick(bit, high, low), **{name: 1})
    return block[0]


def order_tokens(at, values):
    seqs, length = values.shape
    view = values.reshape(seqs, 2, 2, length // 4)
    view = pick(at.x, view, view[:, ::-1])
    view = pick(at.c, view, view[:, :, ::-1])
    return jnp.swapaxes(view, 1, 2).reshape(seqs, length)


def body(
    layer_input,
    segment_ids,
    positions,
    ln1_gain,
    ln1_bias,
    qkv_weight,
    qkv_bias,
    out_weight,
    ln2_gain,
    ln2_bias,
    gate_weight,
    up_weight,
    down_weight,
    cotangent,
):
    at = Places()
    width = layer_input.shape[1]
    rows = qkv_weight.shape[0]
    bias_rows = qkv_bias.shape[0]
    length = segment_ids.shape[1]
    heads_here = HEADS // 8
    part = width // 8
    units = gate_weight.shape[1] // 8
    step = width // (2 * at.outer)
    slot = at.b * 4 + at.x * 2 + at.c

    qkv_block, out_block = fetch_group(
        at, [qkv_weight, out_weight], (3, 1), (3 * part, part)
    )
    qkv_blocks = fetch_blocks(at, qkv_block)
    out_blocks = fetch_blocks(at, out_block)
    inputs_low, cotangent_low = to_relative(at, layer_input, cotangent)
    inputs = inputs_low.astype(F32)
    inputs_all = gather_tokens(at, inputs_low)
    small = fetch_small(
        at, jnp.concatenate([qkv_bias, ln1_gain, ln1_bias, ln2_gain, ln2_bias])
    )
    spots = jnp.concatenate([segment_ids, positions[None]], axis=0)
    spots = jnp.stack([spots, at.flip(spots, b=1)])
    segments = order_tokens(at, spots[:, 0])
    places = order_tokens(at, spots[:, 1])
    index = order_tokens(at, jnp.arange(length)[None])[0]

    def vector(i):
        start = bias_rows + i * rows
        return small[..., start : start + rows].reshape(width).astype(F32)

    gain_one, shift_one, gain_two, shift_two = (vector(i) for i in range(4))
    bias = small[..., :bias_rows]
    bias = pick(at.e, bias, bias[:, ::-1])
    bias = jnp.roll(bias, at.a, axis=0)
    bias = bias.reshape(at.outer, 2, 2, 4, bias_rows).swapaxes(1, 2).reshape(3, 8, part)
    bias = lax.dynamic_index_in_dim(bias, slot, 1, keepdims=False).reshape(3 * part).astype(F32)

    def cut(values, i):
        return values[:, i * step : (i + 1) * step]

    def contract(values, blocks):
        total = dot(cut(values, 0), blocks[0])
        for i in range(1, len(blocks)):
            total = total + dot(cut(values, i), blocks[i])
        return total

    def expand(values, blocks):
        half = values.shape[0] // 2
        other = jnp.concatenate([dot_cols(values[half:], w, BF16) for w in blocks], axis=1)
        own = jnp.concatenate([dot_cols(values[:half], w) for w in blocks], axis=1)
        return sum_tokens(at, own, other)

    def by_sequence(values, n):
        view = values.reshape(2, 2, length // 2, n, HEAD_DIM)
        return view.transpose(1, 3, 0, 2, 4).reshape(2, n, length, HEAD_DIM)

    def by_token(values):
        n = values.shape[1]
        view = values.reshape(2, n, 2, length // 2, HEAD_DIM)
        return view.transpose(2, 0, 3, 1, 4).reshape(2 * length, n * HEAD_DIM)

    normed_all = layer_norm(inputs_all.astype(F32), gain_one, shift_one).astype(BF16)
    mixed = contract(normed_all, qkv_blocks) + bias
    cosine, sine = rotary_tables(places)
    cosine, sine = cosine[:, None], sine[:, None]
    query = rotate(by_sequence(mixed[:, :part], heads_here), cosine, sine).astype(BF16)
    key = rotate(by_sequence(mixed[:, part : 2 * part], heads_here), cosine, sine).astype(BF16)
    value = by_sequence(mixed[:, 2 * part :], heads_here).astype(BF16)
    allowed = (segments[:, :, None] == segments[:, None, :]) & (
        index[None, None, :] <= index[None, :, None]
    )
    scores = jnp.einsum("bhtd,bhld->bhtl", query, key, preferred_element_type=F32) * 0.125
    scores = jnp.where(allowed[:, None], scores, -1e30)
    top = jnp.max(scores, axis=-1, keepdims=True)
    expo = jnp.exp(scores - top)
    total = jnp.sum(expo, axis=-1, keepdims=True)
    probs = expo / total
    probs_low = probs.astype(BF16)
    attended = by_token(
        jnp.einsum("bhtl,bhld->bhtd", probs_low, value, preferred_element_type=F32)
    ).astype(BF16)

    hidden = inputs + expand(attended, out_blocks)
    normed2 = layer_norm(hidden, gain_two, shift_two).astype(BF16)
    normed2_all = gather_tokens(at, normed2)
    pair_block, down_block = fetch_group(
        at, [gate_weight, up_weight, down_weight], (1, 1, 1), (2 * units, units)
    )
    pair_blocks = fetch_blocks(at, pair_block)
    down_blocks = fetch_blocks(at, down_block)
    cotangent_all = gather_tokens(at, cotangent_low)

    gate_up = contract(normed2_all, pair_blocks)
    gate = gate_up[:, :units]
    up = gate_up[:, units:]
    sigmoid = 1.0 / (1.0 + jnp.exp(-gate))
    silu = gate * sigmoid
    inner = (silu * up).astype(BF16)
    down_grads = deliver(
        at, lambda i, kind: dot_rows(cut(cotangent_all, i), inner, kind), (1,), (8 * units,)
    )
    inner_grad = contract(cotangent_all, down_blocks)
    gate_grad = inner_grad * up * sigmoid * (1.0 + gate * (1.0 - sigmoid))
    up_grad = inner_grad * silu
    pair_low = jnp.concatenate([gate_grad.astype(BF16), up_grad.astype(BF16)], axis=1)
    normed2_grad = expand(pair_low, pair_blocks)
    pair_grads = deliver(
        at, lambda i, kind: dot_rows(cut(normed2_all, i), pair_low, kind), (1, 1), (8 * units,) * 2
    )
    result = (hidden + expand(inner, down_blocks)).astype(BF16)

    hidden_part, gain_two_grad, shift_two_grad = norm_back(hidden, gain_two, normed2_grad)
    hidden_grad = cotangent_low.astype(F32) + hidden_part
    branch_all = gather_tokens(at, hidden_grad.astype(BF16))
    attended_grad = by_sequence(contract(branch_all, out_blocks), heads_here).astype(BF16)
    out_grads = deliver(
        at, lambda i, kind: dot_rows(cut(branch_all, i), attended, kind), (1,), (8 * part,)
    )
    value_grad = jnp.einsum(
        "bhtl,bhtd->bhld", probs_low, attended_grad, preferred_element_type=F32
    )
    probs_grad = jnp.einsum(
        "bhtd,bhld->bhtl", attended_grad, value, preferred_element_type=F32
    )
    center = jnp.sum(probs * probs_grad, axis=-1, keepdims=True)
    scores_low = (probs * (probs_grad - center)).astype(BF16)
    query_grad = (
        jnp.einsum("bhtl,bhld->bhtd", scores_low, key, preferred_element_type=F32) * 0.125
    )
    key_grad = (
        jnp.einsum("bhtl,bhtd->bhld", scores_low, query, preferred_element_type=F32) * 0.125
    )
    mixed_low = jnp.concatenate(
        [
            by_token(rotate(query_grad, cosine, -sine)),
            by_token(rotate(key_grad, cosine, -sine)),
            by_token(value_grad),
        ],
        axis=1,
    ).astype(BF16)
    qkv_grads = deliver(
        at, lambda i, kind: dot_rows(cut(normed_all, i), mixed_low, kind), (3,), (24 * part,)
    )
    normed_grad = expand(mixed_low, qkv_blocks)
    input_part, gain_one_grad, shift_one_grad = norm_back(inputs, gain_one, normed_grad)
    result, input_grad = to_absolute(at, result, hidden_grad + input_part)

    bias_part = jnp.sum(mixed_low.astype(F32), axis=0).reshape(3, 1, part)
    own_slot = (jnp.arange(8) == slot).astype(F32)[None, :, None]
    bias_whole = (bias_part * own_slot).reshape(at.outer, 2, 2, 4, bias_rows).swapaxes(1, 2)
    bias_whole = jnp.roll(bias_whole, -at.a, axis=0)
    bias_whole = pick(at.e, bias_whole, bias_whole[:, ::-1]).reshape(at.outer, 2, 8, bias_rows)
    grads = [
        v.reshape(at.outer, 2, 8, rows)
        for v in (gain_one_grad, shift_one_grad, gain_two_grad, shift_two_grad)
    ]
    shares = deliver_small(at, jnp.concatenate([bias_whole] + grads, axis=-1))

    def share(i):
        return shares[bias_rows + i * rows : bias_rows + (i + 1) * rows]

    return (
        result,
        input_grad,
        share(0),
        share(1),
        qkv_grads[0],
        shares[:bias_rows],
        out_grads[0],
        share(2),
        share(3),
        pair_grads[0],
        pair_grads[1],
        down_grads[0],
    )


def solution(mesh):
    both = ("fsdp", "seq")
    wide = P(both, None)
    flat = P(both)
    return jax.shard_map(
        body,
        mesh=mesh,
        in_specs=(
            wide, P("fsdp", None), P("fsdp"), flat, flat, wide, flat,
            wide, flat, flat, wide, wide, wide, wide,
        ),
        out_specs=(wide, wide, flat, flat, wide, flat, wide, flat, flat, wide, wide, wide),
        check_vma=False,
    )
```

```python
import functools
import math

import jax
import jax.numpy as jnp
from jax import lax
from jax.experimental import pallas as pl
from jax.experimental.layout import Layout, with_layout_constraint
from jax.experimental.pallas import tpu as pltpu
from jax.sharding import PartitionSpec as P

HEADS = 32
HEAD_DIM = 64
AXES = ("fsdp", "seq")
F32 = jnp.float32
BF16 = jnp.bfloat16


def centered_of(values):
    centered = values - jnp.mean(values, axis=-1, keepdims=True)
    spread = jnp.mean(centered * centered, axis=-1, keepdims=True)
    return centered, lax.rsqrt(spread + 1e-05)


def norm_back(values, gain, grad):
    centered, scale = centered_of(values)
    hat = centered * scale
    lifted = grad * gain
    inner = jnp.mean(lifted * hat, axis=-1, keepdims=True)
    pulled = scale * (lifted - jnp.mean(lifted, axis=-1, keepdims=True) - hat * inner)
    return (
        pulled,
        jnp.sum(grad * hat, axis=0, keepdims=True),
        jnp.sum(grad, axis=0, keepdims=True),
    )


def rotary_tables(spots):
    inverse = 10000.0 ** (-jnp.arange(8).astype(F32) / 8.0)
    angle = inverse[:, None] * spots.astype(F32)[None]
    waves = jnp.concatenate([jnp.cos(angle), jnp.sin(angle)], axis=0)
    lane = jnp.arange(2 * HEAD_DIM) % HEAD_DIM
    row = jnp.arange(16)[:, None]
    turn = row - 8
    picks = [
        (row < 8) & (lane < 16) & (lane % 8 == row),
        (lane < 8) & (lane == turn),
        (lane >= 8) & (lane < 16) & (lane - 8 == turn),
    ]
    signs = (1.0, -1.0, 1.0)
    chosen = jnp.concatenate([p.astype(F32) * g for p, g in zip(picks, signs)], axis=1)
    rest = jnp.concatenate([(lane >= 16).astype(F32), jnp.zeros(4 * HEAD_DIM, F32)])
    table = lax.dot_general(
        waves, chosen, (((0,), (0,)), ((), ())), precision=lax.Precision.HIGHEST
    )
    return table + rest


def turned(values, table, sign):
    wide = values.shape[1]
    many = wide // (2 * HEAD_DIM)
    keep, later, earlier = (
        jnp.concatenate([table[:, i * 128 : (i + 1) * 128]] * many, axis=1) for i in range(3)
    )
    partner = pltpu.roll(values, wide - 8, 1) * later + pltpu.roll(values, 8, 1) * earlier
    return values * keep + sign * partner


def dot_rows(left, right, kind=F32):
    return lax.dot_general(
        left, right, (((0,), (0,)), ((), ())), preferred_element_type=F32
    ).astype(kind)


def dot_cols(left, right, kind=F32):
    return lax.dot_general(
        left, right, (((1,), (1,)), ((), ())), preferred_element_type=F32
    ).astype(kind)


def dot(left, right):
    return jnp.dot(left, right, preferred_element_type=F32)


class Places:
    def __init__(self):
        self.fsdp = lax.axis_size("fsdp")
        self.seq = lax.axis_size("seq")
        self.count = self.fsdp * self.seq
        self.outer = self.fsdp // 4
        spot = lax.axis_index("fsdp")
        side = lax.axis_index("seq")
        self.a = spot // 4
        self.b = (spot // 2) % 2
        self.e = spot % 2
        self.x = side // 2
        self.c = side % 2
        self.last = None
        high, low = 2 * self.seq, self.seq
        self.groups = [
            [(a * 4 + e) * low + b * high + i for b in range(2) for i in range(low)]
            for a in range(self.outer)
            for e in range(2)
        ]
        self.sides = [group[c::2] for group in self.groups for c in range(2)]

    def after(self, values):
        if self.last is None:
            return values
        values, self.last = lax.optimization_barrier((values, self.last))
        return values

    def move(self, values, pairs):
        if values.ndim == 2 and values.shape[1] % 128 and values.shape[0] > 8:
            values = with_layout_constraint(values, Layout((0, 1)))
            return with_layout_constraint(lax.ppermute(values, AXES, pairs), Layout((0, 1)))
        return lax.ppermute(values, AXES, pairs)

    def flip(self, values, c=0, x=0, e=0, b=0):
        mask = c + 2 * x + self.seq * (e + 2 * b)
        return self.move(values, [(i, i ^ mask) for i in range(self.count)])

    def shift(self, values, steps):
        stride = 4 * self.seq * steps
        return self.move(values, [((i + stride) % self.count, i) for i in range(self.count)])

    def push(self, values, steps):
        stride = 4 * self.seq * steps
        return self.move(values, [(i, (i + stride) % self.count) for i in range(self.count)])

    def swap(self, values, groups):
        parts = len(groups[0])
        view = values.reshape(parts, values.shape[0] // parts, values.shape[1])
        view = lax.all_to_all(view, AXES, 0, 0, axis_index_groups=groups, tiled=True)
        return view.reshape(values.shape)


class Window:
    def close(self, at):
        values, tree = jax.tree.flatten(self.__dict__)
        self.__dict__.update(jax.tree.unflatten(tree, lax.optimization_barrier(values)))
        at.last = None


def pick(bit, first, second):
    return jnp.where(bit == 0, first, second)


def joined(bit, own, other, axis):
    return pick(
        bit, jnp.concatenate([own, other], axis=axis), jnp.concatenate([other, own], axis=axis)
    )


def order_kernel(width, spots_ref, ref, *outs):
    for i in range(ref.shape[1] // width):
        start = pl.multiple_of(spots_ref[i] * width, 128)
        block = ref[:, pl.ds(start, width)]
        for out in outs:
            for k in range(out.shape[0] // ref.shape[0]):
                rows = slice(k * ref.shape[0], (k + 1) * ref.shape[0])
                out[rows, i * width : (i + 1) * width] = block


def reorder(at, spots, values, copies):
    width = values.shape[1] // len(spots)
    if width % 128:
        cols = [lax.dynamic_slice_in_dim(values, spot * width, width, 1) for spot in spots]
        ordered = jnp.concatenate(cols, axis=1)
        return [jnp.concatenate([ordered] * n, axis=0) for n in copies]
    order = jnp.stack(spots).astype(jnp.int32)
    rows, wide = values.shape
    outs = [((n * rows, wide), values.dtype) for n in copies]
    return call(at, functools.partial(order_kernel, width), outs, order, values, name="order")


def to_relative(at, values, copies):
    spots = [
        (((at.a + i) % at.outer) * 2 + k) * 2 + (at.e ^ j)
        for i in range(at.outer)
        for j in range(2)
        for k in range(2)
    ]
    return reorder(at, spots, values, copies)


def to_absolute(at, values):
    spots = [
        (((i - at.a) % at.outer) * 2 + (at.e ^ j)) * 2 + k
        for i in range(at.outer)
        for k in range(2)
        for j in range(2)
    ]
    return reorder(at, spots, values, [1])[0]


def rows_of(shape, rows, index=lambda i: i):
    return pl.BlockSpec((rows, shape[1]), lambda i: (index(i), 0))


def call(at, kernel, outs, *args, steps=1, tiles=None, out_tiles=None, scratch=(), name=None):
    def spec(shape, kind, k, given):
        if given and k in given:
            return given[k]
        if kind == jnp.int32:
            return pl.BlockSpec(memory_space=pltpu.SMEM)
        zeros = (0,) * len(shape)
        return pl.BlockSpec(shape, lambda i: zeros, pipeline_mode=pl.Buffered(1))

    size = 0
    for shapes, given in (
        ([(v.shape, v.dtype) for v in args], tiles),
        (list(outs), out_tiles),
        ([(v.shape, v.dtype) for v in scratch], None),
    ):
        for k, (shape, kind) in enumerate(shapes):
            block = given[k].block_shape if given and k in given else shape
            size += math.prod(block) * jnp.dtype(kind).itemsize * (1 + (block is not shape))
    least = min(range(len(args)), key=lambda i: args[i].size)
    in_specs = [spec(v.shape, v.dtype, k, tiles) for k, v in enumerate(args)]
    args = list(args)
    args[least] = at.after(args[least])
    results = pl.pallas_call(
        kernel,
        grid=(steps,),
        out_shape=[jax.ShapeDtypeStruct(shape, kind) for shape, kind in outs],
        in_specs=in_specs,
        out_specs=[spec(shape, kind, k, out_tiles) for k, (shape, kind) in enumerate(outs)],
        scratch_shapes=list(scratch),
        compiler_params=pltpu.CompilerParams(
            vmem_limit_bytes=min(size * 9 // 8 + 12 * 2**20, 60 * 2**20)
        ),
        cost_estimate=pl.CostEstimate(flops=0, bytes_accessed=0, transcendentals=0),
        name=name,
    )(*args)
    at.last = min(results, key=lambda v: v.size)
    return results


TILE = 256


def product(values, chunks):
    outs = []
    for blocks in chunks:
        depth = blocks[0].shape[0]
        total = dot(values[:, :depth], blocks[0][...])
        for i, block in enumerate(blocks[1:], 1):
            total = total + dot(values[:, i * depth : (i + 1) * depth], block[...])
        outs.append(total)
    return outs[0] if len(outs) == 1 else jnp.concatenate(outs, axis=1)


def in_chunks(refs, count):
    return [refs[i : i + count] for i in range(0, len(refs), count)]


def transposed_product(values, chunks, j):
    total, col = None, 0
    for blocks in chunks:
        width = blocks[j].shape[1]
        term = dot_cols(values[:, col : col + width], blocks[j][...])
        total = term if total is None else total + term
        col += width
    return total


def tile_of(i):
    return pl.ds(pl.multiple_of(i * TILE, TILE), TILE)


def near_far(near, far):
    half = near.shape[0] // TILE
    return {
        0: rows_of(near.shape, TILE, lambda i: jnp.minimum(i, half - 1)),
        1: rows_of(far.shape, TILE, lambda i: jnp.maximum(i - half, 0)),
    }


def tile_from(near, far):
    first = pl.program_id(0) < pl.num_programs(0) // 2
    return jnp.where(first, near[...], far[...])


def qkv_kernel(count, near, far, *refs):
    gain, shift, bias, table, normed, mixed = refs[-6:]
    centered, scale = centered_of(tile_from(near, far).astype(F32))
    normed[...] = (centered * scale * gain[...] + shift[...]).astype(BF16)
    turning = mixed.shape[1] * 2 // 3
    values = product(normed, in_chunks(refs[:-6], count)) + bias[...]
    mixed[:, :turning] = turned(values[:, :turning], table[...], 1.0).astype(BF16)
    mixed[:, turning:] = values[:, turning:].astype(BF16)


def attended_grad_kernel(count, near, far, *refs):
    whole, grads = refs[-2:]
    whole[...] = tile_from(near, far)
    grads[...] = product(whole, in_chunks(refs[:-2], count)).astype(BF16)


def head_of(ref, group, head, start):
    part = ref.shape[1] // 3
    low = group * part + head * HEAD_DIM
    return ref[pl.ds(pl.multiple_of(start, TILE), TILE), low : low + HEAD_DIM]


def both_halves(ref, group, head, start, half):
    return jnp.concatenate(
        [head_of(ref, group, head, start), head_of(ref, group, head, start + half)], axis=0
    )


def allowed_at(row, col, sequence, turn):
    spot = pl.ds(pl.multiple_of(turn * TILE, TILE), TILE)
    ours = jnp.where(sequence == 0, row[0:1, spot], row[1:2, spot])
    theirs = jnp.where(sequence == 0, col[:, 0:1], col[:, 1:2])
    return (theirs == ours) & (col[:, 2:3] <= row[2:3, spot])


def scores_of(key, query, allowed):
    return jnp.where(allowed, dot_cols(key, query) * 0.125, -1e30)


def attend_kernel(mixed, row, col, attended, sums):
    half = mixed.shape[0] // 2
    heads = attended.shape[1] // HEAD_DIM

    @pl.loop(0, 4)
    def _(i):
        sequence, turn = i // 2, i % 2
        allowed = allowed_at(row, col, sequence, turn)
        start = turn * half + sequence * TILE
        span = pl.ds(pl.multiple_of(start, TILE), TILE)
        for h in range(heads):
            key = both_halves(mixed, 1, h, sequence * TILE, half)
            value = both_halves(mixed, 2, h, sequence * TILE, half)
            scores = scores_of(key, head_of(mixed, 0, h, start), allowed)
            top = jnp.max(scores, axis=0, keepdims=True)
            expo = jnp.exp(scores - top)
            total = jnp.sum(expo, axis=0, keepdims=True)
            probs = (expo * (1.0 / total)).astype(BF16)
            out = jnp.transpose(dot_rows(value, probs))
            attended[span, h * HEAD_DIM : (h + 1) * HEAD_DIM] = out.astype(BF16)
            sums[pl.ds(i * heads + h, 1), :] = top + jnp.log(total)


def attend_back_kernel(
    grads, mixed, sums, table, row, col, low, bias, query_sum, key_sum, value_sum
):
    half = mixed.shape[0] // 2
    part = grads.shape[1]
    heads = part // HEAD_DIM

    for sequence in range(2):
        for turn in range(2):
            i = sequence * 2 + turn
            allowed = allowed_at(row, col, sequence, turn)
            start = turn * half + sequence * TILE
            span = pl.ds(start, TILE)
            for h in range(heads):
                cols = slice(h * HEAD_DIM, (h + 1) * HEAD_DIM)
                query = head_of(mixed, 0, h, start)
                key = both_halves(mixed, 1, h, sequence * TILE, half)
                value = both_halves(mixed, 2, h, sequence * TILE, half)
                grad = grads[span, cols]
                scores = scores_of(key, query, allowed)
                probs = jnp.exp(scores - sums[i * heads + h : i * heads + h + 1, :])
                probs_grad = dot_cols(value, grad)
                value_grad = dot(probs.astype(BF16), grad)
                center = jnp.sum(probs * probs_grad, axis=0, keepdims=True)
                scores_low = (probs * (probs_grad - center)).astype(BF16)
                key_grad = dot(scores_low, query)
                query_sum[span, cols] = jnp.transpose(dot_rows(key, scores_low))
                for k in range(2):
                    keys = pl.ds(k * half + sequence * TILE, TILE)
                    rows = slice(k * TILE, (k + 1) * TILE)
                    if turn == 0:
                        key_sum[keys, cols] = key_grad[rows]
                        value_sum[keys, cols] = value_grad[rows]
                    else:
                        key_sum[keys, cols] += key_grad[rows]
                        value_sum[keys, cols] += value_grad[rows]

    bias[...] = jnp.zeros_like(bias)

    @pl.loop(0, mixed.shape[0] // TILE)
    def _(i):
        span = tile_of(i)
        factors = table[span, :]
        for k, ref in enumerate((query_sum, key_sum, value_sum)):
            values = ref[span, :]
            if k < 2:
                values = turned(values * 0.125, factors, -1.0)
            values = values.astype(BF16)
            low[span, k * part : (k + 1) * part] = values
            bias[:, k * part : (k + 1) * part] += jnp.sum(
                values.astype(F32), axis=0, keepdims=True
            )


def expand_kernel(count, values, *refs):
    *blocks, out = refs
    chunks = in_chunks(blocks, count)
    width = blocks[0].shape[0]
    for j in range(count):
        total = transposed_product(values, chunks, j)
        out[:, j * width : (j + 1) * width] = total.astype(out.dtype)


def total_of(terms):
    rows = terms.shape[0] // 4
    total = terms[:rows, :].astype(F32)
    for i in range(1, 4):
        total = total + terms[i * rows : (i + 1) * rows, :].astype(F32)
    return total


def four(out, values):
    rows = values.shape[0]
    for i in range(4):
        out[i * rows : (i + 1) * rows, :] = values


def hidden_kernel(inputs, gain, shift, terms, hidden, normed):
    values = inputs[...].astype(F32) + total_of(terms)
    hidden[...] = values
    centered, scale = centered_of(values)
    four(normed, (centered * scale * gain[...] + shift[...]).astype(BF16))


def result_kernel(hidden, terms, out):
    out[...] = (hidden[...] + total_of(terms)).astype(BF16)


def branch_kernel(hidden, cotangent, gain, terms, grad, low, gain_grad, shift_grad):
    pulled, gain_grad[...], shift_grad[...] = norm_back(hidden[...], gain[...], total_of(terms))
    values = cotangent[...].astype(F32) + pulled
    grad[...] = values
    four(low, values.astype(BF16))


def input_kernel(inputs, hidden_grad, gain, terms, grad, gain_grad, shift_grad):
    pulled, gain_grad[...], shift_grad[...] = norm_back(
        inputs[...].astype(F32), gain[...], total_of(terms)
    )
    grad[...] = hidden_grad[...] + pulled


def mlp_kernel(count, near, far, *refs):
    *blocks, normed, inner, gate_factor, up_factor = refs
    units = inner.shape[1]
    normed[...] = tile_from(near, far)
    values = product(normed, in_chunks(blocks, count))
    gate, up = values[:, :units], values[:, units:]
    sigmoid = 1.0 / (1.0 + jnp.exp(-gate))
    silu = gate * sigmoid
    inner[...] = (silu * up).astype(BF16)
    gate_factor[...] = up * sigmoid * (1.0 + gate * (1.0 - sigmoid))
    up_factor[...] = silu


def mlp_back_kernel(count, grads, *refs):
    *blocks, gate_factor, up_factor, pair = refs
    values = product(grads, in_chunks(blocks, count))
    pair[...] = jnp.concatenate(
        [(values * gate_factor[...]).astype(BF16), (values * up_factor[...]).astype(BF16)],
        axis=1,
    )


def segments(widths, chunks):
    out = []
    at_part = at_chunk = part = chunk = 0
    while part < len(widths):
        size = min(widths[part] - at_part, chunks[chunk] - at_chunk)
        out.append((part, at_part, chunk, at_chunk, size))
        at_part, at_chunk = at_part + size, at_chunk + size
        if at_part == widths[part]:
            part, at_part = part + 1, 0
        if at_chunk == chunks[chunk]:
            chunk, at_chunk = chunk + 1, 0
    return out


def part_list(refs, counts):
    return [
        (ref, p, ref.shape[1] // (8 * count)) for ref, count in zip(refs, counts) for p in range(count)
    ]


def cut_kernel(counts, *refs):
    weights, outs = refs[: len(counts)], refs[len(counts) :]
    rows = weights[0].shape[0]
    parts = part_list(weights, counts)
    cuts = segments([width for _, _, width in parts], [out.shape[1] for out in outs])
    for part, begin, chunk, col, size in cuts:
        ref, p, width = parts[part]
        for j in range(8):
            start = (p * 8 + j) * width + begin
            outs[chunk][j * rows : (j + 1) * rows, col : col + size] = ref[:, start : start + size]


def spread_kernel(counts, *refs):
    chunks, outs = refs[: -len(counts)], refs[-len(counts) :]
    rows = outs[0].shape[0]
    parts = part_list(outs, counts)
    cuts = segments([width for _, _, width in parts], [chunk.shape[1] for chunk in chunks])
    for part, begin, chunk, col, size in cuts:
        ref, p, width = parts[part]
        for j in range(8):
            start = (p * 8 + j) * width + begin
            piece = chunks[chunk][j * rows : (j + 1) * rows, col : col + size]
            ref[:, start : start + size] = piece.astype(F32)


def sum_kernel(*refs):
    *terms, out = refs
    total = terms[0][...].astype(F32)
    for term in terms[1:]:
        total = total + term[...].astype(F32)
    out[...] = total.astype(BF16)


def cut_rows(at, weights, counts, chunks):
    rows = weights[0].shape[0]
    return call(
        at,
        functools.partial(cut_kernel, counts),
        [((8 * rows, n), BF16) for n in chunks],
        *weights,
        name="cut",
    )


def split_kernel(whole, *outs):
    col = 0
    for out in outs:
        out[...] = whole[:, col : col + out.shape[1]]
        col += out.shape[1]


def cross_block(at, block):
    return [block] + [at.shift(block, i) for i in range(1, at.outer)]


def merge_blocks(across, beside):
    return [block for pair in zip(across, beside) for block in pair]


def send_block(at, block):
    return [block] + [at.shift(block, i) for i in range(1, at.outer)]


def grad_kernel(count, begin, values, grads, *refs):
    addends, outs = refs[:count], refs[count:]
    each = pl.num_programs(0) // len(outs)
    for k, out in enumerate(outs):

        @pl.when(pl.program_id(0) // each == k)
        def _():
            total = dot_rows(values[...], grads[:, begin : begin + out.shape[1]])
            if k < count:
                total = total + addends[k][...].astype(F32)
            out[...] = total.astype(out.dtype)


def grad_blocks(at, way, spots, kind, addends=()):
    values, grads, begin, size = way
    tokens, wide = values.shape
    width = wide // (2 * at.outer)
    tile = min(TILE, width)
    each = width // tile

    def column(i):
        spot = spots[0]
        for k in range(1, len(spots)):
            spot = jnp.where(i // each == k, spots[k], spot)
        return spot * each + i % each

    def row_of(k):
        return lambda i: jnp.clip(i - k * each, 0, each - 1)

    shape = (width, size)
    tiles = {0: pl.BlockSpec((tokens, tile), lambda i: (0, column(i)))}
    for k in range(len(addends)):
        tiles[2 + k] = rows_of(shape, tile, row_of(k))
    return call(
        at,
        functools.partial(grad_kernel, len(addends), begin),
        [(shape, kind)] * len(spots),
        values,
        grads,
        *addends,
        steps=len(spots) * each,
        tiles=tiles,
        out_tiles={k: rows_of(shape, tile, row_of(k)) for k in range(len(spots))},
        name="grad",
    )


def grad_beside(at, way):
    order = list(range(1, at.outer)) + [0]
    return grad_blocks(at, way, [2 * i + 1 for i in order], BF16)


def grad_own(at, way):
    return grad_blocks(at, way, [0], F32)[0]


def grad_across(at, way, sent):
    if at.outer == 1:
        return []
    return grad_blocks(at, way, [2 * i for i in range(1, at.outer)], BF16, sent[: at.outer - 1])


def push_all(at, made):
    return [at.push(v, i) for i, v in enumerate(made, 1)]


def flip_all(at, made):
    return [at.flip(v, e=1) for v in made]


def grad_spread(at, chunks, counts, widths):
    rows = chunks[0].shape[0] // 8
    return call(
        at,
        functools.partial(spread_kernel, counts),
        [((rows, n), F32) for n in widths],
        *chunks,
        name="spread",
    )


def join_kernel(near, far, out):
    out[...] = tile_from(near, far)


def joined_rows(at, near, far):
    shape = (2 * near.shape[0], near.shape[1])
    (out,) = call(
        at,
        join_kernel,
        [(shape, BF16)],
        near,
        far,
        steps=shape[0] // TILE,
        tiles=near_far(near, far),
        out_tiles={0: rows_of(shape, TILE)},
        name="join",
    )
    return out


def expand(at, values, chunks, side, kind):
    half = values.shape[0] // 2
    blocks = [block for chunk in chunks for block in chunk]
    count = len(chunks[0])
    shape = (half, blocks[0].shape[0] * count)
    steps = half // TILE
    (out,) = call(
        at,
        functools.partial(expand_kernel, count),
        [(shape, kind)],
        values,
        *blocks,
        steps=steps,
        tiles={0: rows_of(values.shape, TILE, lambda i: i + side * steps)},
        out_tiles={0: rows_of(shape, TILE)},
        name="expand",
    )
    return out


def add(at, *terms):
    shape = terms[0].shape
    tile = min(TILE, shape[0])
    (total,) = call(
        at,
        sum_kernel,
        [(shape, BF16)],
        *terms,
        steps=shape[0] // tile,
        tiles={k: rows_of(shape, tile) for k in range(len(terms))},
        out_tiles={0: rows_of(shape, tile)},
        name="add",
    )
    return total


def fetch_small(at, values):
    block = values[None]
    block = joined(at.c, block, at.flip(block, c=1), 0)
    block = joined(at.x, block, at.flip(block, x=1), 0)
    block = joined(at.b, block, at.flip(block, b=1), 0)
    whole = jnp.stack([block] + [at.shift(block, i) for i in range(1, at.outer)])
    return jnp.stack([whole, at.flip(whole, e=1)], axis=1)


def deliver_small(at, values):
    whole = values[:, 0] + at.flip(values[:, 1], e=1)
    block = whole[0]
    for i in range(1, at.outer):
        block = block + at.push(whole[i], i)
    for bit, name in ((at.b, "b"), (at.x, "x"), (at.c, "c")):
        rows = block.shape[0] // 2
        low, high = block[:rows], block[rows:]
        block = pick(bit, low, high) + at.flip(pick(bit, high, low), **{name: 1})
    return block[0]


def order_tokens(at, values):
    seqs, length = values.shape
    view = values.reshape(seqs, 2, 2, length // 4)
    view = pick(at.c, view, view[:, :, ::-1])
    return jnp.swapaxes(view, 1, 2).reshape(seqs, length)


def body(
    layer_input,
    segment_ids,
    positions,
    ln1_gain,
    ln1_bias,
    qkv_weight,
    qkv_bias,
    out_weight,
    ln2_gain,
    ln2_bias,
    gate_weight,
    up_weight,
    down_weight,
    cotangent,
):
    at = Places()
    width = layer_input.shape[1]
    rows = qkv_weight.shape[0]
    bias_rows = qkv_bias.shape[0]
    length = segment_ids.shape[1]
    heads_here = HEADS // 8
    part = width // 8
    units = gate_weight.shape[1] // 8
    slot = at.b * 4 + at.x * 2 + at.c

    tokens = 2 * length
    count = 2 * at.outer
    near = layer_input.shape[0]

    first = 2 * units // 256 * 128
    second = 2 * units - first
    v = Window()
    thin, wide = (tokens, units), (tokens, 2 * units)

    (cut_now,) = cut_rows(at, [qkv_weight, out_weight], (3, 1), (4 * part,))
    v.front = at.swap(cut_now, at.groups)
    v.inputs, v.inputs_four = to_relative(at, layer_input, [1, 4])
    v.first_cut, v.second_cut = cut_rows(at, [gate_weight, up_weight], (1, 1), (first, second))
    (v.down_cut,) = cut_rows(at, [down_weight], (1,), (units,))
    v.cotangent, v.cotangent_four = to_relative(at, cotangent, [1, 4])
    v.small = jnp.concatenate([qkv_bias, ln1_gain, ln1_bias, ln2_gain, ln2_bias])
    spots = jnp.concatenate([segment_ids, positions[None]], axis=0)[None]
    v.spots = joined(at.b, spots, at.flip(spots, b=1), 0)
    v.close(at)

    v.qkv, v.out = call(
        at,
        split_kernel,
        [((8 * rows, 3 * part), BF16), ((8 * rows, part), BF16)],
        v.front,
        name="split",
    )
    del v.front
    v.qkv_across = cross_block(at, v.qkv)
    v.qkv_beside = [at.flip(v.qkv, e=1)]
    v.near = at.swap(v.inputs_four, at.sides)
    v.first = at.swap(v.first_cut, at.groups)
    v.small = fetch_small(at, v.small)
    segments_here = order_tokens(at, v.spots[:, 0])
    places = order_tokens(at, v.spots[:, 1])
    index = order_tokens(at, jnp.arange(length)[None])
    v.row = jnp.concatenate([segments_here, index], axis=0).astype(F32)
    v.col = jnp.transpose(v.row)
    places = places.reshape(2, 2, length // 2).swapaxes(0, 1).reshape(2 * length)
    v.table = rotary_tables(places)
    v.close(at)

    v.qkv_beside += flip_all(at, v.qkv_across[1:])
    v.far = at.flip(v.near, c=1)
    v.out_across = cross_block(at, v.out)
    v.out_beside = [at.flip(v.out, e=1)]
    v.cotangent_near = at.swap(v.cotangent_four, at.sides)

    def vector(i):
        start = bias_rows + i * rows
        return v.small[..., start : start + rows].reshape(1, width).astype(F32)

    v.gains = [vector(i) for i in range(4)]
    bias = v.small[..., :bias_rows]
    bias = pick(at.e, bias, bias[:, ::-1])
    bias = jnp.roll(bias, at.a, axis=0)
    bias = bias.reshape(at.outer, 2, 2, 4, bias_rows).swapaxes(1, 2).reshape(3, 8, part)
    bias = lax.dynamic_index_in_dim(bias, slot, 1, keepdims=False)
    v.bias = bias.reshape(1, 3 * part).astype(F32)
    v.close(at)
    v.qkv_blocks = [merge_blocks(v.qkv_across, v.qkv_beside)]
    del v.qkv_across, v.qkv_beside, v.qkv, v.small, v.spots, v.inputs_four, v.cotangent_four, v.first_cut

    v.first_across = cross_block(at, v.first)
    v.first_beside = [at.flip(v.first, e=1)]
    v.out_beside += flip_all(at, v.out_across[1:])
    v.cotangent_far = at.flip(v.cotangent_near, c=1)
    v.second = at.swap(v.second_cut, at.groups)
    v.down = at.swap(v.down_cut, at.groups)
    v.normed, v.mixed = call(
        at,
        functools.partial(qkv_kernel, count),
        [((tokens, width), BF16), ((tokens, 3 * part), BF16)],
        v.near,
        v.far,
        *v.qkv_blocks[0],
        v.gains[0],
        v.gains[1],
        v.bias,
        v.table,
        steps=tokens // TILE,
        tiles=near_far(v.near, v.far) | {5 + count: rows_of(v.table.shape, TILE)},
        out_tiles={0: rows_of((tokens, width), TILE), 1: rows_of((tokens, 3 * part), TILE)},
        name="qkv",
    )
    v.attended, v.sums = call(
        at,
        attend_kernel,
        [((tokens, part), BF16), ((4 * heads_here, TILE), F32)],
        v.mixed,
        v.row,
        v.col,
        name="attend",
    )
    v.out_blocks = [merge_blocks(v.out_across, v.out_beside)]
    v.other = expand(at, v.attended, v.out_blocks, 1, BF16)
    v.own = expand(at, v.attended, v.out_blocks, 0, F32)
    v.close(at)
    del v.out_across, v.out_beside, v.out, v.second_cut, v.down_cut

    v.other = at.flip(v.other, c=1)
    v.cotangent_all = joined_rows(at, v.cotangent_near, v.cotangent_far)
    v.close(at)
    del v.cotangent_near, v.cotangent_far

    v.terms = at.swap(add(at, v.own, v.other), at.sides)
    v.second_across = cross_block(at, v.second)
    v.second_beside = [at.flip(v.second, e=1)]
    v.first_beside += flip_all(at, v.first_across[1:])
    v.close(at)
    del v.own, v.other

    v.hidden, normed2_four = call(
        at,
        hidden_kernel,
        [((near, width), F32), ((4 * near, width), BF16)],
        v.inputs,
        v.gains[2],
        v.gains[3],
        v.terms,
        name="hidden",
    )
    v.near = at.swap(normed2_four, at.sides)
    v.down_across = cross_block(at, v.down)
    v.down_beside = [at.flip(v.down, e=1)]
    v.second_beside += flip_all(at, v.second_across[1:])
    v.close(at)
    v.pair_blocks = [
        merge_blocks(v.first_across, v.first_beside),
        merge_blocks(v.second_across, v.second_beside),
    ]
    del v.first_across, v.first_beside, v.second_across, v.second_beside, v.first, v.second

    v.far = at.flip(v.near, c=1)
    v.down_beside += flip_all(at, v.down_across[1:])
    v.normed2, v.inner, v.gate_factor, v.up_factor = call(
        at,
        functools.partial(mlp_kernel, count),
        [((tokens, width), BF16), (thin, BF16), (thin, F32), (thin, F32)],
        v.near,
        v.far,
        *v.pair_blocks[0],
        *v.pair_blocks[1],
        steps=tokens // TILE,
        tiles=near_far(v.near, v.far),
        out_tiles={0: rows_of((tokens, width), TILE)}
        | {k: rows_of(thin, TILE) for k in range(1, 4)},
        name="mlp",
    )
    v.down_made = grad_beside(at, (v.cotangent_all, v.inner, 0, units))
    v.close(at)
    v.down_blocks = [merge_blocks(v.down_across, v.down_beside)]
    del v.down_across, v.down_beside, v.down, v.near, v.far

    v.down_sent = flip_all(at, v.down_made[:-1])
    (v.pair_low,) = call(
        at,
        functools.partial(mlp_back_kernel, count),
        [(wide, BF16)],
        v.cotangent_all,
        *v.down_blocks[0],
        v.gate_factor,
        v.up_factor,
        steps=tokens // TILE,
        tiles={
            0: rows_of((tokens, width), TILE),
            1 + count: rows_of(thin, TILE),
            2 + count: rows_of(thin, TILE),
        },
        out_tiles={0: rows_of(wide, TILE)},
        name="mlp_back",
    )
    v.other = expand(at, v.pair_low, v.pair_blocks, 1, BF16)
    v.own = expand(at, v.pair_low, v.pair_blocks, 0, F32)
    v.down_own = grad_own(at, (v.cotangent_all, v.inner, 0, units))
    v.close(at)

    v.other = at.flip(v.other, c=1)
    v.down_cross = grad_across(at, (v.cotangent_all, v.inner, 0, units), v.down_sent)
    v.first_made = grad_beside(at, (v.normed2, v.pair_low, 0, first))
    v.close(at)

    v.terms = at.swap(add(at, v.own, v.other), at.sides)
    v.down_far = push_all(at, v.down_cross)
    v.down_sent += flip_all(at, v.down_made[-1:])
    v.first_sent = flip_all(at, v.first_made[:-1])
    v.second_made = grad_beside(at, (v.normed2, v.pair_low, first, second))
    v.first_own = grad_own(at, (v.normed2, v.pair_low, 0, first))
    v.second_own = grad_own(at, (v.normed2, v.pair_low, first, second))
    v.result_other = expand(at, v.inner, v.down_blocks, 1, BF16)
    v.result_own = expand(at, v.inner, v.down_blocks, 0, F32)
    v.close(at)
    del v.down_cross, v.down_made, v.own, v.other

    v.hidden_grad, branch_four, v.gain_two_grad, v.shift_two_grad = call(
        at,
        branch_kernel,
        [((near, width), F32), ((4 * near, width), BF16)] + [((1, width), F32)] * 2,
        v.hidden,
        v.cotangent,
        v.gains[2],
        v.terms,
        name="branch",
    )
    v.near = at.swap(branch_four, at.sides)
    v.first_far = push_all(at, grad_across(at, (v.normed2, v.pair_low, 0, first), v.first_sent))
    v.first_sent += flip_all(at, v.first_made[-1:])
    v.second_sent = flip_all(at, v.second_made[:-1])
    v.result_other = at.flip(v.result_other, c=1)
    v.down_total = add(at, v.down_own, v.down_sent[-1], *v.down_far)
    v.close(at)
    del v.first_made, v.down_own, v.down_sent, v.down_far

    v.far = at.flip(v.near, c=1)
    v.second_far = push_all(
        at, grad_across(at, (v.normed2, v.pair_low, first, second), v.second_sent)
    )
    v.second_sent += flip_all(at, v.second_made[-1:])
    v.down_pieces = at.swap(v.down_total, at.groups)
    v.branch, v.attended_grad = call(
        at,
        functools.partial(attended_grad_kernel, count),
        [((tokens, width), BF16), ((tokens, part), BF16)],
        v.near,
        v.far,
        *v.out_blocks[0],
        steps=tokens // TILE,
        tiles=near_far(v.near, v.far),
        out_tiles={0: rows_of((tokens, width), TILE), 1: rows_of((tokens, part), TILE)},
        name="attended_grad",
    )
    v.mixed_low, v.bias_part = call(
        at,
        attend_back_kernel,
        [((tokens, 3 * part), BF16), ((1, 3 * part), F32)],
        v.attended_grad,
        v.mixed,
        v.sums,
        v.table,
        v.row,
        v.col,
        scratch=[pltpu.VMEM((tokens, part), F32)] * 3,
        name="attend_back",
    )
    v.qkv_made = grad_beside(at, (v.normed, v.mixed_low, 0, 3 * part))
    v.other = expand(at, v.mixed_low, v.qkv_blocks, 1, BF16)
    v.own = expand(at, v.mixed_low, v.qkv_blocks, 0, F32)
    v.out_made = grad_beside(at, (v.branch, v.attended, 0, part))
    v.first_total = add(at, v.first_own, v.first_sent[-1], *v.first_far)
    v.result_terms = add(at, v.result_own, v.result_other)
    v.close(at)
    del v.near, v.far, v.second_made, v.attended_grad, v.down_total, v.result_own, v.result_other
    del v.first_own, v.first_sent, v.first_far

    v.other = at.flip(v.other, c=1)
    v.qkv_sent = flip_all(at, v.qkv_made[:-1])
    v.out_sent = flip_all(at, v.out_made)
    v.result_terms = at.swap(v.result_terms, at.sides)
    v.qkv_own = grad_own(at, (v.normed, v.mixed_low, 0, 3 * part))
    v.out_own = grad_own(at, (v.branch, v.attended, 0, part))
    v.second_total = add(at, v.second_own, v.second_sent[-1], *v.second_far)
    (v.down_grad,) = grad_spread(at, [v.down_pieces], (1,), (8 * units,))
    v.close(at)
    del v.second_own, v.second_sent, v.second_far, v.down_pieces

    v.qkv_far = push_all(at, grad_across(at, (v.normed, v.mixed_low, 0, 3 * part), v.qkv_sent))
    v.terms = at.swap(add(at, v.own, v.other), at.sides)
    v.qkv_sent += flip_all(at, v.qkv_made[-1:])
    v.first_pieces = at.swap(v.first_total, at.groups)
    v.out_cross = grad_across(at, (v.branch, v.attended, 0, part), v.out_sent)
    (v.result,) = call(
        at, result_kernel, [((near, width), BF16)], v.hidden, v.result_terms, name="result"
    )
    v.result = to_absolute(at, v.result)
    v.close(at)

    v.qkv_pieces = at.swap(add(at, v.qkv_own, v.qkv_sent[-1], *v.qkv_far), at.groups)
    v.out_far = push_all(at, v.out_cross)
    v.second_pieces = at.swap(v.second_total, at.groups)
    v.input_grad, v.gain_one_grad, v.shift_one_grad = call(
        at,
        input_kernel,
        [((near, width), F32)] + [((1, width), F32)] * 2,
        v.inputs,
        v.hidden_grad,
        v.gains[0],
        v.terms,
        name="inputs",
    )
    v.close(at)
    v.out_pieces = at.swap(add(at, v.out_own, v.out_sent[-1], *v.out_far), at.groups)
    input_grad = to_absolute(at, v.input_grad)
    gate_wgrad, up_wgrad = grad_spread(
        at, [v.first_pieces, v.second_pieces], (1, 1), (8 * units,) * 2
    )
    (qkv_wgrad,) = grad_spread(at, [v.qkv_pieces], (3,), (24 * part,))
    (out_wgrad,) = grad_spread(at, [v.out_pieces], (1,), (8 * part,))
    result, down_grad, bias_part = v.result, v.down_grad, v.bias_part
    gain_one_grad, shift_one_grad = v.gain_one_grad, v.shift_one_grad
    gain_two_grad, shift_two_grad = v.gain_two_grad, v.shift_two_grad

    bias_part = bias_part.reshape(3, 1, part)
    own_slot = (jnp.arange(8) == slot).astype(F32)[None, :, None]
    bias_whole = (bias_part * own_slot).reshape(at.outer, 2, 2, 4, bias_rows).swapaxes(1, 2)
    bias_whole = jnp.roll(bias_whole, -at.a, axis=0)
    bias_whole = pick(at.e, bias_whole, bias_whole[:, ::-1]).reshape(at.outer, 2, 8, bias_rows)
    grads = [
        v.reshape(at.outer, 2, 8, rows)
        for v in (gain_one_grad, shift_one_grad, gain_two_grad, shift_two_grad)
    ]
    shares = deliver_small(at, jnp.concatenate([bias_whole] + grads, axis=-1))

    def share(i):
        return shares[bias_rows + i * rows : bias_rows + (i + 1) * rows]

    return (
        result,
        input_grad,
        share(0),
        share(1),
        qkv_wgrad,
        shares[:bias_rows],
        out_wgrad,
        share(2),
        share(3),
        gate_wgrad,
        up_wgrad,
        down_grad,
    )


def solution(mesh):
    both = ("fsdp", "seq")
    wide = P(both, None)
    flat = P(both)
    return jax.shard_map(
        body,
        mesh=mesh,
        in_specs=(
            wide, P("fsdp", None), P("fsdp"), flat, flat, wide, flat,
            wide, flat, flat, wide, wide, wide, wide,
        ),
        out_specs=(wide, wide, flat, flat, wide, flat, wide, flat, flat, wide, wide, wide),
        check_vma=False,
    )
```

```python
import functools
import math

import jax
import jax.numpy as jnp
from jax import lax
from jax.experimental import pallas as pl
from jax.experimental.pallas import tpu as pltpu
from jax.sharding import PartitionSpec as P

HEADS = 32
HEAD_DIM = 64
AXES = ("fsdp", "seq")
F32 = jnp.float32
BF16 = jnp.bfloat16


def centered_of(values):
    centered = values - jnp.mean(values, axis=-1, keepdims=True)
    spread = jnp.mean(centered * centered, axis=-1, keepdims=True)
    return centered, lax.rsqrt(spread + 1e-05)


def norm_back(values, gain, grad):
    centered, scale = centered_of(values)
    hat = centered * scale
    lifted = grad * gain
    inner = jnp.mean(lifted * hat, axis=-1, keepdims=True)
    pulled = scale * (lifted - jnp.mean(lifted, axis=-1, keepdims=True) - hat * inner)
    return (
        pulled,
        jnp.sum(grad * hat, axis=0, keepdims=True),
        jnp.sum(grad, axis=0, keepdims=True),
    )


def rotary_tables(spots):
    inverse = 10000.0 ** (-jnp.arange(8).astype(F32) / 8.0)
    angle = inverse[:, None] * spots.astype(F32)[None]
    waves = jnp.concatenate([jnp.cos(angle), jnp.sin(angle)], axis=0)
    lane = jnp.arange(2 * HEAD_DIM) % HEAD_DIM
    row = jnp.arange(16)[:, None]
    turn = row - 8
    picks = [
        (row < 8) & (lane < 16) & (lane % 8 == row),
        (lane < 8) & (lane == turn),
        (lane >= 8) & (lane < 16) & (lane - 8 == turn),
    ]
    signs = (1.0, -1.0, 1.0)
    chosen = jnp.concatenate([p.astype(F32) * g for p, g in zip(picks, signs)], axis=1)
    rest = jnp.concatenate([(lane >= 16).astype(F32), jnp.zeros(4 * HEAD_DIM, F32)])
    table = lax.dot_general(
        waves, chosen, (((0,), (0,)), ((), ())), precision=lax.Precision.HIGHEST
    )
    return table + rest


def turned(values, table, sign):
    wide = values.shape[1]
    many = wide // (2 * HEAD_DIM)
    keep, later, earlier = (
        jnp.concatenate([table[:, i * 128 : (i + 1) * 128]] * many, axis=1) for i in range(3)
    )
    partner = pltpu.roll(values, wide - 8, 1) * later + pltpu.roll(values, 8, 1) * earlier
    return values * keep + sign * partner


def dot_rows(left, right, kind=F32):
    return lax.dot_general(
        left, right, (((0,), (0,)), ((), ())), preferred_element_type=F32
    ).astype(kind)


def dot_cols(left, right, kind=F32):
    return lax.dot_general(
        left, right, (((1,), (1,)), ((), ())), preferred_element_type=F32
    ).astype(kind)


def dot(left, right):
    return jnp.dot(left, right, preferred_element_type=F32)


class Places:
    def __init__(self):
        self.fsdp = lax.axis_size("fsdp")
        self.seq = lax.axis_size("seq")
        self.count = self.fsdp * self.seq
        self.outer = self.fsdp // 4
        spot = lax.axis_index("fsdp")
        side = lax.axis_index("seq")
        self.a = spot // 4
        self.b = (spot // 2) % 2
        self.e = spot % 2
        self.x = side // 2
        self.c = side % 2
        self.last = None
        high, low = 2 * self.seq, self.seq
        self.groups = [
            [(a * 4 + e) * low + b * high + i for b in range(2) for i in range(low)]
            for a in range(self.outer)
            for e in range(2)
        ]
        self.sides = [group[c::2] for group in self.groups for c in range(2)]

    def after(self, values):
        if self.last is None:
            return values
        values, self.last = lax.optimization_barrier((values, self.last))
        return values

    def move(self, values, pairs):
        return lax.ppermute(values, AXES, pairs)

    def flip(self, values, c=0, x=0, e=0, b=0):
        mask = c + 2 * x + self.seq * (e + 2 * b)
        return self.move(values, [(i, i ^ mask) for i in range(self.count)])

    def shift(self, values, steps):
        stride = 4 * self.seq * steps
        return self.move(values, [((i + stride) % self.count, i) for i in range(self.count)])

    def push(self, values, steps):
        stride = 4 * self.seq * steps
        return self.move(values, [(i, (i + stride) % self.count) for i in range(self.count)])

    def push_beside(self, values, steps):
        stride = 4 * self.seq * steps
        pairs = [(i, (i + stride) % self.count ^ self.seq) for i in range(self.count)]
        return self.move(values, pairs)

    def swap(self, values, groups):
        parts = len(groups[0])
        view = values.reshape(parts, values.shape[0] // parts, values.shape[1])
        view = lax.all_to_all(view, AXES, 0, 0, axis_index_groups=groups, tiled=True)
        return view.reshape(values.shape)


class Window:
    def close(self, at):
        values, tree = jax.tree.flatten(self.__dict__)
        self.__dict__.update(jax.tree.unflatten(tree, lax.optimization_barrier(values)))
        at.last = None


def pick(bit, first, second):
    return jnp.where(bit == 0, first, second)


def joined(bit, own, other, axis):
    return pick(
        bit, jnp.concatenate([own, other], axis=axis), jnp.concatenate([other, own], axis=axis)
    )


def order_kernel(width, spots_ref, ref, *outs):
    for i in range(ref.shape[1] // width):
        start = pl.multiple_of(spots_ref[i] * width, 128)
        block = ref[:, pl.ds(start, width)]
        for out in outs:
            for k in range(out.shape[0] // ref.shape[0]):
                rows = slice(k * ref.shape[0], (k + 1) * ref.shape[0])
                out[rows, i * width : (i + 1) * width] = block


def reorder(at, spots, values, copies):
    width = values.shape[1] // len(spots)
    if width % 128:
        cols = [lax.dynamic_slice_in_dim(values, spot * width, width, 1) for spot in spots]
        ordered = jnp.concatenate(cols, axis=1)
        return [jnp.concatenate([ordered] * n, axis=0) for n in copies]
    order = jnp.stack(spots).astype(jnp.int32)
    rows, wide = values.shape
    outs = [((n * rows, wide), values.dtype) for n in copies]
    return call(at, functools.partial(order_kernel, width), outs, order, values, name="order")


def to_relative(at, values, copies):
    spots = [
        (((at.a + i) % at.outer) * 2 + k) * 2 + (at.e ^ j)
        for i in range(at.outer)
        for j in range(2)
        for k in range(2)
    ]
    return reorder(at, spots, values, copies)


def to_absolute(at, values):
    spots = [
        (((i - at.a) % at.outer) * 2 + (at.e ^ j)) * 2 + k
        for i in range(at.outer)
        for k in range(2)
        for j in range(2)
    ]
    return reorder(at, spots, values, [1])


def rows_of(shape, rows, index=lambda i: i):
    return pl.BlockSpec((rows, shape[1]), lambda i: (index(i), 0))


def need(args, outs, scratch, tiles, out_tiles):
    total = 6 * 2**20
    for shapes, given in (
        ([(v.shape, v.dtype) for v in args], tiles),
        (list(outs), out_tiles),
        ([(v.shape, v.dtype) for v in scratch], None),
    ):
        for k, (shape, kind) in enumerate(shapes):
            block = given[k].block_shape if given and k in given else shape
            total += math.prod(block) * jnp.dtype(kind).itemsize * (1 + (block is not shape)) * 9 // 8
    return total


def call(at, kernel, outs, *args, steps=1, tiles=None, out_tiles=None, scratch=(), name=None):
    def spec(shape, kind, k, given):
        if given and k in given:
            return given[k]
        if kind == jnp.int32:
            return pl.BlockSpec(memory_space=pltpu.SMEM)
        zeros = (0,) * len(shape)
        return pl.BlockSpec(shape, lambda i: zeros, pipeline_mode=pl.Buffered(1))

    least = min(range(len(args)), key=lambda i: args[i].size)
    in_specs = [spec(v.shape, v.dtype, k, tiles) for k, v in enumerate(args)]
    args = list(args)
    args[least] = at.after(args[least])
    results = pl.pallas_call(
        kernel,
        grid=(steps,),
        out_shape=[jax.ShapeDtypeStruct(shape, kind) for shape, kind in outs],
        in_specs=in_specs,
        out_specs=[spec(shape, kind, k, out_tiles) for k, (shape, kind) in enumerate(outs)],
        scratch_shapes=list(scratch),
        compiler_params=pltpu.CompilerParams(
            vmem_limit_bytes=max(need(args, outs, scratch, tiles, out_tiles), 20 * 2**20)
        ),
        cost_estimate=pl.CostEstimate(flops=0, bytes_accessed=0, transcendentals=0),
        name=name,
    )(*args)
    at.last = min(results, key=lambda v: v.size)
    return results


TILE = 256


def product(values, chunks):
    outs = []
    for blocks in chunks:
        depth = blocks[0].shape[0]
        total = dot(values[:, :depth], blocks[0][...])
        for i, block in enumerate(blocks[1:], 1):
            total = total + dot(values[:, i * depth : (i + 1) * depth], block[...])
        outs.append(total)
    return outs[0] if len(outs) == 1 else jnp.concatenate(outs, axis=1)


def in_chunks(refs, count):
    return [refs[i : i + count] for i in range(0, len(refs), count)]


def transposed_product(values, chunks, j):
    total, col = None, 0
    for blocks in chunks:
        width = blocks[j].shape[1]
        term = dot_cols(values[:, col : col + width], blocks[j][...])
        total = term if total is None else total + term
        col += width
    return total


def tile_of(i):
    return pl.ds(pl.multiple_of(i * TILE, TILE), TILE)


def gathered(pieces, out):
    rows = pieces[0].shape[0]
    for i in range(4):

        @pl.when(pl.program_id(0) == i)
        def _():
            out[:rows, :] = pieces[2 * i][...]
            out[rows:, :] = pieces[2 * i + 1][...]


def qkv_kernel(count, *refs):
    pieces, blocks = refs[:8], refs[8:-7]
    gain, shift, bias, table, normed, mixed, tile = refs[-7:]
    gathered(pieces, tile)
    centered, scale = centered_of(tile[...].astype(F32))
    normed[...] = (centered * scale * gain[...] + shift[...]).astype(BF16)
    turning = mixed.shape[1] * 2 // 3
    values = product(normed, in_chunks(blocks, count)) + bias[...]
    both = turned(values[:, :turning], table[...], 1.0).astype(BF16)
    mixed[:, : turning // 2] = both[:, : turning // 2] * 0.125
    mixed[:, turning // 2 : turning] = both[:, turning // 2 :]
    mixed[:, turning:] = values[:, turning:].astype(BF16)


def attended_grad_kernel(count, *refs):
    pieces, blocks = refs[:8], refs[8:-2]
    whole, grads = refs[-2:]
    gathered(pieces, whole)
    grads[...] = product(whole, in_chunks(blocks, count)).astype(BF16)


def head_of(ref, group, head, start):
    part = ref.shape[1] // 3
    low = group * part + head * HEAD_DIM
    return ref[pl.ds(pl.multiple_of(start, TILE), TILE), low : low + HEAD_DIM]


def both_halves(ref, group, head, start, half):
    return jnp.concatenate(
        [head_of(ref, group, head, start), head_of(ref, group, head, start + half)], axis=0
    )


def allowed_at(row, col, sequence, turn):
    spot = pl.ds(pl.multiple_of(turn * TILE, TILE), TILE)
    ours = jnp.where(sequence == 0, row[0:1, spot], row[1:2, spot])
    theirs = jnp.where(sequence == 0, col[:, 0:1], col[:, 1:2])
    return (theirs == ours) & (col[:, 2:3] <= row[2:3, spot])


def scores_of(key, query, allowed):
    return jnp.where(allowed, dot_cols(key, query), -1e30)


def attend_kernel(mixed, row, col, attended, sums):
    half = mixed.shape[0] // 2
    heads = attended.shape[1] // HEAD_DIM

    @pl.loop(0, 4)
    def _(i):
        sequence, turn = i // 2, i % 2
        allowed = allowed_at(row, col, sequence, turn)
        start = turn * half + sequence * TILE
        span = pl.ds(pl.multiple_of(start, TILE), TILE)
        for h in range(heads):
            key = both_halves(mixed, 1, h, sequence * TILE, half)
            value = both_halves(mixed, 2, h, sequence * TILE, half)
            scores = scores_of(key, head_of(mixed, 0, h, start), allowed)
            top = jnp.max(scores, axis=0, keepdims=True)
            expo = jnp.exp(scores - top)
            total = jnp.sum(expo, axis=0, keepdims=True)
            out = jnp.transpose(dot_rows(value, (expo * (1.0 / total)).astype(BF16)))
            attended[span, h * HEAD_DIM : (h + 1) * HEAD_DIM] = out.astype(BF16)
            sums[pl.ds(i * heads + h, 1), :] = top + jnp.log(total)


def attend_back_kernel(
    grads, mixed, sums, table, row, col, low, bias, query_sum, key_sum, value_sum
):
    half = mixed.shape[0] // 2
    part = grads.shape[1]
    heads = part // HEAD_DIM

    for sequence in range(2):
        for turn in range(2):
            i = sequence * 2 + turn
            allowed = allowed_at(row, col, sequence, turn)
            start = turn * half + sequence * TILE
            span = pl.ds(start, TILE)
            for h in range(heads):
                cols = slice(h * HEAD_DIM, (h + 1) * HEAD_DIM)
                query = head_of(mixed, 0, h, start)
                key = both_halves(mixed, 1, h, sequence * TILE, half)
                value = both_halves(mixed, 2, h, sequence * TILE, half)
                grad = grads[span, cols]
                scores = scores_of(key, query, allowed)
                probs = jnp.exp(scores - sums[i * heads + h : i * heads + h + 1, :])
                probs_grad = dot_cols(value, grad)
                value_grad = dot(probs.astype(BF16), grad)
                center = jnp.sum(probs * probs_grad, axis=0, keepdims=True)
                scores_low = (probs * (probs_grad - center)).astype(BF16)
                key_grad = dot(scores_low, query)
                query_sum[span, cols] = jnp.transpose(dot_rows(key, scores_low))
                for k in range(2):
                    keys = pl.ds(k * half + sequence * TILE, TILE)
                    rows = slice(k * TILE, (k + 1) * TILE)
                    if turn == 0:
                        key_sum[keys, cols] = key_grad[rows]
                        value_sum[keys, cols] = value_grad[rows]
                    else:
                        key_sum[keys, cols] += key_grad[rows]
                        value_sum[keys, cols] += value_grad[rows]

    bias[...] = jnp.zeros_like(bias)

    @pl.loop(0, mixed.shape[0] // TILE)
    def _(i):
        span = tile_of(i)
        factors = table[span, :]
        for k, ref in enumerate((query_sum, key_sum, value_sum)):
            values = ref[span, :]
            if k == 0:
                values = values * 0.125
            if k < 2:
                values = turned(values, factors, -1.0)
            values = values.astype(BF16)
            low[span, k * part : (k + 1) * part] = values
            bias[:, k * part : (k + 1) * part] += jnp.sum(
                values.astype(F32), axis=0, keepdims=True
            )


def expand_kernel(count, values, *refs):
    *blocks, out = refs
    chunks = in_chunks(blocks, count)
    width = blocks[0].shape[0]
    for j in range(count):
        total = transposed_product(values, chunks, j)
        out[:, j * width : (j + 1) * width] = total.astype(out.dtype)


def total_of(terms):
    total = terms[0][...].astype(F32)
    for term in terms[1:]:
        total = total + term[...].astype(F32)
    return total


def hidden_kernel(inputs, gain, shift, *refs):
    *terms, hidden, normed = refs
    values = inputs[...].astype(F32) + total_of(terms)
    hidden[...] = values
    centered, scale = centered_of(values)
    normed[...] = (centered * scale * gain[...] + shift[...]).astype(BF16)


def result_kernel(hidden, *refs):
    *terms, out = refs
    out[...] = (hidden[...] + total_of(terms)).astype(BF16)


def branch_kernel(hidden, cotangent, gain, *refs):
    *terms, grad, low, gain_grad, shift_grad = refs
    pulled, gain_grad[...], shift_grad[...] = norm_back(hidden[...], gain[...], total_of(terms))
    values = cotangent[...].astype(F32) + pulled
    grad[...] = values
    low[...] = values.astype(BF16)


def input_kernel(inputs, hidden_grad, gain, *refs):
    *terms, grad, gain_grad, shift_grad = refs
    pulled, gain_grad[...], shift_grad[...] = norm_back(
        inputs[...].astype(F32), gain[...], total_of(terms)
    )
    grad[...] = hidden_grad[...] + pulled


def mlp_kernel(count, *refs):
    pieces, blocks = refs[:8], refs[8:-4]
    normed, inner, gate_factor, up_factor = refs[-4:]
    units = gate_factor.shape[1]
    gathered(pieces, normed)
    values = product(normed, in_chunks(blocks, count))
    gate, up = values[:, :units], values[:, units:]
    sigmoid = 1.0 / (1.0 + jnp.exp(-gate))
    silu = gate * sigmoid
    inner[:, :units] = (silu * up).astype(BF16)
    if inner.shape[1] > units:
        inner[:, units:] = jnp.zeros((inner.shape[0], inner.shape[1] - units), BF16)
    gate_factor[...] = up * sigmoid * (1.0 + gate * (1.0 - sigmoid))
    up_factor[...] = silu


def mlp_back_kernel(count, grads, *refs):
    *blocks, gate_factor, up_factor, pair = refs
    values = product(grads, in_chunks(blocks, count))[:, : gate_factor.shape[1]]
    pair[...] = jnp.concatenate(
        [(values * gate_factor[...]).astype(BF16), (values * up_factor[...]).astype(BF16)],
        axis=1,
    )


def segments(widths, chunks):
    out = []
    at_part = at_chunk = part = chunk = 0
    while part < len(widths):
        size = min(widths[part] - at_part, chunks[chunk] - at_chunk)
        out.append((part, at_part, chunk, at_chunk, size))
        at_part, at_chunk = at_part + size, at_chunk + size
        if at_part == widths[part]:
            part, at_part = part + 1, 0
        if at_chunk == chunks[chunk]:
            chunk, at_chunk = chunk + 1, 0
    return out


def part_list(refs, counts):
    return [
        (ref, p, ref.shape[1] // (8 * count)) for ref, count in zip(refs, counts) for p in range(count)
    ]


def cut_kernel(counts, *refs):
    *weights, out = refs
    rows = weights[0].shape[0]
    col = 0
    for ref, p, width in part_list(weights, counts):
        for j in range(8):
            start = (p * 8 + j) * width
            out[j * rows : (j + 1) * rows, col : col + width] = ref[:, start : start + width]
        col += width
    if col < out.shape[1]:
        out[:, col:] = jnp.zeros((out.shape[0], out.shape[1] - col), BF16)


def spread_kernel(counts, strips, *refs):
    chunks, outs = refs[: -len(counts)], refs[-len(counts) :]
    rows = outs[0].shape[0]
    parts = part_list(outs, counts)
    cuts = segments([width for _, _, width in parts], [width for _, _, width in strips])
    for part, begin, strip, col, size in cuts:
        ref, p, width = parts[part]
        chunk, first, _ = strips[strip]
        for j in range(8):
            start = (p * 8 + j) * width + begin
            piece = chunks[chunk][j * rows : (j + 1) * rows, first + col : first + col + size]
            ref[:, start : start + size] = piece.astype(F32)


def sum_kernel(counts, *refs):
    *terms, out = refs
    col = 0
    for count in counts:
        mine, terms = terms[:count], terms[count:]
        total = mine[0][...].astype(F32)
        for term in mine[1:]:
            total = total + term[...].astype(F32)
        out[:, col : col + total.shape[1]] = total.astype(BF16)
        col += total.shape[1]


def cut_rows(at, weights, counts, wide):
    (out,) = call(
        at,
        functools.partial(cut_kernel, counts),
        [((8 * weights[0].shape[0], wide), BF16)],
        *weights,
        name="cut",
    )
    return out


def split_kernel(col, whole, *outs):
    for out in outs:
        out[...] = whole[:, col : col + out.shape[1]]
        col += out.shape[1]


def split(at, whole, begin, widths):
    outs = [((whole.shape[0], n), BF16) for n in widths]
    return call(at, functools.partial(split_kernel, begin), outs, whole, name="split")


def cross_block(at, block):
    return [block] + [at.shift(block, i) for i in range(1, at.outer)]


def merge_blocks(across, beside):
    return [block for pair in zip(across, beside) for block in pair]


def send_block(at, block):
    return [block] + [at.shift(block, i) for i in range(1, at.outer)]


def grad_kernel(count, ways, *refs):
    many = 2 * len(ways)
    pairs, addends, outs = refs[:many], refs[many : many + count], refs[many + count :]
    each = pl.num_programs(0) // len(outs)
    for k, out in enumerate(outs):

        @pl.when(pl.program_id(0) // each == k)
        def _():
            col = 0
            for i, (begin, size) in enumerate(ways):
                values, grads = pairs[2 * i : 2 * i + 2]
                total = dot_rows(values[...], grads[:, begin : begin + size])
                if k < count:
                    total = total + addends[k][:, col : col + size].astype(F32)
                out[:, col : col + size] = total.astype(out.dtype)
                col += size


def grad_blocks(at, ways, spots, kind, addends=()):
    tokens, wide = ways[0][0].shape
    width = wide // (2 * at.outer)
    tile = min(TILE, width)
    each = width // tile

    def column(i):
        spot = spots[0]
        for k in range(1, len(spots)):
            spot = jnp.where(i // each == k, spots[k], spot)
        return spot * each + i % each

    def row_of(k):
        return lambda i: jnp.clip(i - k * each, 0, each - 1)

    shape = (width, sum(way[3] for way in ways))
    tiles = {2 * i: pl.BlockSpec((tokens, tile), lambda i: (0, column(i))) for i in range(len(ways))}
    for k in range(len(addends)):
        tiles[2 * len(ways) + k] = rows_of(shape, tile, row_of(k))
    return call(
        at,
        functools.partial(grad_kernel, len(addends), tuple(way[2:] for way in ways)),
        [(shape, kind)] * len(spots),
        *[v for way in ways for v in way[:2]],
        *addends,
        steps=len(spots) * each,
        tiles=tiles,
        out_tiles={k: rows_of(shape, tile, row_of(k)) for k in range(len(spots))},
        name="grad",
    )


def grad_beside(at, *way):
    order = list(range(1, at.outer)) + [0]
    return grad_blocks(at, way, [2 * i + 1 for i in order], BF16)


def grad_own(at, *way):
    return grad_blocks(at, way, [0], F32)[0]


def grad_across(at, sent, *way):
    if at.outer == 1:
        return []
    return grad_blocks(at, way, [2 * i for i in range(1, at.outer)], BF16, sent[: at.outer - 1])


def push_all(at, made):
    return [at.push(v, i) for i, v in enumerate(made, 1)]


def flip_all(at, made):
    return [at.flip(v, e=1) for v in made]


def grad_spread(at, chunks, counts, strips, widths):
    rows = chunks[0].shape[0] // 8
    return call(
        at,
        functools.partial(spread_kernel, counts, strips),
        [((rows, n), F32) for n in widths],
        *chunks,
        name="spread",
    )


def join_kernel(place, near, far, out):
    rows = near.shape[0] // 4
    for half, ref in enumerate((near, far)):
        for d in range(4):
            start = pl.multiple_of((place[0] ^ d) * rows, rows)
            low = (half * 4 + d) * rows
            out[low : low + rows, :] = ref[pl.ds(start, rows), :]


def joined_rows(at, near, far):
    place = jnp.reshape(at.b * 2 + at.x, (1,)).astype(jnp.int32)
    shape = (2 * near.shape[0], near.shape[1])
    (out,) = call(at, join_kernel, [(shape, BF16)], place, near, far, name="join")
    return out


def spread_tokens(at, values):
    low = at.flip(values, b=1)
    beside = at.flip(values, x=1)
    return [values, beside, low, at.flip(low, x=1)]


def send_pieces(at, pieces):
    return [pieces[0], at.flip(pieces[1], x=1), pieces[2], at.flip(pieces[3], x=1)]


def pass_pieces(at, pieces):
    return [pieces[0], pieces[1], at.flip(add(at, pieces[2:]), b=1)]


def expand_add_kernel(count, values, *refs):
    blocks, other, outs = refs[:-5], refs[-5], refs[-4:]
    chunks = in_chunks(blocks, count)
    width = blocks[0].shape[0]
    rows = outs[0].shape[0]
    for j in range(count):
        cols = slice(j * width, (j + 1) * width)
        total = transposed_product(values, chunks, j) + other[:, cols].astype(F32)
        total = total.astype(BF16)
        for i in range(2):

            @pl.when(pl.program_id(0) == i)
            def _():
                outs[2 * i][:, cols] = total[:rows]
                outs[2 * i + 1][:, cols] = total[rows:]


def expand_pieces(at, values, chunks, other):
    blocks = [block for chunk in chunks for block in chunk]
    shape = (other.shape[0] // 4, other.shape[1])
    return call(
        at,
        functools.partial(expand_add_kernel, len(chunks[0])),
        [(shape, BF16)] * 4,
        values,
        *blocks,
        other,
        steps=other.shape[0] // TILE,
        tiles={
            0: rows_of(values.shape, TILE),
            1 + len(blocks): rows_of(other.shape, TILE),
        },
        name="expand_add",
    )


def add_pieces_kernel(own, other, *outs):
    rows = outs[0].shape[0]
    for d, out in enumerate(outs):
        span = slice(d * rows, (d + 1) * rows)
        out[...] = (own[span, :] + other[span, :].astype(F32)).astype(BF16)


def add_pieces(at, own, other):
    shape = (own.shape[0] // 4, own.shape[1])
    return call(at, add_pieces_kernel, [(shape, BF16)] * 4, own, other, name="pieces")


def expand(at, values, chunks, side, kind):
    half = values.shape[0] // 2
    blocks = [block for chunk in chunks for block in chunk]
    count = len(chunks[0])
    shape = (half, blocks[0].shape[0] * count)
    steps = half // TILE
    (out,) = call(
        at,
        functools.partial(expand_kernel, count),
        [(shape, kind)],
        values,
        *blocks,
        steps=steps,
        tiles={0: rows_of(values.shape, TILE, lambda i: i + side * steps)},
        out_tiles={0: rows_of(shape, TILE)},
        name="expand",
    )
    return out


def add(at, *sums):
    rows = sums[0][0].shape[0]
    tile = min(TILE, rows)
    terms = [v for each in sums for v in each]
    shape = (rows, sum(each[0].shape[1] for each in sums))
    (total,) = call(
        at,
        functools.partial(sum_kernel, tuple(len(each) for each in sums)),
        [(shape, BF16)],
        *terms,
        steps=rows // tile,
        tiles={k: rows_of(v.shape, tile) for k, v in enumerate(terms)},
        out_tiles={0: rows_of(shape, tile)},
        name="add",
    )
    return total


def send_small(at, values):
    total = values[0, 0] + at.flip(values[0, 1], e=1)
    for i in range(1, at.outer):
        total = total + at.push(values[i, 0], i)
        total = total + at.push_beside(values[i, 1], i)
    return total


def order_tokens(at, values):
    seqs, length = values.shape
    view = values.reshape(seqs, 2, 2, length // 4)
    view = pick(at.x, view, view[:, ::-1])
    view = pick(at.c, view, view[:, :, ::-1])
    return jnp.swapaxes(view, 1, 2).reshape(seqs, length)


def body(
    layer_input,
    segment_ids,
    positions,
    ln1_gain,
    ln1_bias,
    qkv_weight,
    qkv_bias,
    out_weight,
    ln2_gain,
    ln2_bias,
    gate_weight,
    up_weight,
    down_weight,
    cotangent,
):
    at = Places()
    width = layer_input.shape[1]
    rows = qkv_weight.shape[0]
    bias_rows = qkv_bias.shape[0]
    length = segment_ids.shape[1]
    heads_here = HEADS // 8
    part = width // 8
    units = gate_weight.shape[1] // 8
    slot = at.b * 4 + at.x * 2 + at.c

    tokens = 2 * length
    count = 2 * at.outer
    near = layer_input.shape[0]

    second = 2 * units // 256 * 128
    first = 2 * units - second
    v = Window()
    padded = (units + 127) // 128 * 128
    thin, wide = (tokens, units), (tokens, 2 * units)

    v.front = at.swap(cut_rows(at, [qkv_weight, out_weight], (3, 1), 4 * part), at.groups)
    v.small = jnp.concatenate([at.after(qkv_bias), ln1_gain, ln1_bias, ln2_gain, ln2_bias])[None]
    v.small = joined(at.c, v.small, at.flip(v.small, c=1), 0)
    v.small = joined(at.x, v.small, at.flip(v.small, x=1), 0)
    (v.inputs,) = to_relative(at, layer_input, [1])
    v.later = cut_rows(at, [gate_weight, up_weight, down_weight], (1, 1, 1), 2 * units + padded)
    v.cotangent, v.cotangent_four = to_relative(at, cotangent, [1, 4])
    spots = jnp.concatenate([segment_ids, positions[None]], axis=0)[None]
    v.spots = jnp.concatenate([spots, at.flip(spots, b=1)], axis=0)
    v.close(at)

    v.qkv, v.out = split(at, v.front, 0, (3 * part, part))
    del v.front
    v.qkv_across = cross_block(at, v.qkv)
    v.qkv_beside = [at.flip(v.qkv, e=1)]
    v.tokens = spread_tokens(at, v.inputs)
    v.turned = [at.flip(v.tokens[1], c=1)]
    v.small = joined(at.b, v.small, at.flip(v.small, b=1), 0)
    v.small = jnp.stack([v.small] + [at.shift(v.small, i) for i in range(1, at.outer)])
    segments_here = order_tokens(at, v.spots[:, 0])
    places = order_tokens(at, v.spots[:, 1])
    index = order_tokens(at, jnp.arange(length)[None])
    v.row = jnp.concatenate([segments_here, index, jnp.zeros((5, length), index.dtype)], axis=0)
    v.row = v.row.astype(F32)
    v.col = jnp.pad(jnp.transpose(v.row), ((0, 0), (0, 120)))
    places = places.reshape(2, 2, length // 2).swapaxes(0, 1).reshape(2 * length)
    v.table = rotary_tables(places)
    v.close(at)

    v.qkv_beside += flip_all(at, v.qkv_across[1:])
    v.turned = [at.flip(v.tokens[0], c=1), *v.turned] + [at.flip(t, c=1) for t in v.tokens[2:]]
    v.out_across = cross_block(at, v.out)
    v.later = at.swap(v.later, at.groups)

    v.small = jnp.stack([v.small, at.flip(v.small, e=1)], axis=1)

    def vector(i):
        start = bias_rows + i * rows
        return v.small[..., start : start + rows].reshape(1, width).astype(F32)

    v.gains = [vector(i) for i in range(4)]
    bias = v.small[..., :bias_rows]
    bias = pick(at.e, bias, bias[:, ::-1])
    bias = jnp.roll(bias, at.a, axis=0)
    bias = bias.reshape(at.outer, 2, 2, 4, bias_rows).swapaxes(1, 2).reshape(3, 8, part)
    bias = lax.dynamic_index_in_dim(bias, slot, 1, keepdims=False)
    v.bias = bias.reshape(1, 3 * part).astype(F32)
    v.close(at)
    v.qkv_blocks = [merge_blocks(v.qkv_across, v.qkv_beside)]
    del v.qkv_across, v.qkv_beside, v.qkv, v.small, v.spots

    (v.first,) = split(at, v.later, 0, (first,))
    v.first_across = cross_block(at, v.first)
    v.first_beside = [at.flip(v.first, e=1)]
    v.out_beside = flip_all(at, v.out_across)
    v.cotangent_near = at.swap(v.cotangent_four, at.sides)
    v.normed, v.mixed = call(
        at,
        functools.partial(qkv_kernel, count),
        [((tokens, width), BF16), ((tokens, 3 * part), BF16)],
        *v.tokens,
        *v.turned,
        *v.qkv_blocks[0],
        v.gains[0],
        v.gains[1],
        v.bias,
        v.table,
        steps=tokens // TILE,
        tiles={11 + count: rows_of(v.table.shape, TILE)},
        out_tiles={0: rows_of((tokens, width), TILE), 1: rows_of((tokens, 3 * part), TILE)},
        scratch=[pltpu.VMEM((TILE, width), BF16)],
        name="qkv",
    )
    v.attended, v.sums = call(
        at,
        attend_kernel,
        [((tokens, part), BF16), ((4 * heads_here, TILE), F32)],
        v.mixed,
        v.row,
        v.col,
        name="attend",
    )
    v.out_blocks = [merge_blocks(v.out_across, v.out_beside)]
    v.other = expand(at, v.attended, v.out_blocks, 1, BF16)
    v.second, v.down = split(at, v.later, first, (second, padded))
    v.close(at)
    del v.later
    del v.out_across, v.out_beside, v.out, v.cotangent_four

    v.other = at.flip(v.other, c=1)
    v.cotangent_far = at.flip(v.cotangent_near, c=1)
    v.pieces = expand_pieces(at, v.attended, v.out_blocks, v.other)
    v.close(at)

    v.terms = pass_pieces(at, send_pieces(at, v.pieces))
    v.cotangent_all = joined_rows(at, v.cotangent_near, v.cotangent_far)
    v.second_across = cross_block(at, v.second)
    v.second_beside = [at.flip(v.second, e=1)]
    v.first_beside += flip_all(at, v.first_across[1:])
    v.close(at)
    del v.other, v.pieces, v.cotangent_near, v.cotangent_far

    v.hidden, normed2 = call(
        at,
        hidden_kernel,
        [((near, width), F32), ((near, width), BF16)],
        v.inputs,
        v.gains[2],
        v.gains[3],
        *v.terms,
        name="hidden",
    )
    v.tokens = spread_tokens(at, normed2)
    v.turned = [at.flip(v.tokens[1], c=1)]
    v.down_across = cross_block(at, v.down)
    v.down_beside = [at.flip(v.down, e=1)]
    v.second_beside += flip_all(at, v.second_across[1:])
    v.close(at)
    v.pair_blocks = [
        merge_blocks(v.first_across, v.first_beside),
        merge_blocks(v.second_across, v.second_beside),
    ]
    del v.first_across, v.first_beside, v.second_across, v.second_beside, v.first, v.second

    v.turned = [at.flip(v.tokens[0], c=1), *v.turned] + [at.flip(t, c=1) for t in v.tokens[2:]]
    v.down_beside += flip_all(at, v.down_across[1:])
    v.normed2, v.inner, v.gate_factor, v.up_factor = call(
        at,
        functools.partial(mlp_kernel, count),
        [((tokens, width), BF16), ((tokens, padded), BF16), (thin, F32), (thin, F32)],
        *v.tokens,
        *v.turned,
        *v.pair_blocks[0],
        *v.pair_blocks[1],
        steps=tokens // TILE,
        out_tiles={0: rows_of((tokens, width), TILE)}
        | {1: rows_of((tokens, padded), TILE)}
        | {k: rows_of(thin, TILE) for k in (2, 3)},
        name="mlp",
    )
    v.down_made = grad_beside(at, (v.cotangent_all, v.inner, 0, padded))
    v.close(at)
    v.down_blocks = [merge_blocks(v.down_across, v.down_beside)]
    del v.down_across, v.down_beside, v.down, v.tokens, v.turned

    v.down_sent = flip_all(at, v.down_made[:-1])
    (v.pair_low,) = call(
        at,
        functools.partial(mlp_back_kernel, count),
        [(wide, BF16)],
        v.cotangent_all,
        *v.down_blocks[0],
        v.gate_factor,
        v.up_factor,
        steps=tokens // TILE,
        tiles={
            0: rows_of((tokens, width), TILE),
            1 + count: rows_of(thin, TILE),
            2 + count: rows_of(thin, TILE),
        },
        out_tiles={0: rows_of(wide, TILE)},
        name="mlp_back",
    )
    v.other = expand(at, v.pair_low, v.pair_blocks, 1, BF16)
    v.own = expand(at, v.pair_low, v.pair_blocks, 0, F32)
    v.down_own = grad_own(at, (v.cotangent_all, v.inner, 0, padded))
    v.close(at)

    v.other = at.flip(v.other, c=1)
    v.down_cross = grad_across(at, v.down_sent, (v.cotangent_all, v.inner, 0, padded))
    v.first_made = grad_beside(at, (v.normed2, v.pair_low, first, second))
    v.pieces = add_pieces(at, v.own, v.other)
    v.close(at)

    v.terms = pass_pieces(at, send_pieces(at, v.pieces))
    v.down_far = push_all(at, v.down_cross)
    v.down_sent += flip_all(at, v.down_made[-1:])
    v.first_sent = flip_all(at, v.first_made[:-1])
    v.second_made = grad_beside(at, (v.normed2, v.pair_low, 0, first))
    v.first_own = grad_own(at, (v.normed2, v.pair_low, first, second))
    v.second_own = grad_own(at, (v.normed2, v.pair_low, 0, first))
    v.result_other = expand(at, v.inner, v.down_blocks, 1, BF16)
    v.result_own = expand(at, v.inner, v.down_blocks, 0, F32)
    v.close(at)
    del v.down_cross, v.down_made, v.own, v.other

    v.hidden_grad, branch, v.gain_two_grad, v.shift_two_grad = call(
        at,
        branch_kernel,
        [((near, width), F32), ((near, width), BF16)] + [((1, width), F32)] * 2,
        v.hidden,
        v.cotangent,
        v.gains[2],
        *v.terms,
        name="branch",
    )
    v.tokens = spread_tokens(at, branch)
    v.turned = [at.flip(v.tokens[1], c=1)]
    v.first_far = push_all(at, grad_across(at, v.first_sent, (v.normed2, v.pair_low, first, second)))
    v.first_sent += flip_all(at, v.first_made[-1:])
    v.second_sent = flip_all(at, v.second_made[:-1])
    v.close(at)
    del v.first_made, v.pieces

    v.turned = [at.flip(v.tokens[0], c=1), *v.turned] + [at.flip(t, c=1) for t in v.tokens[2:]]
    v.result_other = at.flip(v.result_other, c=1)
    v.early = add(
        at,
        [v.down_own, v.down_sent[-1], *v.down_far],
        [v.first_own, v.first_sent[-1], *v.first_far],
    )
    v.second_cross = grad_across(at, v.second_sent, (v.normed2, v.pair_low, 0, first))
    v.pieces = add_pieces(at, v.result_own, v.result_other)
    v.close(at)
    del v.first_own, v.first_sent, v.first_far, v.down_own, v.down_sent, v.down_far
    del v.result_own, v.result_other

    v.early = at.swap(v.early, at.groups)
    v.second_far = push_all(at, v.second_cross)
    v.second_sent += flip_all(at, v.second_made[-1:])
    v.branch, v.attended_grad = call(
        at,
        functools.partial(attended_grad_kernel, count),
        [((tokens, width), BF16), ((tokens, part), BF16)],
        *v.tokens,
        *v.turned,
        *v.out_blocks[0],
        steps=tokens // TILE,
        out_tiles={0: rows_of((tokens, width), TILE), 1: rows_of((tokens, part), TILE)},
        name="attended_grad",
    )
    v.out_sent = flip_all(at, grad_beside(at, (v.branch, v.attended, 0, part)))
    v.mixed_low, v.bias_part = call(
        at,
        attend_back_kernel,
        [((tokens, 3 * part), BF16), ((1, 3 * part), F32)],
        v.attended_grad,
        v.mixed,
        v.sums,
        v.table,
        v.row,
        v.col,
        scratch=[pltpu.VMEM((tokens, part), F32)] * 3,
        name="attend_back",
    )
    v.qkv_made = grad_beside(at, (v.normed, v.mixed_low, 0, 3 * part))
    v.other = expand(at, v.mixed_low, v.qkv_blocks, 1, BF16)
    v.close(at)
    del v.tokens, v.turned, v.second_made, v.second_cross, v.attended_grad

    v.late = at.swap(add(at, [v.second_own, v.second_sent[-1], *v.second_far]), at.groups)
    v.out_far = push_all(at, grad_across(at, v.out_sent, (v.branch, v.attended, 0, part)))
    v.other = at.flip(v.other, c=1)
    v.qkv_sent = flip_all(at, v.qkv_made[:-1])
    result_pieces = send_pieces(at, v.pieces)
    v.qkv_own = grad_own(at, (v.normed, v.mixed_low, 0, 3 * part))
    v.out_own = grad_own(at, (v.branch, v.attended, 0, part))
    v.result_terms = pass_pieces(at, result_pieces)
    v.pieces = expand_pieces(at, v.mixed_low, v.qkv_blocks, v.other)
    v.qkv_cross = grad_across(at, v.qkv_sent, (v.normed, v.mixed_low, 0, 3 * part))
    v.close(at)
    del v.second_own, v.second_sent, v.second_far

    v.qkv_far = push_all(at, v.qkv_cross)
    v.terms = pass_pieces(at, send_pieces(at, v.pieces))
    v.qkv_sent += flip_all(at, v.qkv_made[-1:])
    (v.result,) = call(
        at, result_kernel, [((near, width), BF16)], v.hidden, *v.result_terms, name="result"
    )
    (v.result,) = to_absolute(at, v.result)
    (v.down_grad,) = grad_spread(at, [v.early], (1,), ((0, 0, units),), (8 * units,))
    v.close(at)
    del v.other, v.qkv_made, v.pieces

    v.back = at.swap(
        add(
            at,
            [v.qkv_own, v.qkv_sent[-1], *v.qkv_far],
            [v.out_own, v.out_sent[-1], *v.out_far],
        ),
        at.groups,
    )
    v.input_grad, gain_one_grad, shift_one_grad = call(
        at,
        input_kernel,
        [((near, width), F32)] + [((1, width), F32)] * 2,
        v.inputs,
        v.hidden_grad,
        v.gains[0],
        *v.terms,
        name="inputs",
    )
    gate_wgrad, up_wgrad = grad_spread(
        at,
        [v.early, v.late],
        (1, 1),
        ((1, 0, first), (0, padded, second)),
        (8 * units,) * 2,
    )
    (input_grad,) = to_absolute(at, v.input_grad)
    v.done = [gate_wgrad, up_wgrad, input_grad]
    bias_part = v.bias_part.reshape(3, 1, part)
    own_slot = (jnp.arange(8) == slot).astype(F32)[None, :, None]
    bias_whole = (bias_part * own_slot).reshape(at.outer, 2, 2, 4, bias_rows).swapaxes(1, 2)
    bias_whole = jnp.roll(bias_whole, -at.a, axis=0)
    bias_whole = pick(at.e, bias_whole, bias_whole[:, ::-1]).reshape(at.outer, 2, 8, bias_rows)
    grads = [
        g.reshape(at.outer, 2, 8, rows)
        for g in (gain_one_grad, shift_one_grad, v.gain_two_grad, v.shift_two_grad)
    ]
    v.small = send_small(at, jnp.concatenate([bias_whole] + grads, axis=-1))
    v.close(at)
    gate_wgrad, up_wgrad, input_grad = v.done
    result, down_grad = v.result, v.down_grad
    shares = jnp.sum(at.swap(v.small, at.groups), axis=0)
    qkv_wgrad, out_wgrad = grad_spread(
        at, [v.back], (3, 1), ((0, 0, 4 * part),), (24 * part, 8 * part)
    )

    def share(i):
        return shares[bias_rows + i * rows : bias_rows + (i + 1) * rows]

    return (
        result,
        input_grad,
        share(0),
        share(1),
        qkv_wgrad,
        shares[:bias_rows],
        out_wgrad,
        share(2),
        share(3),
        gate_wgrad,
        up_wgrad,
        down_grad,
    )


def solution(mesh):
    both = ("fsdp", "seq")
    wide = P(both, None)
    flat = P(both)
    return jax.shard_map(
        body,
        mesh=mesh,
        in_specs=(
            wide, P("fsdp", None), P("fsdp"), flat, flat, wide, flat,
            wide, flat, flat, wide, wide, wide, wide,
        ),
        out_specs=(wide, wide, flat, flat, wide, flat, wide, flat, flat, wide, wide, wide),
        check_vma=False,
    )
```

```python
import functools
import math

import jax
import jax.numpy as jnp
from jax import lax
from jax.experimental import pallas as pl
from jax.experimental.pallas import tpu as pltpu
from jax.sharding import PartitionSpec as P

HEADS = 32
HEAD_DIM = 64
AXES = ("fsdp", "seq")
F32 = jnp.float32
BF16 = jnp.bfloat16


def centered_of(values):
    centered = values - jnp.mean(values, axis=-1, keepdims=True)
    spread = jnp.mean(centered * centered, axis=-1, keepdims=True)
    return centered, lax.rsqrt(spread + 1e-05)


def norm_back(values, gain, grad):
    centered, scale = centered_of(values)
    hat = centered * scale
    lifted = grad * gain
    inner = jnp.mean(lifted * hat, axis=-1, keepdims=True)
    pulled = scale * (lifted - jnp.mean(lifted, axis=-1, keepdims=True) - hat * inner)
    return (
        pulled,
        jnp.sum(grad * hat, axis=0, keepdims=True),
        jnp.sum(grad, axis=0, keepdims=True),
    )


def rotary_tables(spots):
    inverse = 10000.0 ** (-jnp.arange(8).astype(F32) / 8.0)
    angle = inverse[:, None] * spots.astype(F32)[None]
    waves = jnp.concatenate([jnp.cos(angle), jnp.sin(angle)], axis=0)
    lane = jnp.arange(2 * HEAD_DIM) % HEAD_DIM
    row = jnp.arange(16)[:, None]
    turn = row - 8
    picks = [
        (row < 8) & (lane < 16) & (lane % 8 == row),
        (lane < 8) & (lane == turn),
        (lane >= 8) & (lane < 16) & (lane - 8 == turn),
    ]
    signs = (1.0, -1.0, 1.0)
    chosen = jnp.concatenate([p.astype(F32) * g for p, g in zip(picks, signs)], axis=1)
    rest = jnp.concatenate([(lane >= 16).astype(F32), jnp.zeros(4 * HEAD_DIM, F32)])
    table = lax.dot_general(
        waves, chosen, (((0,), (0,)), ((), ())), precision=lax.Precision.HIGHEST
    )
    return table + rest


def turned(values, table, sign):
    wide = values.shape[1]
    many = wide // (2 * HEAD_DIM)
    keep, later, earlier = (
        jnp.concatenate([table[:, i * 128 : (i + 1) * 128]] * many, axis=1) for i in range(3)
    )
    partner = pltpu.roll(values, wide - 8, 1) * later + pltpu.roll(values, 8, 1) * earlier
    return values * keep + sign * partner


def dot_rows(left, right, kind=F32):
    return lax.dot_general(
        left, right, (((0,), (0,)), ((), ())), preferred_element_type=F32
    ).astype(kind)


def dot_cols(left, right, kind=F32):
    return lax.dot_general(
        left, right, (((1,), (1,)), ((), ())), preferred_element_type=F32
    ).astype(kind)


def dot(left, right):
    return jnp.dot(left, right, preferred_element_type=F32)


class Places:
    def __init__(self):
        self.fsdp = lax.axis_size("fsdp")
        self.seq = lax.axis_size("seq")
        self.count = self.fsdp * self.seq
        self.outer = self.fsdp // 4
        spot = lax.axis_index("fsdp")
        side = lax.axis_index("seq")
        self.a = spot // 4
        self.b = (spot // 2) % 2
        self.e = spot % 2
        self.x = side // 2
        self.c = side % 2
        self.last = None
        high, low = 2 * self.seq, self.seq
        self.groups = [
            [(a * 4 + e) * low + b * high + i for b in range(2) for i in range(low)]
            for a in range(self.outer)
            for e in range(2)
        ]
        self.sides = [group[c::2] for group in self.groups for c in range(2)]

    def after(self, values):
        if self.last is None:
            return values
        values, self.last = lax.optimization_barrier((values, self.last))
        return values

    def move(self, values, pairs):
        return lax.ppermute(values, AXES, pairs)

    def flip(self, values, c=0, x=0, e=0, b=0):
        mask = c + 2 * x + self.seq * (e + 2 * b)
        return self.move(values, [(i, i ^ mask) for i in range(self.count)])

    def shift(self, values, steps):
        stride = 4 * self.seq * steps
        return self.move(values, [((i + stride) % self.count, i) for i in range(self.count)])

    def push(self, values, steps):
        stride = 4 * self.seq * steps
        return self.move(values, [(i, (i + stride) % self.count) for i in range(self.count)])

    def push_beside(self, values, steps):
        stride = 4 * self.seq * steps
        pairs = [(i, (i + stride) % self.count ^ self.seq) for i in range(self.count)]
        return self.move(values, pairs)

    def swap(self, values, groups):
        parts = len(groups[0])
        view = values.reshape(parts, values.shape[0] // parts, values.shape[1])
        view = lax.all_to_all(view, AXES, 0, 0, axis_index_groups=groups, tiled=True)
        return view.reshape(values.shape)


class Window:
    def close(self, at):
        values, tree = jax.tree.flatten(self.__dict__)
        self.__dict__.update(jax.tree.unflatten(tree, lax.optimization_barrier(values)))
        at.last = None


def pick(bit, first, second):
    return jnp.where(bit == 0, first, second)


def joined(bit, own, other, axis):
    return pick(
        bit, jnp.concatenate([own, other], axis=axis), jnp.concatenate([other, own], axis=axis)
    )


def order_kernel(width, spots_ref, ref, *outs):
    for i in range(ref.shape[1] // width):
        start = pl.multiple_of(spots_ref[i] * width, 128)
        block = ref[:, pl.ds(start, width)]
        for out in outs:
            for k in range(out.shape[0] // ref.shape[0]):
                rows = slice(k * ref.shape[0], (k + 1) * ref.shape[0])
                out[rows, i * width : (i + 1) * width] = block


def reorder(at, spots, values, copies):
    width = values.shape[1] // len(spots)
    if width % 128:
        cols = [lax.dynamic_slice_in_dim(values, spot * width, width, 1) for spot in spots]
        ordered = jnp.concatenate(cols, axis=1)
        return [jnp.concatenate([ordered] * n, axis=0) for n in copies]
    order = jnp.stack(spots).astype(jnp.int32)
    rows, wide = values.shape
    outs = [((n * rows, wide), values.dtype) for n in copies]
    return call(at, functools.partial(order_kernel, width), outs, order, values, name="order")


def to_relative(at, values, copies):
    spots = [
        (((at.a + i) % at.outer) * 2 + k) * 2 + (at.e ^ j)
        for i in range(at.outer)
        for j in range(2)
        for k in range(2)
    ]
    return reorder(at, spots, values, copies)


def to_absolute(at, values):
    spots = [
        (((i - at.a) % at.outer) * 2 + (at.e ^ j)) * 2 + k
        for i in range(at.outer)
        for k in range(2)
        for j in range(2)
    ]
    return reorder(at, spots, values, [1])


def rows_of(shape, rows, index=lambda i: i):
    return pl.BlockSpec((rows, shape[1]), lambda i: (index(i), 0))


def need(args, outs, scratch, tiles, out_tiles):
    total = 6 * 2**20
    for shapes, given in (
        ([(v.shape, v.dtype) for v in args], tiles),
        (list(outs), out_tiles),
        ([(v.shape, v.dtype) for v in scratch], None),
    ):
        for k, (shape, kind) in enumerate(shapes):
            block = given[k].block_shape if given and k in given else shape
            total += math.prod(block) * jnp.dtype(kind).itemsize * (1 + (block is not shape)) * 9 // 8
    return total


def call(at, kernel, outs, *args, steps=1, tiles=None, out_tiles=None, scratch=(), name=None):
    def spec(shape, kind, k, given):
        if given and k in given:
            return given[k]
        if kind == jnp.int32:
            return pl.BlockSpec(memory_space=pltpu.SMEM)
        zeros = (0,) * len(shape)
        return pl.BlockSpec(shape, lambda i: zeros, pipeline_mode=pl.Buffered(1))

    least = min(range(len(args)), key=lambda i: args[i].size)
    in_specs = [spec(v.shape, v.dtype, k, tiles) for k, v in enumerate(args)]
    args = list(args)
    args[least] = at.after(args[least])
    results = pl.pallas_call(
        kernel,
        grid=(steps,),
        out_shape=[jax.ShapeDtypeStruct(shape, kind) for shape, kind in outs],
        in_specs=in_specs,
        out_specs=[spec(shape, kind, k, out_tiles) for k, (shape, kind) in enumerate(outs)],
        scratch_shapes=list(scratch),
        compiler_params=pltpu.CompilerParams(
            vmem_limit_bytes=max(need(args, outs, scratch, tiles, out_tiles), 20 * 2**20)
        ),
        cost_estimate=pl.CostEstimate(flops=0, bytes_accessed=0, transcendentals=0),
        name=name,
    )(*args)
    at.last = min(results, key=lambda v: v.size)
    return results


TILE = 256


def product(values, chunks):
    outs = []
    for blocks in chunks:
        depth = blocks[0].shape[0]
        total = dot(values[:, :depth], blocks[0][...])
        for i, block in enumerate(blocks[1:], 1):
            total = total + dot(values[:, i * depth : (i + 1) * depth], block[...])
        outs.append(total)
    return outs[0] if len(outs) == 1 else jnp.concatenate(outs, axis=1)


def in_chunks(refs, count):
    return [refs[i : i + count] for i in range(0, len(refs), count)]


def transposed_product(values, chunks, j):
    total, col = None, 0
    for blocks in chunks:
        width = blocks[j].shape[1]
        term = dot_cols(values[:, col : col + width], blocks[j][...])
        total = term if total is None else total + term
        col += width
    return total


def tile_of(i):
    return pl.ds(pl.multiple_of(i * TILE, TILE), TILE)


def gathered(pieces, out):
    rows = pieces[0].shape[0]
    for i in range(4):

        @pl.when(pl.program_id(0) == i)
        def _():
            out[:rows, :] = pieces[2 * i][...]
            out[rows:, :] = pieces[2 * i + 1][...]


def attended_grad_kernel(count, *refs):
    pieces, blocks = refs[:8], refs[8:-2]
    whole, grads = refs[-2:]
    gathered(pieces, whole)
    grads[...] = product(whole, in_chunks(blocks, count)).astype(BF16)


def head_of(ref, group, head, start):
    part = ref.shape[1] // 3
    low = group * part + head * HEAD_DIM
    return ref[pl.ds(pl.multiple_of(start, TILE), TILE), low : low + HEAD_DIM]


def both_halves(ref, group, head, start, half):
    return jnp.concatenate(
        [head_of(ref, group, head, start), head_of(ref, group, head, start + half)], axis=0
    )


def allowed_at(row, col, sequence, turn):
    spot = pl.ds(pl.multiple_of(turn * TILE, TILE), TILE)
    ours = jnp.where(sequence == 0, row[0:1, spot], row[1:2, spot])
    theirs = jnp.where(sequence == 0, col[:, 0:1], col[:, 1:2])
    return (theirs == ours) & (col[:, 2:3] <= row[2:3, spot])


def scores_of(key, query, allowed):
    return jnp.where(allowed, dot_cols(key, query), -1e30)


def attention_kernel(count, *refs):
    pieces, blocks = refs[:8], refs[8:-12]
    gain, shift, bias, table, row, col, normed, mixed, attended, sums, tile, low = refs[-12:]
    tiles = pl.num_programs(0) // 2
    half = mixed.shape[0] // 2
    heads = attended.shape[1] // HEAD_DIM
    gathered(pieces, tile)

    @pl.when(pl.program_id(0) < tiles)
    def _():
        centered, scale = centered_of(tile[...].astype(F32))
        low[...] = (centered * scale * gain[...] + shift[...]).astype(BF16)
        normed[...] = low[...]
        turning = mixed.shape[1] * 2 // 3
        values = product(low, in_chunks(blocks, count)) + bias[...]
        both = turned(values[:, :turning], table[...], 1.0).astype(BF16)
        span = tile_of(pl.program_id(0))
        mixed[span, : turning // 2] = both[:, : turning // 2] * 0.125
        mixed[span, turning // 2 : turning] = both[:, turning // 2 :]
        mixed[span, turning:] = values[:, turning:].astype(BF16)

    @pl.when(pl.program_id(0) >= tiles)
    def _():
        i = pl.program_id(0) - tiles
        sequence, turn = i // 2, i % 2
        allowed = allowed_at(row, col, sequence, turn)
        start = turn * half + sequence * TILE
        span = pl.ds(pl.multiple_of(start, TILE), TILE)
        for h in range(heads):
            key = both_halves(mixed, 1, h, sequence * TILE, half)
            value = both_halves(mixed, 2, h, sequence * TILE, half)
            scores = scores_of(key, head_of(mixed, 0, h, start), allowed)
            top = jnp.max(scores, axis=0, keepdims=True)
            expo = jnp.exp(scores - top)
            total = jnp.sum(expo, axis=0, keepdims=True)
            out = jnp.transpose(dot_rows(value, (expo * (1.0 / total)).astype(BF16)))
            attended[span, h * HEAD_DIM : (h + 1) * HEAD_DIM] = out.astype(BF16)
            sums[pl.ds(i * heads + h, 1), :] = top + jnp.log(total)


def attend_back_kernel(
    grads, mixed, sums, table, row, col, low, bias, query_sum, key_sum, value_sum
):
    half = mixed.shape[0] // 2
    part = grads.shape[1]
    heads = part // HEAD_DIM

    for sequence in range(2):
        for turn in range(2):
            i = sequence * 2 + turn
            allowed = allowed_at(row, col, sequence, turn)
            start = turn * half + sequence * TILE
            span = pl.ds(start, TILE)
            for h in range(heads):
                cols = slice(h * HEAD_DIM, (h + 1) * HEAD_DIM)
                query = head_of(mixed, 0, h, start)
                key = both_halves(mixed, 1, h, sequence * TILE, half)
                value = both_halves(mixed, 2, h, sequence * TILE, half)
                grad = grads[span, cols]
                scores = scores_of(key, query, allowed)
                probs = jnp.exp(scores - sums[i * heads + h : i * heads + h + 1, :])
                probs_grad = dot_cols(value, grad)
                value_grad = dot(probs.astype(BF16), grad)
                center = jnp.sum(probs * probs_grad, axis=0, keepdims=True)
                scores_low = (probs * (probs_grad - center)).astype(BF16)
                key_grad = dot(scores_low, query)
                query_sum[span, cols] = jnp.transpose(dot_rows(key, scores_low))
                for k in range(2):
                    keys = pl.ds(k * half + sequence * TILE, TILE)
                    rows = slice(k * TILE, (k + 1) * TILE)
                    if turn == 0:
                        key_sum[keys, cols] = key_grad[rows]
                        value_sum[keys, cols] = value_grad[rows]
                    else:
                        key_sum[keys, cols] += key_grad[rows]
                        value_sum[keys, cols] += value_grad[rows]

    bias[...] = jnp.zeros_like(bias)

    @pl.loop(0, mixed.shape[0] // TILE)
    def _(i):
        span = tile_of(i)
        factors = table[span, :]
        for k, ref in enumerate((query_sum, key_sum, value_sum)):
            values = ref[span, :]
            if k == 0:
                values = values * 0.125
            if k < 2:
                values = turned(values, factors, -1.0)
            values = values.astype(BF16)
            low[span, k * part : (k + 1) * part] = values
            bias[:, k * part : (k + 1) * part] += jnp.sum(
                values.astype(F32), axis=0, keepdims=True
            )


def expand_kernel(count, values, *refs):
    *blocks, out = refs
    chunks = in_chunks(blocks, count)
    width = blocks[0].shape[0]
    for j in range(count):
        total = transposed_product(values, chunks, j)
        out[:, j * width : (j + 1) * width] = total.astype(out.dtype)


def total_of(terms):
    total = terms[0][...].astype(F32)
    for term in terms[1:]:
        total = total + term[...].astype(F32)
    return total


def hidden_kernel(inputs, gain, shift, *refs):
    *terms, hidden, normed = refs
    values = inputs[...].astype(F32) + total_of(terms)
    hidden[...] = values
    centered, scale = centered_of(values)
    normed[...] = (centered * scale * gain[...] + shift[...]).astype(BF16)


def result_kernel(hidden, *refs):
    *terms, out = refs
    out[...] = (hidden[...] + total_of(terms)).astype(BF16)


def branch_kernel(hidden, cotangent, gain, *refs):
    *terms, grad, low, gain_grad, shift_grad = refs
    pulled, gain_grad[...], shift_grad[...] = norm_back(hidden[...], gain[...], total_of(terms))
    values = cotangent[...].astype(F32) + pulled
    grad[...] = values
    low[...] = values.astype(BF16)


def input_kernel(inputs, hidden_grad, gain, *refs):
    *terms, grad, gain_grad, shift_grad = refs
    pulled, gain_grad[...], shift_grad[...] = norm_back(
        inputs[...].astype(F32), gain[...], total_of(terms)
    )
    grad[...] = hidden_grad[...] + pulled


def mlp_kernel(count, *refs):
    pieces, blocks = refs[:8], refs[8:-4]
    normed, inner, gate_factor, up_factor = refs[-4:]
    units = gate_factor.shape[1]
    gathered(pieces, normed)
    values = product(normed, in_chunks(blocks, count))
    gate, up = values[:, :units], values[:, units:]
    sigmoid = 1.0 / (1.0 + jnp.exp(-gate))
    silu = gate * sigmoid
    inner[:, :units] = (silu * up).astype(BF16)
    if inner.shape[1] > units:
        inner[:, units:] = jnp.zeros((inner.shape[0], inner.shape[1] - units), BF16)
    gate_factor[...] = up * sigmoid * (1.0 + gate * (1.0 - sigmoid))
    up_factor[...] = silu


def mlp_back_kernel(count, grads, *refs):
    *blocks, gate_factor, up_factor, pair = refs
    values = product(grads, in_chunks(blocks, count))[:, : gate_factor.shape[1]]
    pair[...] = jnp.concatenate(
        [(values * gate_factor[...]).astype(BF16), (values * up_factor[...]).astype(BF16)],
        axis=1,
    )


def segments(widths, chunks):
    out = []
    at_part = at_chunk = part = chunk = 0
    while part < len(widths):
        size = min(widths[part] - at_part, chunks[chunk] - at_chunk)
        out.append((part, at_part, chunk, at_chunk, size))
        at_part, at_chunk = at_part + size, at_chunk + size
        if at_part == widths[part]:
            part, at_part = part + 1, 0
        if at_chunk == chunks[chunk]:
            chunk, at_chunk = chunk + 1, 0
    return out


def part_list(refs, counts):
    return [
        (ref, p, ref.shape[1] // (8 * count)) for ref, count in zip(refs, counts) for p in range(count)
    ]


def cut_kernel(counts, *refs):
    *weights, out = refs
    rows = weights[0].shape[0]
    col = 0
    for ref, p, width in part_list(weights, counts):
        for j in range(8):
            start = (p * 8 + j) * width
            out[j * rows : (j + 1) * rows, col : col + width] = ref[:, start : start + width]
        col += width
    if col < out.shape[1]:
        out[:, col:] = jnp.zeros((out.shape[0], out.shape[1] - col), BF16)


def spread_kernel(counts, strips, *refs):
    chunks, outs = refs[: -len(counts)], refs[-len(counts) :]
    rows = outs[0].shape[0]
    parts = part_list(outs, counts)
    cuts = segments([width for _, _, width in parts], [width for _, _, width in strips])
    for part, begin, strip, col, size in cuts:
        ref, p, width = parts[part]
        chunk, first, _ = strips[strip]
        for j in range(8):
            start = (p * 8 + j) * width + begin
            piece = chunks[chunk][j * rows : (j + 1) * rows, first + col : first + col + size]
            ref[:, start : start + size] = piece.astype(F32)


def sum_kernel(counts, *refs):
    *terms, out = refs
    col = 0
    for count in counts:
        mine, terms = terms[:count], terms[count:]
        total = mine[0][...].astype(F32)
        for term in mine[1:]:
            total = total + term[...].astype(F32)
        out[:, col : col + total.shape[1]] = total.astype(BF16)
        col += total.shape[1]


def cut_rows(at, weights, counts, wide):
    (out,) = call(
        at,
        functools.partial(cut_kernel, counts),
        [((8 * weights[0].shape[0], wide), BF16)],
        *weights,
        name="cut",
    )
    return out


def split_kernel(col, whole, *outs):
    for out in outs:
        out[...] = whole[:, col : col + out.shape[1]]
        col += out.shape[1]


def split(at, whole, begin, widths):
    outs = [((whole.shape[0], n), BF16) for n in widths]
    return call(at, functools.partial(split_kernel, begin), outs, whole, name="split")


def cross_block(at, block):
    return [block] + [at.shift(block, i) for i in range(1, at.outer)]


def merge_blocks(across, beside):
    return [block for pair in zip(across, beside) for block in pair]


def send_block(at, block):
    return [block] + [at.shift(block, i) for i in range(1, at.outer)]


def grad_kernel(count, ways, *refs):
    many = 2 * len(ways)
    pairs, addends, outs = refs[:many], refs[many : many + count], refs[many + count :]
    each = pl.num_programs(0) // len(outs)
    for k, out in enumerate(outs):

        @pl.when(pl.program_id(0) // each == k)
        def _():
            col = 0
            for i, (begin, size) in enumerate(ways):
                values, grads = pairs[2 * i : 2 * i + 2]
                total = dot_rows(values[...], grads[:, begin : begin + size])
                if k < count:
                    total = total + addends[k][:, col : col + size].astype(F32)
                out[:, col : col + size] = total.astype(out.dtype)
                col += size


def grad_blocks(at, ways, spots, kind, addends=(), stacked=False):
    tokens, wide = ways[0][0].shape
    width = wide // (2 * at.outer)
    tile = min(TILE, width)
    each = width // tile

    def column(i):
        spot = spots[0]
        for k in range(1, len(spots)):
            spot = jnp.where(i // each == k, spots[k], spot)
        return spot * each + i % each

    def row_of(k):
        return lambda i: jnp.clip(i - k * each, 0, each - 1)

    shape = (width, sum(way[3] for way in ways))
    tiles = {2 * i: pl.BlockSpec((tokens, tile), lambda i: (0, column(i))) for i in range(len(ways))}
    for k in range(len(addends)):
        tiles[2 * len(ways) + k] = rows_of(shape, tile, row_of(k))
    kernel = functools.partial(grad_kernel, len(addends), tuple(way[2:] for way in ways))
    if stacked:
        shape = (width * len(spots), shape[1])
        return call(
            at,
            kernel,
            [(shape, kind)],
            *[v for way in ways for v in way[:2]],
            steps=len(spots) * each,
            tiles=tiles,
            out_tiles={0: rows_of(shape, tile)},
            name="grad",
        )[0]
    return call(
        at,
        kernel,
        [(shape, kind)] * len(spots),
        *[v for way in ways for v in way[:2]],
        *addends,
        steps=len(spots) * each,
        tiles=tiles,
        out_tiles={k: rows_of(shape, tile, row_of(k)) for k in range(len(spots))},
        name="grad",
    )


def grad_beside(at, *way, stacked=False):
    order = list(range(1, at.outer)) + [0]
    return grad_blocks(at, way, [2 * i + 1 for i in order], BF16, stacked=stacked)


def grad_own(at, *way):
    return grad_blocks(at, way, [0], F32)[0]


def grad_across(at, sent, *way):
    if at.outer == 1:
        return []
    return grad_blocks(at, way, [2 * i for i in range(1, at.outer)], BF16, sent[: at.outer - 1])


def push_all(at, made):
    return [at.push(v, i) for i, v in enumerate(made, 1)]


def flip_all(at, made):
    return [at.flip(v, e=1) for v in made]


def grad_spread(at, chunks, counts, strips, widths):
    rows = chunks[0].shape[0] // 8
    return call(
        at,
        functools.partial(spread_kernel, counts, strips),
        [((rows, n), F32) for n in widths],
        *chunks,
        name="spread",
    )


def join_kernel(*refs):
    *pieces, out = refs
    rows = pieces[0].shape[0]
    for i, piece in enumerate(pieces):
        out[i * rows : (i + 1) * rows, :] = piece[...]


def joined_rows(at, pieces):
    shape = (8 * pieces[0].shape[0], pieces[0].shape[1])
    (out,) = call(at, join_kernel, [(shape, BF16)], *pieces, name="join")
    return out


def spread_tokens(at, values):
    low = at.flip(values, b=1)
    beside = at.flip(values, x=1)
    return [values, beside, low, at.flip(low, x=1)]


def send_pieces(at, pieces):
    return [pieces[0], at.flip(pieces[1], x=1), pieces[2], at.flip(pieces[3], x=1)]


def pass_pieces(at, pieces):
    return [pieces[0], pieces[1], at.flip(add(at, pieces[2:]), b=1)]


def expand_add_kernel(count, values, *refs):
    blocks, other, outs = refs[:-5], refs[-5], refs[-4:]
    chunks = in_chunks(blocks, count)
    width = blocks[0].shape[0]
    rows = outs[0].shape[0]
    for j in range(count):
        cols = slice(j * width, (j + 1) * width)
        total = transposed_product(values, chunks, j) + other[:, cols].astype(F32)
        total = total.astype(BF16)
        for i in range(2):

            @pl.when(pl.program_id(0) == i)
            def _():
                outs[2 * i][:, cols] = total[:rows]
                outs[2 * i + 1][:, cols] = total[rows:]


def expand_pieces(at, values, chunks, other):
    blocks = [block for chunk in chunks for block in chunk]
    shape = (other.shape[0] // 4, other.shape[1])
    return call(
        at,
        functools.partial(expand_add_kernel, len(chunks[0])),
        [(shape, BF16)] * 4,
        values,
        *blocks,
        other,
        steps=other.shape[0] // TILE,
        tiles={
            0: rows_of(values.shape, TILE),
            1 + len(blocks): rows_of(other.shape, TILE),
        },
        name="expand_add",
    )


def add_pieces_kernel(own, other, *outs):
    rows = outs[0].shape[0]
    for d, out in enumerate(outs):
        span = slice(d * rows, (d + 1) * rows)
        out[...] = (own[span, :] + other[span, :].astype(F32)).astype(BF16)


def add_pieces(at, own, other):
    shape = (own.shape[0] // 4, own.shape[1])
    return call(at, add_pieces_kernel, [(shape, BF16)] * 4, own, other, name="pieces")


def expand(at, values, chunks, side, kind):
    half = values.shape[0] // 2
    blocks = [block for chunk in chunks for block in chunk]
    count = len(chunks[0])
    shape = (half, blocks[0].shape[0] * count)
    steps = half // TILE
    (out,) = call(
        at,
        functools.partial(expand_kernel, count),
        [(shape, kind)],
        values,
        *blocks,
        steps=steps,
        tiles={0: rows_of(values.shape, TILE, lambda i: i + side * steps)},
        out_tiles={0: rows_of(shape, TILE)},
        name="expand",
    )
    return out


def add(at, *sums):
    rows = sums[0][0].shape[0]
    tile = min(TILE, rows)
    terms = [v for each in sums for v in each]
    shape = (rows, sum(each[0].shape[1] for each in sums))
    (total,) = call(
        at,
        functools.partial(sum_kernel, tuple(len(each) for each in sums)),
        [(shape, BF16)],
        *terms,
        steps=rows // tile,
        tiles={k: rows_of(v.shape, tile) for k, v in enumerate(terms)},
        out_tiles={0: rows_of(shape, tile)},
        name="add",
    )
    return total


def send_small(at, values):
    total = values[0, 0] + at.flip(values[0, 1], e=1)
    for i in range(1, at.outer):
        total = total + at.push(values[i, 0], i)
        total = total + at.push_beside(values[i, 1], i)
    return total


def order_tokens(at, values):
    seqs, length = values.shape
    view = values.reshape(seqs, 2, 2, length // 4)
    view = pick(at.x, view, view[:, ::-1])
    view = pick(at.c, view, view[:, :, ::-1])
    return jnp.swapaxes(view, 1, 2).reshape(seqs, length)


def body(
    layer_input,
    segment_ids,
    positions,
    ln1_gain,
    ln1_bias,
    qkv_weight,
    qkv_bias,
    out_weight,
    ln2_gain,
    ln2_bias,
    gate_weight,
    up_weight,
    down_weight,
    cotangent,
):
    at = Places()
    width = layer_input.shape[1]
    rows = qkv_weight.shape[0]
    bias_rows = qkv_bias.shape[0]
    length = segment_ids.shape[1]
    heads_here = HEADS // 8
    part = width // 8
    units = gate_weight.shape[1] // 8
    slot = at.b * 4 + at.x * 2 + at.c

    tokens = 2 * length
    count = 2 * at.outer
    near = layer_input.shape[0]

    second = 2 * units // 256 * 128
    first = 2 * units - second
    v = Window()
    padded = (units + 127) // 128 * 128
    thin, wide = (tokens, units), (tokens, 2 * units)

    (v.cotangent,) = to_relative(at, cotangent, [1])
    v.cotangent_near = [at.flip(v.cotangent, x=1), at.flip(v.cotangent, b=1)]
    v.front = at.swap(cut_rows(at, [qkv_weight, out_weight], (3, 1), 4 * part), at.groups)
    v.small = jnp.concatenate([at.after(qkv_bias), ln1_gain, ln1_bias, ln2_gain, ln2_bias])[None]
    v.small = joined(at.c, v.small, at.flip(v.small, c=1), 0)
    v.small = joined(at.x, v.small, at.flip(v.small, x=1), 0)
    (v.inputs,) = to_relative(at, layer_input, [1])
    v.first, v.later = split(
        at,
        cut_rows(at, [gate_weight, up_weight, down_weight], (1, 1, 1), 2 * units + padded),
        0,
        (first, second + padded),
    )
    spots = jnp.concatenate([segment_ids, positions[None]], axis=0)[None]
    v.spots = jnp.concatenate([spots, at.flip(spots, b=1)], axis=0)
    v.close(at)

    v.qkv, v.out = split(at, v.front, 0, (3 * part, part))
    del v.front
    v.qkv_across = cross_block(at, v.qkv)
    v.qkv_beside = [at.flip(v.qkv, e=1)]
    v.tokens = spread_tokens(at, v.inputs)
    v.turned = [at.flip(v.tokens[1], c=1)]
    v.small = joined(at.b, v.small, at.flip(v.small, b=1), 0)
    v.small = jnp.stack([v.small] + [at.shift(v.small, i) for i in range(1, at.outer)])
    segments_here = order_tokens(at, v.spots[:, 0])
    places = order_tokens(at, v.spots[:, 1])
    index = order_tokens(at, jnp.arange(length)[None])
    v.row = jnp.concatenate([segments_here, index, jnp.zeros((5, length), index.dtype)], axis=0)
    v.row = v.row.astype(F32)
    v.col = jnp.pad(jnp.transpose(v.row), ((0, 0), (0, 120)))
    places = places.reshape(2, 2, length // 2).swapaxes(0, 1).reshape(2 * length)
    v.table = rotary_tables(places)
    v.close(at)

    v.qkv_beside += flip_all(at, v.qkv_across[1:])
    v.turned = [at.flip(v.tokens[0], c=1), *v.turned] + [at.flip(t, c=1) for t in v.tokens[2:]]
    v.out_across = cross_block(at, v.out)
    v.first = at.swap(v.first, at.groups)

    v.small = jnp.stack([v.small, at.flip(v.small, e=1)], axis=1)

    def vector(i):
        start = bias_rows + i * rows
        return v.small[..., start : start + rows].reshape(1, width).astype(F32)

    v.gains = [vector(i) for i in range(4)]
    bias = v.small[..., :bias_rows]
    bias = pick(at.e, bias, bias[:, ::-1])
    bias = jnp.roll(bias, at.a, axis=0)
    bias = bias.reshape(at.outer, 2, 2, 4, bias_rows).swapaxes(1, 2).reshape(3, 8, part)
    bias = lax.dynamic_index_in_dim(bias, slot, 1, keepdims=False)
    v.bias = bias.reshape(1, 3 * part).astype(F32)
    v.close(at)
    v.qkv_blocks = [merge_blocks(v.qkv_across, v.qkv_beside)]
    del v.qkv_across, v.qkv_beside, v.qkv, v.small, v.spots

    v.first_across = cross_block(at, v.first)
    v.first_beside = [at.flip(v.first, e=1)]
    v.out_beside = flip_all(at, v.out_across)
    v.cotangent_near.append(at.flip(v.cotangent_near[1], x=1))
    v.later = at.swap(v.later, at.groups)
    steps = tokens // TILE
    v.normed, v.mixed, v.attended, v.sums = call(
        at,
        functools.partial(attention_kernel, count),
        [
            ((tokens, width), BF16),
            ((tokens, 3 * part), BF16),
            ((tokens, part), BF16),
            ((4 * heads_here, TILE), F32),
        ],
        *v.tokens,
        *v.turned,
        *v.qkv_blocks[0],
        v.gains[0],
        v.gains[1],
        v.bias,
        v.table,
        v.row,
        v.col,
        steps=2 * steps,
        tiles={11 + count: rows_of(v.table.shape, TILE, lambda i: jnp.minimum(i, steps - 1))},
        out_tiles={0: rows_of((tokens, width), TILE, lambda i: jnp.minimum(i, steps - 1))},
        scratch=[pltpu.VMEM((TILE, width), BF16)] * 2,
        name="attention",
    )
    v.out_blocks = [merge_blocks(v.out_across, v.out_beside)]
    v.other = expand(at, v.attended, v.out_blocks, 1, BF16)
    v.close(at)
    del v.out_across, v.out_beside, v.out

    v.other = at.flip(v.other, c=1)
    v.cotangent_far = [at.flip(t, c=1) for t in (v.cotangent, *v.cotangent_near)]
    v.second, v.down = split(at, v.later, 0, (second, padded))
    v.pieces = expand_pieces(at, v.attended, v.out_blocks, v.other)
    v.close(at)
    del v.later

    v.terms = pass_pieces(at, send_pieces(at, v.pieces))
    v.cotangent_all = joined_rows(at, [v.cotangent, *v.cotangent_near, *v.cotangent_far])
    v.second_across = cross_block(at, v.second)
    v.second_beside = [at.flip(v.second, e=1)]
    v.first_beside += flip_all(at, v.first_across[1:])
    v.close(at)
    del v.other, v.pieces, v.cotangent_near, v.cotangent_far

    v.hidden, normed2 = call(
        at,
        hidden_kernel,
        [((near, width), F32), ((near, width), BF16)],
        v.inputs,
        v.gains[2],
        v.gains[3],
        *v.terms,
        name="hidden",
    )
    v.tokens = spread_tokens(at, normed2)
    v.turned = [at.flip(v.tokens[1], c=1)]
    v.down_across = cross_block(at, v.down)
    v.down_beside = [at.flip(v.down, e=1)]
    v.second_beside += flip_all(at, v.second_across[1:])
    v.close(at)
    v.pair_blocks = [
        merge_blocks(v.first_across, v.first_beside),
        merge_blocks(v.second_across, v.second_beside),
    ]
    del v.first_across, v.first_beside, v.second_across, v.second_beside, v.first, v.second

    v.turned = [at.flip(v.tokens[0], c=1), *v.turned] + [at.flip(t, c=1) for t in v.tokens[2:]]
    v.down_beside += flip_all(at, v.down_across[1:])
    v.normed2, v.inner, v.gate_factor, v.up_factor = call(
        at,
        functools.partial(mlp_kernel, count),
        [((tokens, width), BF16), ((tokens, padded), BF16), (thin, F32), (thin, F32)],
        *v.tokens,
        *v.turned,
        *v.pair_blocks[0],
        *v.pair_blocks[1],
        steps=tokens // TILE,
        out_tiles={0: rows_of((tokens, width), TILE)}
        | {1: rows_of((tokens, padded), TILE)}
        | {k: rows_of(thin, TILE) for k in (2, 3)},
        name="mlp",
    )
    v.down_made = grad_beside(at, (v.cotangent_all, v.inner, 0, padded))
    v.close(at)
    v.down_blocks = [merge_blocks(v.down_across, v.down_beside)]
    del v.down_across, v.down_beside, v.down, v.tokens, v.turned

    v.down_sent = flip_all(at, v.down_made[:-1])
    (v.pair_low,) = call(
        at,
        functools.partial(mlp_back_kernel, count),
        [(wide, BF16)],
        v.cotangent_all,
        *v.down_blocks[0],
        v.gate_factor,
        v.up_factor,
        steps=tokens // TILE,
        tiles={
            0: rows_of((tokens, width), TILE),
            1 + count: rows_of(thin, TILE),
            2 + count: rows_of(thin, TILE),
        },
        out_tiles={0: rows_of(wide, TILE)},
        name="mlp_back",
    )
    v.other = expand(at, v.pair_low, v.pair_blocks, 1, BF16)
    v.own = expand(at, v.pair_low, v.pair_blocks, 0, F32)
    v.down_own = grad_own(at, (v.cotangent_all, v.inner, 0, padded))
    v.close(at)

    v.other = at.flip(v.other, c=1)
    v.down_cross = grad_across(at, v.down_sent, (v.cotangent_all, v.inner, 0, padded))
    v.first_made = grad_beside(at, (v.normed2, v.pair_low, first, second))
    v.pieces = add_pieces(at, v.own, v.other)
    v.close(at)

    v.terms = pass_pieces(at, send_pieces(at, v.pieces))
    v.down_far = push_all(at, v.down_cross)
    v.down_sent += flip_all(at, v.down_made[-1:])
    v.first_sent = flip_all(at, v.first_made[:-1])
    v.second_made = grad_beside(at, (v.normed2, v.pair_low, 0, first))
    v.first_own = grad_own(at, (v.normed2, v.pair_low, first, second))
    v.second_own = grad_own(at, (v.normed2, v.pair_low, 0, first))
    v.result_other = expand(at, v.inner, v.down_blocks, 1, BF16)
    v.result_own = expand(at, v.inner, v.down_blocks, 0, F32)
    v.close(at)
    del v.down_cross, v.down_made, v.own, v.other

    v.hidden_grad, branch, v.gain_two_grad, v.shift_two_grad = call(
        at,
        branch_kernel,
        [((near, width), F32), ((near, width), BF16)] + [((1, width), F32)] * 2,
        v.hidden,
        v.cotangent,
        v.gains[2],
        *v.terms,
        name="branch",
    )
    v.tokens = spread_tokens(at, branch)
    v.turned = [at.flip(v.tokens[1], c=1)]
    v.first_far = push_all(at, grad_across(at, v.first_sent, (v.normed2, v.pair_low, first, second)))
    v.first_sent += flip_all(at, v.first_made[-1:])
    v.second_sent = flip_all(at, v.second_made[:-1])
    v.close(at)
    del v.first_made, v.pieces

    v.turned = [at.flip(v.tokens[0], c=1), *v.turned] + [at.flip(t, c=1) for t in v.tokens[2:]]
    v.result_other = at.flip(v.result_other, c=1)
    v.early = add(
        at,
        [v.down_own, v.down_sent[-1], *v.down_far],
        [v.first_own, v.first_sent[-1], *v.first_far],
    )
    v.second_cross = grad_across(at, v.second_sent, (v.normed2, v.pair_low, 0, first))
    v.pieces = add_pieces(at, v.result_own, v.result_other)
    v.close(at)
    del v.first_own, v.first_sent, v.first_far, v.down_own, v.down_sent, v.down_far
    del v.result_own, v.result_other

    v.early = at.swap(v.early, at.groups)
    v.second_far = push_all(at, v.second_cross)
    v.second_sent += flip_all(at, v.second_made[-1:])
    v.result_pieces = send_pieces(at, v.pieces)
    v.branch, v.attended_grad = call(
        at,
        functools.partial(attended_grad_kernel, count),
        [((tokens, width), BF16), ((tokens, part), BF16)],
        *v.tokens,
        *v.turned,
        *v.out_blocks[0],
        steps=tokens // TILE,
        out_tiles={0: rows_of((tokens, width), TILE), 1: rows_of((tokens, part), TILE)},
        name="attended_grad",
    )
    v.out_sent = at.flip(grad_beside(at, (v.branch, v.attended, 0, part), stacked=True), e=1)
    v.mixed_low, v.bias_part = call(
        at,
        attend_back_kernel,
        [((tokens, 3 * part), BF16), ((1, 3 * part), F32)],
        v.attended_grad,
        v.mixed,
        v.sums,
        v.table,
        v.row,
        v.col,
        scratch=[pltpu.VMEM((tokens, part), F32)] * 3,
        name="attend_back",
    )
    v.qkv_made = grad_beside(at, (v.normed, v.mixed_low, 0, 3 * part))
    v.other = expand(at, v.mixed_low, v.qkv_blocks, 1, BF16)
    v.close(at)
    del v.tokens, v.turned, v.second_made, v.second_cross, v.attended_grad

    v.late = at.swap(add(at, [v.second_own, v.second_sent[-1], *v.second_far]), at.groups)
    v.other = at.flip(v.other, c=1)
    v.qkv_sent = flip_all(at, v.qkv_made[:-1])
    v.result_terms = pass_pieces(at, v.result_pieces)
    v.out_sent = jnp.split(v.out_sent, at.outer)
    v.out_far = push_all(at, grad_across(at, v.out_sent, (v.branch, v.attended, 0, part)))
    v.qkv_own = grad_own(at, (v.normed, v.mixed_low, 0, 3 * part))
    v.out_own = grad_own(at, (v.branch, v.attended, 0, part))
    v.pieces = expand_pieces(at, v.mixed_low, v.qkv_blocks, v.other)
    v.qkv_cross = grad_across(at, v.qkv_sent, (v.normed, v.mixed_low, 0, 3 * part))
    v.close(at)
    del v.second_own, v.second_sent, v.second_far

    v.qkv_far = push_all(at, v.qkv_cross)
    v.terms = pass_pieces(at, send_pieces(at, v.pieces))
    v.qkv_sent += flip_all(at, v.qkv_made[-1:])
    (v.result,) = call(
        at, result_kernel, [((near, width), BF16)], v.hidden, *v.result_terms, name="result"
    )
    (v.result,) = to_absolute(at, v.result)
    (v.down_grad,) = grad_spread(at, [v.early], (1,), ((0, 0, units),), (8 * units,))
    v.close(at)
    del v.other, v.qkv_made, v.pieces

    v.back = at.swap(
        add(
            at,
            [v.qkv_own, v.qkv_sent[-1], *v.qkv_far],
            [v.out_own, v.out_sent[-1], *v.out_far],
        ),
        at.groups,
    )
    v.input_grad, gain_one_grad, shift_one_grad = call(
        at,
        input_kernel,
        [((near, width), F32)] + [((1, width), F32)] * 2,
        v.inputs,
        v.hidden_grad,
        v.gains[0],
        *v.terms,
        name="inputs",
    )
    gate_wgrad, up_wgrad = grad_spread(
        at,
        [v.early, v.late],
        (1, 1),
        ((1, 0, first), (0, padded, second)),
        (8 * units,) * 2,
    )
    (input_grad,) = to_absolute(at, v.input_grad)
    v.done = [gate_wgrad, up_wgrad, input_grad]
    bias_part = v.bias_part.reshape(3, 1, part)
    own_slot = (jnp.arange(8) == slot).astype(F32)[None, :, None]
    bias_whole = (bias_part * own_slot).reshape(at.outer, 2, 2, 4, bias_rows).swapaxes(1, 2)
    bias_whole = jnp.roll(bias_whole, -at.a, axis=0)
    bias_whole = pick(at.e, bias_whole, bias_whole[:, ::-1]).reshape(at.outer, 2, 8, bias_rows)
    grads = [
        g.reshape(at.outer, 2, 8, rows)
        for g in (gain_one_grad, shift_one_grad, v.gain_two_grad, v.shift_two_grad)
    ]
    v.small = send_small(at, jnp.concatenate([bias_whole] + grads, axis=-1))
    v.close(at)
    gate_wgrad, up_wgrad, input_grad = v.done
    result, down_grad = v.result, v.down_grad
    shares = jnp.sum(at.swap(v.small, at.groups), axis=0)
    qkv_wgrad, out_wgrad = grad_spread(
        at, [v.back], (3, 1), ((0, 0, 4 * part),), (24 * part, 8 * part)
    )

    def share(i):
        return shares[bias_rows + i * rows : bias_rows + (i + 1) * rows]

    return (
        result,
        input_grad,
        share(0),
        share(1),
        qkv_wgrad,
        shares[:bias_rows],
        out_wgrad,
        share(2),
        share(3),
        gate_wgrad,
        up_wgrad,
        down_grad,
    )


def solution(mesh):
    both = ("fsdp", "seq")
    wide = P(both, None)
    flat = P(both)
    return jax.shard_map(
        body,
        mesh=mesh,
        in_specs=(
            wide, P("fsdp", None), P("fsdp"), flat, flat, wide, flat,
            wide, flat, flat, wide, wide, wide, wide,
        ),
        out_specs=(wide, wide, flat, flat, wide, flat, wide, flat, flat, wide, wide, wide),
        check_vma=False,
    )
```

```python
import functools
import math

import jax
import jax.numpy as jnp
from jax import lax
from jax.experimental import pallas as pl
from jax.experimental.pallas import tpu as pltpu
from jax.sharding import PartitionSpec as P

HEADS = 32
HEAD_DIM = 64
AXES = ("fsdp", "seq")
F32 = jnp.float32
BF16 = jnp.bfloat16


def centered_of(values):
    centered = values - jnp.mean(values, axis=-1, keepdims=True)
    spread = jnp.mean(centered * centered, axis=-1, keepdims=True)
    return centered, lax.rsqrt(spread + 1e-05)


def norm_back(values, gain, grad):
    centered, scale = centered_of(values)
    hat = centered * scale
    lifted = grad * gain
    inner = jnp.mean(lifted * hat, axis=-1, keepdims=True)
    pulled = scale * (lifted - jnp.mean(lifted, axis=-1, keepdims=True) - hat * inner)
    return (
        pulled,
        jnp.sum(grad * hat, axis=0, keepdims=True),
        jnp.sum(grad, axis=0, keepdims=True),
    )


def rotary_tables(spots):
    inverse = 10000.0 ** (-jnp.arange(8).astype(F32) / 8.0)
    angle = inverse[:, None] * spots.astype(F32)[None]
    waves = jnp.concatenate([jnp.cos(angle), jnp.sin(angle)], axis=0)
    lane = jnp.arange(2 * HEAD_DIM) % HEAD_DIM
    row = jnp.arange(16)[:, None]
    turn = row - 8
    picks = [
        (row < 8) & (lane < 16) & (lane % 8 == row),
        (lane < 8) & (lane == turn),
        (lane >= 8) & (lane < 16) & (lane - 8 == turn),
    ]
    signs = (1.0, -1.0, 1.0)
    chosen = jnp.concatenate([p.astype(F32) * g for p, g in zip(picks, signs)], axis=1)
    rest = jnp.concatenate([(lane >= 16).astype(F32), jnp.zeros(4 * HEAD_DIM, F32)])
    table = lax.dot_general(
        waves, chosen, (((0,), (0,)), ((), ())), precision=lax.Precision.HIGHEST
    )
    return table + rest


def turned(values, table, sign):
    wide = values.shape[1]
    many = wide // (2 * HEAD_DIM)
    keep, later, earlier = (
        jnp.concatenate([table[:, i * 128 : (i + 1) * 128]] * many, axis=1) for i in range(3)
    )
    partner = pltpu.roll(values, wide - 8, 1) * later + pltpu.roll(values, 8, 1) * earlier
    return values * keep + sign * partner


def dot_rows(left, right, kind=F32):
    return lax.dot_general(
        left, right, (((0,), (0,)), ((), ())), preferred_element_type=F32
    ).astype(kind)


def dot_cols(left, right, kind=F32):
    return lax.dot_general(
        left, right, (((1,), (1,)), ((), ())), preferred_element_type=F32
    ).astype(kind)


def dot(left, right):
    return jnp.dot(left, right, preferred_element_type=F32)


class Places:
    def __init__(self):
        self.fsdp = lax.axis_size("fsdp")
        self.seq = lax.axis_size("seq")
        self.count = self.fsdp * self.seq
        self.outer = self.fsdp // 4
        spot = lax.axis_index("fsdp")
        side = lax.axis_index("seq")
        self.a = spot // 4
        self.b = (spot // 2) % 2
        self.e = spot % 2
        self.x = side // 2
        self.c = side % 2
        self.last = None
        high, low = 2 * self.seq, self.seq
        self.groups = [
            [(a * 4 + e) * low + b * high + i for b in range(2) for i in range(low)]
            for a in range(self.outer)
            for e in range(2)
        ]
        self.sides = [group[c::2] for group in self.groups for c in range(2)]

    def after(self, values):
        if self.last is None:
            return values
        values, self.last = lax.optimization_barrier((values, self.last))
        return values

    def move(self, values, pairs):
        return lax.ppermute(values, AXES, pairs)

    def flip(self, values, c=0, x=0, e=0, b=0):
        mask = c + 2 * x + self.seq * (e + 2 * b)
        return self.move(values, [(i, i ^ mask) for i in range(self.count)])

    def shift(self, values, steps):
        stride = 4 * self.seq * steps
        return self.move(values, [((i + stride) % self.count, i) for i in range(self.count)])

    def push(self, values, steps):
        stride = 4 * self.seq * steps
        return self.move(values, [(i, (i + stride) % self.count) for i in range(self.count)])

    def push_beside(self, values, steps):
        stride = 4 * self.seq * steps
        pairs = [(i, (i + stride) % self.count ^ self.seq) for i in range(self.count)]
        return self.move(values, pairs)

    def swap(self, values, groups):
        parts = len(groups[0])
        view = values.reshape(parts, values.shape[0] // parts, values.shape[1])
        view = lax.all_to_all(view, AXES, 0, 0, axis_index_groups=groups, tiled=True)
        return view.reshape(values.shape)


class Window:
    def close(self, at):
        values, tree = jax.tree.flatten(self.__dict__)
        self.__dict__.update(jax.tree.unflatten(tree, lax.optimization_barrier(values)))
        at.last = None


def pick(bit, first, second):
    return jnp.where(bit == 0, first, second)


def joined(bit, own, other, axis):
    return pick(
        bit, jnp.concatenate([own, other], axis=axis), jnp.concatenate([other, own], axis=axis)
    )


def order_kernel(width, spots_ref, ref, *outs):
    for i in range(ref.shape[1] // width):
        start = pl.multiple_of(spots_ref[i] * width, 128)
        block = ref[:, pl.ds(start, width)]
        for out in outs:
            for k in range(out.shape[0] // ref.shape[0]):
                rows = slice(k * ref.shape[0], (k + 1) * ref.shape[0])
                out[rows, i * width : (i + 1) * width] = block


def reorder(at, spots, values, copies):
    width = values.shape[1] // len(spots)
    if width % 128:
        cols = [lax.dynamic_slice_in_dim(values, spot * width, width, 1) for spot in spots]
        ordered = jnp.concatenate(cols, axis=1)
        return [jnp.concatenate([ordered] * n, axis=0) for n in copies]
    order = jnp.stack(spots).astype(jnp.int32)
    rows, wide = values.shape
    outs = [((n * rows, wide), values.dtype) for n in copies]
    return call(at, functools.partial(order_kernel, width), outs, order, values, name="order")


def to_relative(at, values, copies):
    spots = [
        (((at.a + i) % at.outer) * 2 + k) * 2 + (at.e ^ j)
        for i in range(at.outer)
        for j in range(2)
        for k in range(2)
    ]
    return reorder(at, spots, values, copies)


def to_absolute(at, values):
    spots = [
        (((i - at.a) % at.outer) * 2 + (at.e ^ j)) * 2 + k
        for i in range(at.outer)
        for k in range(2)
        for j in range(2)
    ]
    return reorder(at, spots, values, [1])


def rows_of(shape, rows, index=lambda i: i):
    return pl.BlockSpec((rows, shape[1]), lambda i: (index(i), 0))


def need(args, outs, scratch, tiles, out_tiles):
    total = 6 * 2**20
    for shapes, given in (
        ([(v.shape, v.dtype) for v in args], tiles),
        (list(outs), out_tiles),
        ([(v.shape, v.dtype) for v in scratch], None),
    ):
        for k, (shape, kind) in enumerate(shapes):
            block = given[k].block_shape if given and k in given else shape
            total += math.prod(block) * jnp.dtype(kind).itemsize * (1 + (block is not shape)) * 9 // 8
    return total


def call(at, kernel, outs, *args, steps=1, tiles=None, out_tiles=None, scratch=(), name=None):
    def spec(shape, kind, k, given):
        if given and k in given:
            return given[k]
        if kind == jnp.int32:
            return pl.BlockSpec(memory_space=pltpu.SMEM)
        zeros = (0,) * len(shape)
        return pl.BlockSpec(shape, lambda i: zeros, pipeline_mode=pl.Buffered(1))

    least = min(range(len(args)), key=lambda i: args[i].size)
    in_specs = [spec(v.shape, v.dtype, k, tiles) for k, v in enumerate(args)]
    args = list(args)
    args[least] = at.after(args[least])
    results = pl.pallas_call(
        kernel,
        grid=(steps,),
        out_shape=[jax.ShapeDtypeStruct(shape, kind) for shape, kind in outs],
        in_specs=in_specs,
        out_specs=[spec(shape, kind, k, out_tiles) for k, (shape, kind) in enumerate(outs)],
        scratch_shapes=list(scratch),
        compiler_params=pltpu.CompilerParams(
            vmem_limit_bytes=max(need(args, outs, scratch, tiles, out_tiles), 20 * 2**20)
        ),
        cost_estimate=pl.CostEstimate(flops=0, bytes_accessed=0, transcendentals=0),
        name=name,
    )(*args)
    at.last = min(results, key=lambda v: v.size)
    return results


TILE = 256


def product(values, chunks):
    outs = []
    for blocks in chunks:
        depth = blocks[0].shape[0]
        total = dot(values[:, :depth], blocks[0][...])
        for i, block in enumerate(blocks[1:], 1):
            total = total + dot(values[:, i * depth : (i + 1) * depth], block[...])
        outs.append(total)
    return outs[0] if len(outs) == 1 else jnp.concatenate(outs, axis=1)


def in_chunks(refs, count):
    return [refs[i : i + count] for i in range(0, len(refs), count)]


def transposed_product(values, chunks, j):
    total, col = None, 0
    for blocks in chunks:
        width = blocks[j].shape[1]
        term = dot_cols(values[:, col : col + width], blocks[j][...])
        total = term if total is None else total + term
        col += width
    return total


def tile_of(i):
    return pl.ds(pl.multiple_of(i * TILE, TILE), TILE)


def gathered(pieces, out):
    rows = pieces[0].shape[0]
    for i in range(4):

        @pl.when(pl.program_id(0) == i)
        def _():
            out[:rows, :] = pieces[2 * i][...]
            out[rows:, :] = pieces[2 * i + 1][...]


def attended_grad_kernel(count, *refs):
    pieces, blocks = refs[:8], refs[8:-2]
    whole, grads = refs[-2:]
    gathered(pieces, whole)
    grads[...] = product(whole, in_chunks(blocks, count)).astype(BF16)


def head_of(ref, group, head, start):
    part = ref.shape[1] // 3
    low = group * part + head * HEAD_DIM
    return ref[pl.ds(pl.multiple_of(start, TILE), TILE), low : low + HEAD_DIM]


def both_halves(ref, group, head, start, half):
    return jnp.concatenate(
        [head_of(ref, group, head, start), head_of(ref, group, head, start + half)], axis=0
    )


def allowed_at(row, col, sequence, turn):
    spot = pl.ds(pl.multiple_of(turn * TILE, TILE), TILE)
    ours = jnp.where(sequence == 0, row[0:1, spot], row[1:2, spot])
    theirs = jnp.where(sequence == 0, col[:, 0:1], col[:, 1:2])
    return (theirs == ours) & (col[:, 2:3] <= row[2:3, spot])


def scores_of(key, query, allowed):
    return jnp.where(allowed, dot_cols(key, query), -1e30)


def attention_kernel(count, *refs):
    pieces, blocks = refs[:8], refs[8:-12]
    gain, shift, bias, table, row, col, normed, mixed, attended, sums, tile, low = refs[-12:]
    tiles = pl.num_programs(0) // 2
    half = mixed.shape[0] // 2
    heads = attended.shape[1] // HEAD_DIM
    gathered(pieces, tile)

    @pl.when(pl.program_id(0) < tiles)
    def _():
        centered, scale = centered_of(tile[...].astype(F32))
        low[...] = (centered * scale * gain[...] + shift[...]).astype(BF16)
        normed[...] = low[...]
        turning = mixed.shape[1] * 2 // 3
        values = product(low, in_chunks(blocks, count)) + bias[...]
        both = turned(values[:, :turning], table[...], 1.0).astype(BF16)
        span = tile_of(pl.program_id(0))
        mixed[span, : turning // 2] = both[:, : turning // 2] * 0.125
        mixed[span, turning // 2 : turning] = both[:, turning // 2 :]
        mixed[span, turning:] = values[:, turning:].astype(BF16)

    @pl.when(pl.program_id(0) >= tiles)
    def _():
        i = pl.program_id(0) - tiles
        sequence, turn = i // 2, i % 2
        allowed = allowed_at(row, col, sequence, turn)
        start = turn * half + sequence * TILE
        span = pl.ds(pl.multiple_of(start, TILE), TILE)
        for h in range(heads):
            key = both_halves(mixed, 1, h, sequence * TILE, half)
            value = both_halves(mixed, 2, h, sequence * TILE, half)
            scores = scores_of(key, head_of(mixed, 0, h, start), allowed)
            top = jnp.max(scores, axis=0, keepdims=True)
            expo = jnp.exp(scores - top)
            total = jnp.sum(expo, axis=0, keepdims=True)
            out = jnp.transpose(dot_rows(value, (expo * (1.0 / total)).astype(BF16)))
            attended[span, h * HEAD_DIM : (h + 1) * HEAD_DIM] = out.astype(BF16)
            sums[pl.ds(i * heads + h, 1), :] = top + jnp.log(total)


def attend_back_kernel(
    grads, mixed, sums, table, row, col, low, bias, query_sum, key_sum, value_sum
):
    half = mixed.shape[0] // 2
    part = grads.shape[1]
    heads = part // HEAD_DIM

    for sequence in range(2):
        for turn in range(2):
            i = sequence * 2 + turn
            allowed = allowed_at(row, col, sequence, turn)
            start = turn * half + sequence * TILE
            span = pl.ds(start, TILE)
            for h in range(heads):
                cols = slice(h * HEAD_DIM, (h + 1) * HEAD_DIM)
                query = head_of(mixed, 0, h, start)
                key = both_halves(mixed, 1, h, sequence * TILE, half)
                value = both_halves(mixed, 2, h, sequence * TILE, half)
                grad = grads[span, cols]
                scores = scores_of(key, query, allowed)
                probs = jnp.exp(scores - sums[i * heads + h : i * heads + h + 1, :])
                probs_grad = dot_cols(value, grad)
                value_grad = dot(probs.astype(BF16), grad)
                center = jnp.sum(probs * probs_grad, axis=0, keepdims=True)
                scores_low = (probs * (probs_grad - center)).astype(BF16)
                key_grad = dot(scores_low, query)
                query_sum[span, cols] = jnp.transpose(dot_rows(key, scores_low))
                for k in range(2):
                    keys = pl.ds(k * half + sequence * TILE, TILE)
                    rows = slice(k * TILE, (k + 1) * TILE)
                    if turn == 0:
                        key_sum[keys, cols] = key_grad[rows]
                        value_sum[keys, cols] = value_grad[rows]
                    else:
                        key_sum[keys, cols] += key_grad[rows]
                        value_sum[keys, cols] += value_grad[rows]

    bias[...] = jnp.zeros_like(bias)

    @pl.loop(0, mixed.shape[0] // TILE)
    def _(i):
        span = tile_of(i)
        factors = table[span, :]
        for k, ref in enumerate((query_sum, key_sum, value_sum)):
            values = ref[span, :]
            if k == 0:
                values = values * 0.125
            if k < 2:
                values = turned(values, factors, -1.0)
            values = values.astype(BF16)
            low[span, k * part : (k + 1) * part] = values
            bias[:, k * part : (k + 1) * part] += jnp.sum(
                values.astype(F32), axis=0, keepdims=True
            )


def expand_kernel(count, values, *refs):
    *blocks, out = refs
    chunks = in_chunks(blocks, count)
    width = blocks[0].shape[0]
    for j in range(count):
        total = transposed_product(values, chunks, j)
        out[:, j * width : (j + 1) * width] = total.astype(out.dtype)


def total_of(terms):
    total = terms[0][...].astype(F32)
    for term in terms[1:]:
        total = total + term[...].astype(F32)
    return total


def hidden_kernel(inputs, gain, shift, *refs):
    *terms, hidden, normed = refs
    values = inputs[...].astype(F32) + total_of(terms)
    hidden[...] = values
    centered, scale = centered_of(values)
    normed[...] = (centered * scale * gain[...] + shift[...]).astype(BF16)


def result_kernel(hidden, *refs):
    *terms, out = refs
    out[...] = (hidden[...] + total_of(terms)).astype(BF16)


def branch_kernel(hidden, cotangent, gain, *refs):
    *terms, grad, low, gain_grad, shift_grad = refs
    pulled, gain_grad[...], shift_grad[...] = norm_back(hidden[...], gain[...], total_of(terms))
    values = cotangent[...].astype(F32) + pulled
    grad[...] = values
    low[...] = values.astype(BF16)


def input_kernel(inputs, hidden_grad, gain, *refs):
    *terms, grad, gain_grad, shift_grad = refs
    pulled, gain_grad[...], shift_grad[...] = norm_back(
        inputs[...].astype(F32), gain[...], total_of(terms)
    )
    grad[...] = hidden_grad[...] + pulled


def mlp_kernel(count, *refs):
    pieces, blocks = refs[:8], refs[8:-4]
    normed, inner, gate_factor, up_factor = refs[-4:]
    units = gate_factor.shape[1]
    gathered(pieces, normed)
    values = product(normed, in_chunks(blocks, count))
    gate, up = values[:, :units], values[:, units:]
    sigmoid = 1.0 / (1.0 + jnp.exp(-gate))
    silu = gate * sigmoid
    inner[:, :units] = (silu * up).astype(BF16)
    if inner.shape[1] > units:
        inner[:, units:] = jnp.zeros((inner.shape[0], inner.shape[1] - units), BF16)
    gate_factor[...] = up * sigmoid * (1.0 + gate * (1.0 - sigmoid))
    up_factor[...] = silu


def mlp_back_kernel(count, grads, *refs):
    *blocks, gate_factor, up_factor, pair = refs
    values = product(grads, in_chunks(blocks, count))[:, : gate_factor.shape[1]]
    pair[...] = jnp.concatenate(
        [(values * gate_factor[...]).astype(BF16), (values * up_factor[...]).astype(BF16)],
        axis=1,
    )


def segments(widths, chunks):
    out = []
    at_part = at_chunk = part = chunk = 0
    while part < len(widths):
        size = min(widths[part] - at_part, chunks[chunk] - at_chunk)
        out.append((part, at_part, chunk, at_chunk, size))
        at_part, at_chunk = at_part + size, at_chunk + size
        if at_part == widths[part]:
            part, at_part = part + 1, 0
        if at_chunk == chunks[chunk]:
            chunk, at_chunk = chunk + 1, 0
    return out


def part_list(refs, counts):
    return [
        (ref, p, ref.shape[1] // (8 * count)) for ref, count in zip(refs, counts) for p in range(count)
    ]


def cut_kernel(counts, *refs):
    *weights, out = refs
    rows = weights[0].shape[0]
    col = 0
    for ref, p, width in part_list(weights, counts):
        for j in range(8):
            start = (p * 8 + j) * width
            out[j * rows : (j + 1) * rows, col : col + width] = ref[:, start : start + width]
        col += width
    if col < out.shape[1]:
        out[:, col:] = jnp.zeros((out.shape[0], out.shape[1] - col), BF16)


def spread_kernel(counts, strips, *refs):
    chunks, outs = refs[: -len(counts)], refs[-len(counts) :]
    rows = outs[0].shape[0]
    parts = part_list(outs, counts)
    cuts = segments([width for _, _, width in parts], [width for _, _, width in strips])
    for part, begin, strip, col, size in cuts:
        ref, p, width = parts[part]
        chunk, first, _ = strips[strip]
        for j in range(8):
            start = (p * 8 + j) * width + begin
            piece = chunks[chunk][j * rows : (j + 1) * rows, first + col : first + col + size]
            ref[:, start : start + size] = piece.astype(F32)


def sum_kernel(counts, *refs):
    *terms, out = refs
    col = 0
    for count in counts:
        mine, terms = terms[:count], terms[count:]
        total = mine[0][...].astype(F32)
        for term in mine[1:]:
            total = total + term[...].astype(F32)
        out[:, col : col + total.shape[1]] = total.astype(BF16)
        col += total.shape[1]


def cut_rows(at, weights, counts, wide):
    (out,) = call(
        at,
        functools.partial(cut_kernel, counts),
        [((8 * weights[0].shape[0], wide), BF16)],
        *weights,
        name="cut",
    )
    return out


def split_kernel(col, whole, *outs):
    for out in outs:
        out[...] = whole[:, col : col + out.shape[1]]
        col += out.shape[1]


def split(at, whole, begin, widths):
    outs = [((whole.shape[0], n), BF16) for n in widths]
    return call(at, functools.partial(split_kernel, begin), outs, whole, name="split")


def cross_block(at, block):
    return [block] + [at.shift(block, i) for i in range(1, at.outer)]


def merge_blocks(across, beside):
    return [block for pair in zip(across, beside) for block in pair]


def send_block(at, block):
    return [block] + [at.shift(block, i) for i in range(1, at.outer)]


def grad_kernel(count, ways, *refs):
    many = 2 * len(ways)
    pairs, addends, outs = refs[:many], refs[many : many + count], refs[many + count :]
    each = pl.num_programs(0) // len(outs)
    for k, out in enumerate(outs):

        @pl.when(pl.program_id(0) // each == k)
        def _():
            col = 0
            for i, (begin, size) in enumerate(ways):
                values, grads = pairs[2 * i : 2 * i + 2]
                total = dot_rows(values[...], grads[:, begin : begin + size])
                if k < count:
                    total = total + addends[k][:, col : col + size].astype(F32)
                out[:, col : col + size] = total.astype(out.dtype)
                col += size


def grad_blocks(at, ways, spots, kind, addends=(), stacked=False):
    tokens, wide = ways[0][0].shape
    width = wide // (2 * at.outer)
    tile = min(TILE, width)
    each = width // tile

    def column(i):
        spot = spots[0]
        for k in range(1, len(spots)):
            spot = jnp.where(i // each == k, spots[k], spot)
        return spot * each + i % each

    def row_of(k):
        return lambda i: jnp.clip(i - k * each, 0, each - 1)

    shape = (width, sum(way[3] for way in ways))
    tiles = {2 * i: pl.BlockSpec((tokens, tile), lambda i: (0, column(i))) for i in range(len(ways))}
    for k in range(len(addends)):
        tiles[2 * len(ways) + k] = rows_of(shape, tile, row_of(k))
    kernel = functools.partial(grad_kernel, len(addends), tuple(way[2:] for way in ways))
    if stacked:
        shape = (width * len(spots), shape[1])
        return call(
            at,
            kernel,
            [(shape, kind)],
            *[v for way in ways for v in way[:2]],
            steps=len(spots) * each,
            tiles=tiles,
            out_tiles={0: rows_of(shape, tile)},
            name="grad",
        )[0]
    return call(
        at,
        kernel,
        [(shape, kind)] * len(spots),
        *[v for way in ways for v in way[:2]],
        *addends,
        steps=len(spots) * each,
        tiles=tiles,
        out_tiles={k: rows_of(shape, tile, row_of(k)) for k in range(len(spots))},
        name="grad",
    )


def grad_beside(at, *way, stacked=False):
    order = list(range(1, at.outer)) + [0]
    return grad_blocks(at, way, [2 * i + 1 for i in order], BF16, stacked=stacked)


def grad_own(at, *way):
    return grad_blocks(at, way, [0], F32)[0]


def grad_across(at, sent, *way):
    if at.outer == 1:
        return []
    return grad_blocks(at, way, [2 * i for i in range(1, at.outer)], BF16, sent[: at.outer - 1])


def push_all(at, made):
    return [at.push(v, i) for i, v in enumerate(made, 1)]


def flip_all(at, made):
    return [at.flip(v, e=1) for v in made]


def grad_spread(at, chunks, counts, strips, widths):
    rows = chunks[0].shape[0] // 8
    return call(
        at,
        functools.partial(spread_kernel, counts, strips),
        [((rows, n), F32) for n in widths],
        *chunks,
        name="spread",
    )


def join_kernel(*refs):
    *pieces, out = refs
    rows = pieces[0].shape[0]
    for i, piece in enumerate(pieces):
        out[i * rows : (i + 1) * rows, :] = piece[...]


def joined_rows(at, pieces):
    shape = (8 * pieces[0].shape[0], pieces[0].shape[1])
    (out,) = call(at, join_kernel, [(shape, BF16)], *pieces, name="join")
    return out


def spread_tokens(at, values):
    low = at.flip(values, b=1)
    beside = at.flip(values, x=1)
    return [values, beside, low, at.flip(low, x=1)]


def send_pieces(at, pieces):
    return [pieces[0], at.flip(pieces[1], x=1), pieces[2], at.flip(pieces[3], x=1)]


def pass_pieces(at, pieces):
    return [pieces[0], pieces[1], at.flip(add(at, pieces[2:]), b=1)]


def expand_add_kernel(count, values, *refs):
    blocks, other, outs = refs[:-5], refs[-5], refs[-4:]
    chunks = in_chunks(blocks, count)
    width = blocks[0].shape[0]
    rows = outs[0].shape[0]
    for j in range(count):
        cols = slice(j * width, (j + 1) * width)
        total = transposed_product(values, chunks, j) + other[:, cols].astype(F32)
        total = total.astype(BF16)
        for i in range(2):

            @pl.when(pl.program_id(0) == i)
            def _():
                outs[2 * i][:, cols] = total[:rows]
                outs[2 * i + 1][:, cols] = total[rows:]


def expand_pieces(at, values, chunks, other):
    blocks = [block for chunk in chunks for block in chunk]
    shape = (other.shape[0] // 4, other.shape[1])
    return call(
        at,
        functools.partial(expand_add_kernel, len(chunks[0])),
        [(shape, BF16)] * 4,
        values,
        *blocks,
        other,
        steps=other.shape[0] // TILE,
        tiles={
            0: rows_of(values.shape, TILE),
            1 + len(blocks): rows_of(other.shape, TILE),
        },
        name="expand_add",
    )


def add_pieces_kernel(own, other, *outs):
    rows = outs[0].shape[0]
    for d, out in enumerate(outs):
        span = slice(d * rows, (d + 1) * rows)
        out[...] = (own[span, :] + other[span, :].astype(F32)).astype(BF16)


def add_pieces(at, own, other):
    shape = (own.shape[0] // 4, own.shape[1])
    return call(at, add_pieces_kernel, [(shape, BF16)] * 4, own, other, name="pieces")


def expand(at, values, chunks, side, kind):
    half = values.shape[0] // 2
    blocks = [block for chunk in chunks for block in chunk]
    count = len(chunks[0])
    shape = (half, blocks[0].shape[0] * count)
    steps = half // TILE
    (out,) = call(
        at,
        functools.partial(expand_kernel, count),
        [(shape, kind)],
        values,
        *blocks,
        steps=steps,
        tiles={0: rows_of(values.shape, TILE, lambda i: i + side * steps)},
        out_tiles={0: rows_of(shape, TILE)},
        name="expand",
    )
    return out


def add(at, *sums):
    rows = sums[0][0].shape[0]
    tile = min(TILE, rows)
    terms = [v for each in sums for v in each]
    shape = (rows, sum(each[0].shape[1] for each in sums))
    (total,) = call(
        at,
        functools.partial(sum_kernel, tuple(len(each) for each in sums)),
        [(shape, BF16)],
        *terms,
        steps=rows // tile,
        tiles={k: rows_of(v.shape, tile) for k, v in enumerate(terms)},
        out_tiles={0: rows_of(shape, tile)},
        name="add",
    )
    return total


def send_small(at, values):
    total = values[0, 0] + at.flip(values[0, 1], e=1)
    for i in range(1, at.outer):
        total = total + at.push(values[i, 0], i)
        total = total + at.push_beside(values[i, 1], i)
    return total


def order_tokens(at, values):
    seqs, length = values.shape
    view = values.reshape(seqs, 2, 2, length // 4)
    view = pick(at.x, view, view[:, ::-1])
    view = pick(at.c, view, view[:, :, ::-1])
    return jnp.swapaxes(view, 1, 2).reshape(seqs, length)


def body(
    layer_input,
    segment_ids,
    positions,
    ln1_gain,
    ln1_bias,
    qkv_weight,
    qkv_bias,
    out_weight,
    ln2_gain,
    ln2_bias,
    gate_weight,
    up_weight,
    down_weight,
    cotangent,
):
    at = Places()
    width = layer_input.shape[1]
    rows = qkv_weight.shape[0]
    bias_rows = qkv_bias.shape[0]
    length = segment_ids.shape[1]
    heads_here = HEADS // 8
    part = width // 8
    units = gate_weight.shape[1] // 8
    slot = at.b * 4 + at.x * 2 + at.c

    tokens = 2 * length
    count = 2 * at.outer
    near = layer_input.shape[0]

    second = 2 * units // 256 * 128
    first = 2 * units - second
    v = Window()
    padded = (units + 127) // 128 * 128
    thin, wide = (tokens, units), (tokens, 2 * units)

    (v.cotangent,) = to_relative(at, cotangent, [1])
    v.cotangent_near = [at.flip(v.cotangent, x=1), at.flip(v.cotangent, b=1)]
    v.front = at.swap(cut_rows(at, [qkv_weight, out_weight], (3, 1), 4 * part), at.groups)
    v.small = jnp.concatenate([at.after(qkv_bias), ln1_gain, ln1_bias, ln2_gain, ln2_bias])[None]
    v.small = joined(at.c, v.small, at.flip(v.small, c=1), 0)
    v.small = jnp.stack([v.small, at.flip(v.small, e=1)])
    v.small = jnp.stack([v.small] + [at.shift(v.small, i) for i in range(1, at.outer)])
    (v.inputs,) = to_relative(at, layer_input, [1])
    v.first, v.later = split(
        at,
        cut_rows(at, [gate_weight, up_weight, down_weight], (1, 1, 1), 2 * units + padded),
        0,
        (first, second + padded),
    )
    spots = jnp.concatenate([segment_ids, positions[None]], axis=0)[None]
    v.spots = jnp.concatenate([spots, at.flip(spots, b=1)], axis=0)
    v.close(at)

    v.qkv, v.out = split(at, v.front, 0, (3 * part, part))
    del v.front
    v.qkv_across = cross_block(at, v.qkv)
    v.qkv_beside = [at.flip(v.qkv, e=1)]
    v.tokens = spread_tokens(at, v.inputs)
    v.turned = [at.flip(v.tokens[1], c=1)]
    v.small = joined(at.x, v.small, at.flip(v.small, x=1), 2)
    v.small = joined(at.b, v.small, at.flip(v.small, b=1), 2)
    segments_here = order_tokens(at, v.spots[:, 0])
    places = order_tokens(at, v.spots[:, 1])
    index = order_tokens(at, jnp.arange(length)[None])
    v.row = jnp.concatenate([segments_here, index, jnp.zeros((5, length), index.dtype)], axis=0)
    v.row = v.row.astype(F32)
    v.col = jnp.pad(jnp.transpose(v.row), ((0, 0), (0, 120)))
    places = places.reshape(2, 2, length // 2).swapaxes(0, 1).reshape(2 * length)
    v.table = rotary_tables(places)
    v.close(at)

    v.qkv_beside += flip_all(at, v.qkv_across[1:])
    v.turned = [at.flip(v.tokens[0], c=1), *v.turned] + [at.flip(t, c=1) for t in v.tokens[2:]]
    v.out_across = cross_block(at, v.out)
    v.first = at.swap(v.first, at.groups)


    def vector(i):
        start = bias_rows + i * rows
        return v.small[..., start : start + rows].reshape(1, width).astype(F32)

    v.gains = [vector(i) for i in range(4)]
    bias = v.small[..., :bias_rows]
    bias = pick(at.e, bias, bias[:, ::-1])
    bias = jnp.roll(bias, at.a, axis=0)
    bias = bias.reshape(at.outer, 2, 2, 4, bias_rows).swapaxes(1, 2).reshape(3, 8, part)
    bias = lax.dynamic_index_in_dim(bias, slot, 1, keepdims=False)
    v.bias = bias.reshape(1, 3 * part).astype(F32)
    v.close(at)
    v.qkv_blocks = [merge_blocks(v.qkv_across, v.qkv_beside)]
    del v.qkv_across, v.qkv_beside, v.qkv, v.small, v.spots

    v.first_across = cross_block(at, v.first)
    v.first_beside = [at.flip(v.first, e=1)]
    v.out_beside = flip_all(at, v.out_across)
    v.cotangent_near.append(at.flip(v.cotangent_near[1], x=1))
    v.later = at.swap(v.later, at.groups)
    steps = tokens // TILE
    v.normed, v.mixed, v.attended, v.sums = call(
        at,
        functools.partial(attention_kernel, count),
        [
            ((tokens, width), BF16),
            ((tokens, 3 * part), BF16),
            ((tokens, part), BF16),
            ((4 * heads_here, TILE), F32),
        ],
        *v.tokens,
        *v.turned,
        *v.qkv_blocks[0],
        v.gains[0],
        v.gains[1],
        v.bias,
        v.table,
        v.row,
        v.col,
        steps=2 * steps,
        tiles={11 + count: rows_of(v.table.shape, TILE, lambda i: jnp.minimum(i, steps - 1))},
        out_tiles={0: rows_of((tokens, width), TILE, lambda i: jnp.minimum(i, steps - 1))},
        scratch=[pltpu.VMEM((TILE, width), BF16)] * 2,
        name="attention",
    )
    v.out_blocks = [merge_blocks(v.out_across, v.out_beside)]
    v.other = expand(at, v.attended, v.out_blocks, 1, BF16)
    v.close(at)
    del v.out_across, v.out_beside, v.out

    v.other = at.flip(v.other, c=1)
    v.cotangent_far = [at.flip(t, c=1) for t in (v.cotangent, *v.cotangent_near)]
    v.second, v.down = split(at, v.later, 0, (second, padded))
    v.pieces = expand_pieces(at, v.attended, v.out_blocks, v.other)
    v.close(at)
    del v.later

    v.terms = pass_pieces(at, send_pieces(at, v.pieces))
    v.cotangent_all = joined_rows(at, [v.cotangent, *v.cotangent_near, *v.cotangent_far])
    v.second_across = cross_block(at, v.second)
    v.second_beside = [at.flip(v.second, e=1)]
    v.first_beside += flip_all(at, v.first_across[1:])
    v.close(at)
    del v.other, v.pieces, v.cotangent_near, v.cotangent_far

    v.hidden, normed2 = call(
        at,
        hidden_kernel,
        [((near, width), F32), ((near, width), BF16)],
        v.inputs,
        v.gains[2],
        v.gains[3],
        *v.terms,
        name="hidden",
    )
    v.tokens = spread_tokens(at, normed2)
    v.turned = [at.flip(v.tokens[1], c=1)]
    v.down_across = cross_block(at, v.down)
    v.down_beside = [at.flip(v.down, e=1)]
    v.second_beside += flip_all(at, v.second_across[1:])
    v.close(at)
    v.pair_blocks = [
        merge_blocks(v.first_across, v.first_beside),
        merge_blocks(v.second_across, v.second_beside),
    ]
    del v.first_across, v.first_beside, v.second_across, v.second_beside, v.first, v.second

    v.turned = [at.flip(v.tokens[0], c=1), *v.turned] + [at.flip(t, c=1) for t in v.tokens[2:]]
    v.down_beside += flip_all(at, v.down_across[1:])
    v.normed2, v.inner, v.gate_factor, v.up_factor = call(
        at,
        functools.partial(mlp_kernel, count),
        [((tokens, width), BF16), ((tokens, padded), BF16), (thin, F32), (thin, F32)],
        *v.tokens,
        *v.turned,
        *v.pair_blocks[0],
        *v.pair_blocks[1],
        steps=tokens // TILE,
        out_tiles={0: rows_of((tokens, width), TILE)}
        | {1: rows_of((tokens, padded), TILE)}
        | {k: rows_of(thin, TILE) for k in (2, 3)},
        name="mlp",
    )
    v.down_made = grad_beside(at, (v.cotangent_all, v.inner, 0, padded))
    v.close(at)
    v.down_blocks = [merge_blocks(v.down_across, v.down_beside)]
    del v.down_across, v.down_beside, v.down, v.tokens, v.turned

    v.down_sent = flip_all(at, v.down_made[:-1])
    (v.pair_low,) = call(
        at,
        functools.partial(mlp_back_kernel, count),
        [(wide, BF16)],
        v.cotangent_all,
        *v.down_blocks[0],
        v.gate_factor,
        v.up_factor,
        steps=tokens // TILE,
        tiles={
            0: rows_of((tokens, width), TILE),
            1 + count: rows_of(thin, TILE),
            2 + count: rows_of(thin, TILE),
        },
        out_tiles={0: rows_of(wide, TILE)},
        name="mlp_back",
    )
    v.other = expand(at, v.pair_low, v.pair_blocks, 1, BF16)
    v.own = expand(at, v.pair_low, v.pair_blocks, 0, F32)
    v.down_own = grad_own(at, (v.cotangent_all, v.inner, 0, padded))
    v.close(at)

    v.other = at.flip(v.other, c=1)
    v.down_cross = grad_across(at, v.down_sent, (v.cotangent_all, v.inner, 0, padded))
    v.first_made = grad_beside(at, (v.normed2, v.pair_low, first, second))
    v.pieces = add_pieces(at, v.own, v.other)
    v.close(at)

    v.terms = pass_pieces(at, send_pieces(at, v.pieces))
    v.down_far = push_all(at, v.down_cross)
    v.down_sent += flip_all(at, v.down_made[-1:])
    v.first_sent = flip_all(at, v.first_made[:-1])
    v.second_made = grad_beside(at, (v.normed2, v.pair_low, 0, first))
    v.first_own = grad_own(at, (v.normed2, v.pair_low, first, second))
    v.second_own = grad_own(at, (v.normed2, v.pair_low, 0, first))
    v.result_other = expand(at, v.inner, v.down_blocks, 1, BF16)
    v.result_own = expand(at, v.inner, v.down_blocks, 0, F32)
    v.close(at)
    del v.down_cross, v.down_made, v.own, v.other

    v.hidden_grad, branch, v.gain_two_grad, v.shift_two_grad = call(
        at,
        branch_kernel,
        [((near, width), F32), ((near, width), BF16)] + [((1, width), F32)] * 2,
        v.hidden,
        v.cotangent,
        v.gains[2],
        *v.terms,
        name="branch",
    )
    v.tokens = spread_tokens(at, branch)
    v.turned = [at.flip(v.tokens[1], c=1)]
    v.first_far = push_all(at, grad_across(at, v.first_sent, (v.normed2, v.pair_low, first, second)))
    v.first_sent += flip_all(at, v.first_made[-1:])
    v.second_sent = flip_all(at, v.second_made[:-1])
    v.close(at)
    del v.first_made, v.pieces

    v.turned = [at.flip(v.tokens[0], c=1), *v.turned] + [at.flip(t, c=1) for t in v.tokens[2:]]
    v.result_other = at.flip(v.result_other, c=1)
    v.early = add(
        at,
        [v.down_own, v.down_sent[-1], *v.down_far],
        [v.first_own, v.first_sent[-1], *v.first_far],
    )
    v.second_cross = grad_across(at, v.second_sent, (v.normed2, v.pair_low, 0, first))
    v.pieces = add_pieces(at, v.result_own, v.result_other)
    v.close(at)
    del v.first_own, v.first_sent, v.first_far, v.down_own, v.down_sent, v.down_far
    del v.result_own, v.result_other

    v.early = at.swap(v.early, at.groups)
    v.second_far = push_all(at, v.second_cross)
    v.second_sent += flip_all(at, v.second_made[-1:])
    v.result_pieces = send_pieces(at, v.pieces)
    v.branch, v.attended_grad = call(
        at,
        functools.partial(attended_grad_kernel, count),
        [((tokens, width), BF16), ((tokens, part), BF16)],
        *v.tokens,
        *v.turned,
        *v.out_blocks[0],
        steps=tokens // TILE,
        out_tiles={0: rows_of((tokens, width), TILE), 1: rows_of((tokens, part), TILE)},
        name="attended_grad",
    )
    v.out_sent = at.flip(grad_beside(at, (v.branch, v.attended, 0, part), stacked=True), e=1)
    v.mixed_low, v.bias_part = call(
        at,
        attend_back_kernel,
        [((tokens, 3 * part), BF16), ((1, 3 * part), F32)],
        v.attended_grad,
        v.mixed,
        v.sums,
        v.table,
        v.row,
        v.col,
        scratch=[pltpu.VMEM((tokens, part), F32)] * 3,
        name="attend_back",
    )
    v.qkv_made = grad_beside(at, (v.normed, v.mixed_low, 0, 3 * part))
    v.other = expand(at, v.mixed_low, v.qkv_blocks, 1, BF16)
    v.close(at)
    del v.tokens, v.turned, v.second_made, v.second_cross, v.attended_grad

    v.late = at.swap(add(at, [v.second_own, v.second_sent[-1], *v.second_far]), at.groups)
    v.other = at.flip(v.other, c=1)
    v.qkv_sent = flip_all(at, v.qkv_made[:-1])
    v.result_terms = pass_pieces(at, v.result_pieces)
    v.out_sent = jnp.split(v.out_sent, at.outer)
    v.out_far = push_all(at, grad_across(at, v.out_sent, (v.branch, v.attended, 0, part)))
    v.qkv_own = grad_own(at, (v.normed, v.mixed_low, 0, 3 * part))
    v.out_own = grad_own(at, (v.branch, v.attended, 0, part))
    v.pieces = expand_pieces(at, v.mixed_low, v.qkv_blocks, v.other)
    v.qkv_cross = grad_across(at, v.qkv_sent, (v.normed, v.mixed_low, 0, 3 * part))
    v.close(at)
    del v.second_own, v.second_sent, v.second_far

    v.qkv_far = push_all(at, v.qkv_cross)
    v.terms = pass_pieces(at, send_pieces(at, v.pieces))
    v.qkv_sent += flip_all(at, v.qkv_made[-1:])
    (v.result,) = call(
        at, result_kernel, [((near, width), BF16)], v.hidden, *v.result_terms, name="result"
    )
    (v.result,) = to_absolute(at, v.result)
    v.gate_grad, v.up_grad = grad_spread(
        at,
        [v.early, v.late],
        (1, 1),
        ((1, 0, first), (0, padded, second)),
        (8 * units,) * 2,
    )
    (v.down_grad,) = grad_spread(at, [v.early], (1,), ((0, 0, units),), (8 * units,))
    bias_part = v.bias_part.reshape(3, 1, part)
    own_slot = (jnp.arange(8) == slot).astype(F32)[None, :, None]
    bias_whole = (bias_part * own_slot).reshape(at.outer, 2, 2, 4, bias_rows).swapaxes(1, 2)
    bias_whole = jnp.roll(bias_whole, -at.a, axis=0)
    bias_whole = pick(at.e, bias_whole, bias_whole[:, ::-1])
    v.small_first = bias_whole.reshape(at.outer, 2, 8, bias_rows)
    v.small_last = jnp.concatenate(
        [g.reshape(at.outer, 2, 8, rows) for g in (v.gain_two_grad, v.shift_two_grad)], axis=-1
    )
    v.close(at)
    del v.other, v.qkv_made, v.pieces

    v.back = at.swap(
        add(
            at,
            [v.qkv_own, v.qkv_sent[-1], *v.qkv_far],
            [v.out_own, v.out_sent[-1], *v.out_far],
        ),
        at.groups,
    )
    v.input_grad, gain_one_grad, shift_one_grad = call(
        at,
        input_kernel,
        [((near, width), F32)] + [((1, width), F32)] * 2,
        v.inputs,
        v.hidden_grad,
        v.gains[0],
        *v.terms,
        name="inputs",
    )
    (input_grad,) = to_absolute(at, v.input_grad)
    v.done = [v.gate_grad, v.up_grad, input_grad]
    grads = [g.reshape(at.outer, 2, 8, rows) for g in (gain_one_grad, shift_one_grad)]
    v.small = jnp.concatenate([v.small_first, *grads, v.small_last], axis=-1)
    v.small = send_small(at, v.small)
    v.close(at)
    gate_wgrad, up_wgrad, input_grad = v.done
    result, down_grad = v.result, v.down_grad
    shares = jnp.sum(at.swap(v.small, at.groups), axis=0)
    qkv_wgrad, out_wgrad = grad_spread(
        at, [v.back], (3, 1), ((0, 0, 4 * part),), (24 * part, 8 * part)
    )

    def share(i):
        return shares[bias_rows + i * rows : bias_rows + (i + 1) * rows]

    return (
        result,
        input_grad,
        share(0),
        share(1),
        qkv_wgrad,
        shares[:bias_rows],
        out_wgrad,
        share(2),
        share(3),
        gate_wgrad,
        up_wgrad,
        down_grad,
    )


def solution(mesh):
    both = ("fsdp", "seq")
    wide = P(both, None)
    flat = P(both)
    return jax.shard_map(
        body,
        mesh=mesh,
        in_specs=(
            wide, P("fsdp", None), P("fsdp"), flat, flat, wide, flat,
            wide, flat, flat, wide, wide, wide, wide,
        ),
        out_specs=(wide, wide, flat, flat, wide, flat, wide, flat, flat, wide, wide, wide),
        check_vma=False,
    )
```

```python
import functools
import math

import jax
import jax.numpy as jnp
from jax import lax
from jax.experimental import pallas as pl
from jax.experimental.pallas import tpu as pltpu
from jax.sharding import PartitionSpec as P

HEADS = 32
HEAD_DIM = 64
AXES = ("fsdp", "seq")
F32 = jnp.float32
BF16 = jnp.bfloat16


def centered_of(values):
    centered = values - jnp.mean(values, axis=-1, keepdims=True)
    spread = jnp.mean(centered * centered, axis=-1, keepdims=True)
    return centered, lax.rsqrt(spread + 1e-05)


def norm_back(values, gain, grad):
    centered, scale = centered_of(values)
    hat = centered * scale
    lifted = grad * gain
    inner = jnp.mean(lifted * hat, axis=-1, keepdims=True)
    pulled = scale * (lifted - jnp.mean(lifted, axis=-1, keepdims=True) - hat * inner)
    return (
        pulled,
        jnp.sum(grad * hat, axis=0, keepdims=True),
        jnp.sum(grad, axis=0, keepdims=True),
    )


def rotary_tables(spots):
    inverse = 10000.0 ** (-jnp.arange(8).astype(F32) / 8.0)
    angle = inverse[:, None] * spots.astype(F32)[None]
    waves = jnp.concatenate([jnp.cos(angle), jnp.sin(angle)], axis=0)
    lane = jnp.arange(2 * HEAD_DIM) % HEAD_DIM
    row = jnp.arange(16)[:, None]
    turn = row - 8
    picks = [
        (row < 8) & (lane < 16) & (lane % 8 == row),
        (lane < 8) & (lane == turn),
        (lane >= 8) & (lane < 16) & (lane - 8 == turn),
    ]
    signs = (1.0, -1.0, 1.0)
    chosen = jnp.concatenate([p.astype(F32) * g for p, g in zip(picks, signs)], axis=1)
    rest = jnp.concatenate([(lane >= 16).astype(F32), jnp.zeros(4 * HEAD_DIM, F32)])
    table = lax.dot_general(
        waves, chosen, (((0,), (0,)), ((), ())), precision=lax.Precision.HIGHEST
    )
    return table + rest


def turned(values, table, sign):
    wide = values.shape[1]
    many = wide // (2 * HEAD_DIM)
    keep, later, earlier = (
        jnp.concatenate([table[:, i * 128 : (i + 1) * 128]] * many, axis=1) for i in range(3)
    )
    partner = pltpu.roll(values, wide - 8, 1) * later + pltpu.roll(values, 8, 1) * earlier
    return values * keep + sign * partner


def dot_rows(left, right, kind=F32):
    return lax.dot_general(
        left, right, (((0,), (0,)), ((), ())), preferred_element_type=F32
    ).astype(kind)


def dot_cols(left, right, kind=F32):
    return lax.dot_general(
        left, right, (((1,), (1,)), ((), ())), preferred_element_type=F32
    ).astype(kind)


def dot(left, right):
    return jnp.dot(left, right, preferred_element_type=F32)


class Places:
    def __init__(self):
        self.fsdp = lax.axis_size("fsdp")
        self.seq = lax.axis_size("seq")
        self.count = self.fsdp * self.seq
        self.outer = self.fsdp // 4
        spot = lax.axis_index("fsdp")
        side = lax.axis_index("seq")
        self.a = spot // 4
        self.b = (spot // 2) % 2
        self.e = spot % 2
        self.x = side // 2
        self.c = side % 2
        self.last = None
        high, low = 2 * self.seq, self.seq
        self.groups = [
            [(a * 4 + e) * low + b * high + i for b in range(2) for i in range(low)]
            for a in range(self.outer)
            for e in range(2)
        ]
        self.sides = [group[c::2] for group in self.groups for c in range(2)]

    def after(self, values):
        if self.last is None:
            return values
        values, self.last = lax.optimization_barrier((values, self.last))
        return values

    def move(self, values, pairs):
        return lax.ppermute(values, AXES, pairs)

    def flip(self, values, c=0, x=0, e=0, b=0):
        mask = c + 2 * x + self.seq * (e + 2 * b)
        return self.move(values, [(i, i ^ mask) for i in range(self.count)])

    def shift(self, values, steps):
        stride = 4 * self.seq * steps
        return self.move(values, [((i + stride) % self.count, i) for i in range(self.count)])

    def push(self, values, steps):
        stride = 4 * self.seq * steps
        return self.move(values, [(i, (i + stride) % self.count) for i in range(self.count)])

    def push_beside(self, values, steps):
        stride = 4 * self.seq * steps
        pairs = [(i, (i + stride) % self.count ^ self.seq) for i in range(self.count)]
        return self.move(values, pairs)

    def swap(self, values, groups):
        parts = len(groups[0])
        view = values.reshape(parts, values.shape[0] // parts, values.shape[1])
        view = lax.all_to_all(view, AXES, 0, 0, axis_index_groups=groups, tiled=True)
        return view.reshape(values.shape)


class Window:
    def close(self, at):
        values, tree = jax.tree.flatten(self.__dict__)
        self.__dict__.update(jax.tree.unflatten(tree, lax.optimization_barrier(values)))
        at.last = None


def pick(bit, first, second):
    return jnp.where(bit == 0, first, second)


def joined(bit, own, other, axis):
    return pick(
        bit, jnp.concatenate([own, other], axis=axis), jnp.concatenate([other, own], axis=axis)
    )


def order_kernel(width, spots_ref, ref, *outs):
    for i in range(ref.shape[1] // width):
        start = pl.multiple_of(spots_ref[i] * width, 128)
        block = ref[:, pl.ds(start, width)]
        for out in outs:
            for k in range(out.shape[0] // ref.shape[0]):
                rows = slice(k * ref.shape[0], (k + 1) * ref.shape[0])
                out[rows, i * width : (i + 1) * width] = block


def reorder(at, spots, values, copies):
    width = values.shape[1] // len(spots)
    if width % 128:
        cols = [lax.dynamic_slice_in_dim(values, spot * width, width, 1) for spot in spots]
        ordered = jnp.concatenate(cols, axis=1)
        return [jnp.concatenate([ordered] * n, axis=0) for n in copies]
    order = jnp.stack(spots).astype(jnp.int32)
    rows, wide = values.shape
    outs = [((n * rows, wide), values.dtype) for n in copies]
    return call(at, functools.partial(order_kernel, width), outs, order, values, name="order")


def to_relative(at, values, copies):
    spots = [
        (((at.a + i) % at.outer) * 2 + k) * 2 + (at.e ^ j)
        for i in range(at.outer)
        for j in range(2)
        for k in range(2)
    ]
    return reorder(at, spots, values, copies)


def to_absolute(at, values):
    spots = [
        (((i - at.a) % at.outer) * 2 + (at.e ^ j)) * 2 + k
        for i in range(at.outer)
        for k in range(2)
        for j in range(2)
    ]
    return reorder(at, spots, values, [1])


def rows_of(shape, rows, index=lambda i: i):
    return pl.BlockSpec((rows, shape[1]), lambda i: (index(i), 0))


def need(args, outs, scratch, tiles, out_tiles):
    total = 6 * 2**20
    for shapes, given in (
        ([(v.shape, v.dtype) for v in args], tiles),
        (list(outs), out_tiles),
        ([(v.shape, v.dtype) for v in scratch], None),
    ):
        for k, (shape, kind) in enumerate(shapes):
            block = given[k].block_shape if given and k in given else shape
            total += math.prod(block) * jnp.dtype(kind).itemsize * (1 + (block is not shape)) * 9 // 8
    return total


def call(at, kernel, outs, *args, steps=1, tiles=None, out_tiles=None, scratch=(), name=None):
    def spec(shape, kind, k, given):
        if given and k in given:
            return given[k]
        if kind == jnp.int32:
            return pl.BlockSpec(memory_space=pltpu.SMEM)
        zeros = (0,) * len(shape)
        return pl.BlockSpec(shape, lambda i: zeros, pipeline_mode=pl.Buffered(1))

    least = min(range(len(args)), key=lambda i: args[i].size)
    in_specs = [spec(v.shape, v.dtype, k, tiles) for k, v in enumerate(args)]
    args = list(args)
    args[least] = at.after(args[least])
    results = pl.pallas_call(
        kernel,
        grid=(steps,),
        out_shape=[jax.ShapeDtypeStruct(shape, kind) for shape, kind in outs],
        in_specs=in_specs,
        out_specs=[spec(shape, kind, k, out_tiles) for k, (shape, kind) in enumerate(outs)],
        scratch_shapes=list(scratch),
        compiler_params=pltpu.CompilerParams(
            vmem_limit_bytes=max(need(args, outs, scratch, tiles, out_tiles), 20 * 2**20)
        ),
        cost_estimate=pl.CostEstimate(flops=0, bytes_accessed=0, transcendentals=0),
        name=name,
    )(*args)
    at.last = min(results, key=lambda v: v.size)
    return results


TILE = 256


def product(values, chunks):
    outs = []
    for blocks in chunks:
        depth = blocks[0].shape[0]
        total = dot(values[:, :depth], blocks[0][...])
        for i, block in enumerate(blocks[1:], 1):
            total = total + dot(values[:, i * depth : (i + 1) * depth], block[...])
        outs.append(total)
    return outs[0] if len(outs) == 1 else jnp.concatenate(outs, axis=1)


def in_chunks(refs, count):
    return [refs[i : i + count] for i in range(0, len(refs), count)]


def transposed_product(values, chunks, j):
    total, col = None, 0
    for blocks in chunks:
        width = blocks[j].shape[1]
        term = dot_cols(values[:, col : col + width], blocks[j][...])
        total = term if total is None else total + term
        col += width
    return total


def tile_of(i):
    return pl.ds(pl.multiple_of(i * TILE, TILE), TILE)


def gathered(pieces, out):
    rows = pieces[0].shape[0]
    for i in range(4):

        @pl.when(pl.program_id(0) == i)
        def _():
            out[:rows, :] = pieces[2 * i][...]
            out[rows:, :] = pieces[2 * i + 1][...]


def attended_grad_kernel(count, *refs):
    pieces, blocks = refs[:8], refs[8:-2]
    whole, grads = refs[-2:]
    gathered(pieces, whole)
    grads[...] = product(whole, in_chunks(blocks, count)).astype(BF16)


def head_of(ref, group, head, start):
    part = ref.shape[1] // 3
    low = group * part + head * HEAD_DIM
    return ref[pl.ds(pl.multiple_of(start, TILE), TILE), low : low + HEAD_DIM]


def both_halves(ref, group, head, start, half):
    return jnp.concatenate(
        [head_of(ref, group, head, start), head_of(ref, group, head, start + half)], axis=0
    )


def allowed_at(row, col, sequence, turn):
    spot = pl.ds(pl.multiple_of(turn * TILE, TILE), TILE)
    ours = jnp.where(sequence == 0, row[0:1, spot], row[1:2, spot])
    theirs = jnp.where(sequence == 0, col[:, 0:1], col[:, 1:2])
    return (theirs == ours) & (col[:, 2:3] <= row[2:3, spot])


def scores_of(key, query, allowed):
    return jnp.where(allowed, dot_cols(key, query), -1e30)


def attention_kernel(count, *refs):
    pieces, blocks = refs[:8], refs[8:-12]
    gain, shift, bias, table, row, col, normed, mixed, attended, sums, tile, low = refs[-12:]
    tiles = pl.num_programs(0) // 2
    half = mixed.shape[0] // 2
    heads = attended.shape[1] // HEAD_DIM
    gathered(pieces, tile)

    @pl.when(pl.program_id(0) < tiles)
    def _():
        centered, scale = centered_of(tile[...].astype(F32))
        low[...] = (centered * scale * gain[...] + shift[...]).astype(BF16)
        normed[...] = low[...]
        turning = mixed.shape[1] * 2 // 3
        values = product(low, in_chunks(blocks, count)) + bias[...]
        both = turned(values[:, :turning], table[...], 1.0).astype(BF16)
        span = tile_of(pl.program_id(0))
        mixed[span, : turning // 2] = both[:, : turning // 2] * 0.125
        mixed[span, turning // 2 : turning] = both[:, turning // 2 :]
        mixed[span, turning:] = values[:, turning:].astype(BF16)

    @pl.when(pl.program_id(0) >= tiles)
    def _():
        i = pl.program_id(0) - tiles
        sequence, turn = i // 2, i % 2
        allowed = allowed_at(row, col, sequence, turn)
        start = turn * half + sequence * TILE
        span = pl.ds(pl.multiple_of(start, TILE), TILE)
        for h in range(heads):
            key = both_halves(mixed, 1, h, sequence * TILE, half)
            value = both_halves(mixed, 2, h, sequence * TILE, half)
            scores = scores_of(key, head_of(mixed, 0, h, start), allowed)
            top = jnp.max(scores, axis=0, keepdims=True)
            expo = jnp.exp(scores - top)
            total = jnp.sum(expo, axis=0, keepdims=True)
            out = jnp.transpose(dot_rows(value, (expo * (1.0 / total)).astype(BF16)))
            attended[span, h * HEAD_DIM : (h + 1) * HEAD_DIM] = out.astype(BF16)
            sums[pl.ds(i * heads + h, 1), :] = top + jnp.log(total)


def attend_back_kernel(
    grads, mixed, sums, table, row, col, low, bias, query_sum, key_sum, value_sum
):
    half = mixed.shape[0] // 2
    part = grads.shape[1]
    heads = part // HEAD_DIM

    for sequence in range(2):
        for turn in range(2):
            i = sequence * 2 + turn
            allowed = allowed_at(row, col, sequence, turn)
            start = turn * half + sequence * TILE
            span = pl.ds(start, TILE)
            for h in range(heads):
                cols = slice(h * HEAD_DIM, (h + 1) * HEAD_DIM)
                query = head_of(mixed, 0, h, start)
                key = both_halves(mixed, 1, h, sequence * TILE, half)
                value = both_halves(mixed, 2, h, sequence * TILE, half)
                grad = grads[span, cols]
                scores = scores_of(key, query, allowed)
                probs = jnp.exp(scores - sums[i * heads + h : i * heads + h + 1, :])
                probs_grad = dot_cols(value, grad)
                value_grad = dot(probs.astype(BF16), grad)
                center = jnp.sum(probs * probs_grad, axis=0, keepdims=True)
                scores_low = (probs * (probs_grad - center)).astype(BF16)
                key_grad = dot(scores_low, query)
                query_sum[span, cols] = jnp.transpose(dot_rows(key, scores_low))
                for k in range(2):
                    keys = pl.ds(k * half + sequence * TILE, TILE)
                    rows = slice(k * TILE, (k + 1) * TILE)
                    if turn == 0:
                        key_sum[keys, cols] = key_grad[rows]
                        value_sum[keys, cols] = value_grad[rows]
                    else:
                        key_sum[keys, cols] += key_grad[rows]
                        value_sum[keys, cols] += value_grad[rows]

    bias[...] = jnp.zeros_like(bias)

    @pl.loop(0, mixed.shape[0] // TILE)
    def _(i):
        span = tile_of(i)
        factors = table[span, :]
        for k, ref in enumerate((query_sum, key_sum, value_sum)):
            values = ref[span, :]
            if k == 0:
                values = values * 0.125
            if k < 2:
                values = turned(values, factors, -1.0)
            values = values.astype(BF16)
            low[span, k * part : (k + 1) * part] = values
            bias[:, k * part : (k + 1) * part] += jnp.sum(
                values.astype(F32), axis=0, keepdims=True
            )


def expand_kernel(count, values, *refs):
    *blocks, out = refs
    chunks = in_chunks(blocks, count)
    width = blocks[0].shape[0]
    for j in range(count):
        total = transposed_product(values, chunks, j)
        out[:, j * width : (j + 1) * width] = total.astype(out.dtype)


def total_of(terms):
    total = terms[0][...].astype(F32)
    for term in terms[1:]:
        total = total + term[...].astype(F32)
    return total


def hidden_kernel(inputs, gain, shift, *refs):
    *terms, hidden, normed = refs
    values = inputs[...].astype(F32) + total_of(terms)
    hidden[...] = values
    centered, scale = centered_of(values)
    normed[...] = (centered * scale * gain[...] + shift[...]).astype(BF16)


def result_kernel(hidden, *refs):
    *terms, out = refs
    out[...] = (hidden[...] + total_of(terms)).astype(BF16)


def branch_kernel(hidden, cotangent, gain, *refs):
    *terms, grad, low, gain_grad, shift_grad = refs
    pulled, gain_grad[...], shift_grad[...] = norm_back(hidden[...], gain[...], total_of(terms))
    values = cotangent[...].astype(F32) + pulled
    grad[...] = values
    low[...] = values.astype(BF16)


def input_kernel(inputs, hidden_grad, gain, *refs):
    *terms, grad, gain_grad, shift_grad = refs
    pulled, gain_grad[...], shift_grad[...] = norm_back(
        inputs[...].astype(F32), gain[...], total_of(terms)
    )
    grad[...] = hidden_grad[...] + pulled


def mlp_kernel(count, *refs):
    pieces, blocks = refs[:8], refs[8:-4]
    normed, inner, gate_factor, up_factor = refs[-4:]
    units = gate_factor.shape[1]
    gathered(pieces, normed)
    values = product(normed, in_chunks(blocks, count))
    gate, up = values[:, :units], values[:, units:]
    sigmoid = 1.0 / (1.0 + jnp.exp(-gate))
    silu = gate * sigmoid
    inner[:, :units] = (silu * up).astype(BF16)
    if inner.shape[1] > units:
        inner[:, units:] = jnp.zeros((inner.shape[0], inner.shape[1] - units), BF16)
    gate_factor[...] = up * sigmoid * (1.0 + gate * (1.0 - sigmoid))
    up_factor[...] = silu


def mlp_back_kernel(count, grads, *refs):
    *blocks, gate_factor, up_factor, pair = refs
    values = product(grads, in_chunks(blocks, count))[:, : gate_factor.shape[1]]
    pair[...] = jnp.concatenate(
        [(values * gate_factor[...]).astype(BF16), (values * up_factor[...]).astype(BF16)],
        axis=1,
    )


def segments(widths, chunks):
    out = []
    at_part = at_chunk = part = chunk = 0
    while part < len(widths):
        size = min(widths[part] - at_part, chunks[chunk] - at_chunk)
        out.append((part, at_part, chunk, at_chunk, size))
        at_part, at_chunk = at_part + size, at_chunk + size
        if at_part == widths[part]:
            part, at_part = part + 1, 0
        if at_chunk == chunks[chunk]:
            chunk, at_chunk = chunk + 1, 0
    return out


def part_list(refs, counts):
    return [
        (ref, p, ref.shape[1] // (8 * count)) for ref, count in zip(refs, counts) for p in range(count)
    ]


def cut_kernel(counts, *refs):
    *weights, out = refs
    rows = weights[0].shape[0]
    col = 0
    for ref, p, width in part_list(weights, counts):
        for j in range(8):
            start = (p * 8 + j) * width
            out[j * rows : (j + 1) * rows, col : col + width] = ref[:, start : start + width]
        col += width
    if col < out.shape[1]:
        out[:, col:] = jnp.zeros((out.shape[0], out.shape[1] - col), BF16)


def spread_kernel(counts, strips, *refs):
    chunks, outs = refs[: -len(counts)], refs[-len(counts) :]
    rows = outs[0].shape[0]
    parts = part_list(outs, counts)
    cuts = segments([width for _, _, width in parts], [width for _, _, width in strips])
    for part, begin, strip, col, size in cuts:
        ref, p, width = parts[part]
        chunk, first, _ = strips[strip]
        for j in range(8):
            start = (p * 8 + j) * width + begin
            piece = chunks[chunk][j * rows : (j + 1) * rows, first + col : first + col + size]
            ref[:, start : start + size] = piece.astype(F32)


def sum_kernel(counts, *refs):
    *terms, out = refs
    col = 0
    for count in counts:
        mine, terms = terms[:count], terms[count:]
        total = mine[0][...].astype(F32)
        for term in mine[1:]:
            total = total + term[...].astype(F32)
        out[:, col : col + total.shape[1]] = total.astype(BF16)
        col += total.shape[1]


def cut_rows(at, weights, counts, wide):
    (out,) = call(
        at,
        functools.partial(cut_kernel, counts),
        [((8 * weights[0].shape[0], wide), BF16)],
        *weights,
        name="cut",
    )
    return out


def split_kernel(col, whole, *outs):
    for out in outs:
        out[...] = whole[:, col : col + out.shape[1]]
        col += out.shape[1]


def split(at, whole, begin, widths):
    outs = [((whole.shape[0], n), BF16) for n in widths]
    return call(at, functools.partial(split_kernel, begin), outs, whole, name="split")


def cross_block(at, block):
    return [block] + [at.shift(block, i) for i in range(1, at.outer)]


def merge_blocks(across, beside):
    return [block for pair in zip(across, beside) for block in pair]


def send_block(at, block):
    return [block] + [at.shift(block, i) for i in range(1, at.outer)]


def grad_kernel(count, ways, *refs):
    many = 2 * len(ways)
    pairs, addends, outs = refs[:many], refs[many : many + count], refs[many + count :]
    each = pl.num_programs(0) // len(outs)
    for k, out in enumerate(outs):

        @pl.when(pl.program_id(0) // each == k)
        def _():
            col = 0
            for i, (begin, size) in enumerate(ways):
                values, grads = pairs[2 * i : 2 * i + 2]
                total = dot_rows(values[...], grads[:, begin : begin + size])
                if k < count:
                    total = total + addends[k][:, col : col + size].astype(F32)
                out[:, col : col + size] = total.astype(out.dtype)
                col += size


def grad_blocks(at, ways, spots, kind, addends=(), stacked=False):
    tokens, wide = ways[0][0].shape
    width = wide // (2 * at.outer)
    tile = min(TILE, width)
    each = width // tile

    def column(i):
        spot = spots[0]
        for k in range(1, len(spots)):
            spot = jnp.where(i // each == k, spots[k], spot)
        return spot * each + i % each

    def row_of(k):
        return lambda i: jnp.clip(i - k * each, 0, each - 1)

    shape = (width, sum(way[3] for way in ways))
    tiles = {2 * i: pl.BlockSpec((tokens, tile), lambda i: (0, column(i))) for i in range(len(ways))}
    for k in range(len(addends)):
        tiles[2 * len(ways) + k] = rows_of(shape, tile, row_of(k))
    kernel = functools.partial(grad_kernel, len(addends), tuple(way[2:] for way in ways))
    if stacked:
        shape = (width * len(spots), shape[1])
        return call(
            at,
            kernel,
            [(shape, kind)],
            *[v for way in ways for v in way[:2]],
            steps=len(spots) * each,
            tiles=tiles,
            out_tiles={0: rows_of(shape, tile)},
            name="grad",
        )[0]
    return call(
        at,
        kernel,
        [(shape, kind)] * len(spots),
        *[v for way in ways for v in way[:2]],
        *addends,
        steps=len(spots) * each,
        tiles=tiles,
        out_tiles={k: rows_of(shape, tile, row_of(k)) for k in range(len(spots))},
        name="grad",
    )


def grad_beside(at, *way, stacked=False):
    order = list(range(1, at.outer)) + [0]
    return grad_blocks(at, way, [2 * i + 1 for i in order], BF16, stacked=stacked)


def grad_own(at, *way):
    return grad_blocks(at, way, [0], F32)[0]


def grad_across(at, sent, *way):
    if at.outer == 1:
        return []
    return grad_blocks(at, way, [2 * i for i in range(1, at.outer)], BF16, sent[: at.outer - 1])


def push_all(at, made):
    return [at.push(v, i) for i, v in enumerate(made, 1)]


def flip_all(at, made):
    return [at.flip(v, e=1) for v in made]


def grad_spread(at, chunks, counts, strips, widths):
    rows = chunks[0].shape[0] // 8
    return call(
        at,
        functools.partial(spread_kernel, counts, strips),
        [((rows, n), F32) for n in widths],
        *chunks,
        name="spread",
    )


def join_kernel(*refs):
    *pieces, out = refs
    rows = pieces[0].shape[0]
    for i, piece in enumerate(pieces):
        out[i * rows : (i + 1) * rows, :] = piece[...]


def joined_rows(at, pieces):
    shape = (8 * pieces[0].shape[0], pieces[0].shape[1])
    (out,) = call(at, join_kernel, [(shape, BF16)], *pieces, name="join")
    return out


def spread_tokens(at, values):
    low = at.flip(values, b=1)
    beside = at.flip(values, x=1)
    return [values, beside, low, at.flip(low, x=1)]


def send_pieces(at, pieces):
    return [pieces[0], at.flip(pieces[1], x=1), pieces[2], at.flip(pieces[3], x=1)]


def pass_pieces(at, pieces):
    return [pieces[0], pieces[1], at.flip(add(at, pieces[2:]), b=1)]


def expand_add_kernel(count, values, *refs):
    blocks, other, outs = refs[:-5], refs[-5], refs[-4:]
    chunks = in_chunks(blocks, count)
    width = blocks[0].shape[0]
    rows = outs[0].shape[0]
    for j in range(count):
        cols = slice(j * width, (j + 1) * width)
        total = transposed_product(values, chunks, j) + other[:, cols].astype(F32)
        total = total.astype(BF16)
        for i in range(2):

            @pl.when(pl.program_id(0) == i)
            def _():
                outs[2 * i][:, cols] = total[:rows]
                outs[2 * i + 1][:, cols] = total[rows:]


def expand_pieces(at, values, chunks, other):
    blocks = [block for chunk in chunks for block in chunk]
    shape = (other.shape[0] // 4, other.shape[1])
    return call(
        at,
        functools.partial(expand_add_kernel, len(chunks[0])),
        [(shape, BF16)] * 4,
        values,
        *blocks,
        other,
        steps=other.shape[0] // TILE,
        tiles={
            0: rows_of(values.shape, TILE),
            1 + len(blocks): rows_of(other.shape, TILE),
        },
        name="expand_add",
    )


def add_pieces_kernel(own, other, *outs):
    rows = outs[0].shape[0]
    for d, out in enumerate(outs):
        span = slice(d * rows, (d + 1) * rows)
        out[...] = (own[span, :] + other[span, :].astype(F32)).astype(BF16)


def add_pieces(at, own, other):
    shape = (own.shape[0] // 4, own.shape[1])
    return call(at, add_pieces_kernel, [(shape, BF16)] * 4, own, other, name="pieces")


def expand(at, values, chunks, side, kind):
    half = values.shape[0] // 2
    blocks = [block for chunk in chunks for block in chunk]
    count = len(chunks[0])
    shape = (half, blocks[0].shape[0] * count)
    steps = half // TILE
    (out,) = call(
        at,
        functools.partial(expand_kernel, count),
        [(shape, kind)],
        values,
        *blocks,
        steps=steps,
        tiles={0: rows_of(values.shape, TILE, lambda i: i + side * steps)},
        out_tiles={0: rows_of(shape, TILE)},
        name="expand",
    )
    return out


def add(at, *sums):
    rows = sums[0][0].shape[0]
    tile = min(TILE, rows)
    terms = [v for each in sums for v in each]
    shape = (rows, sum(each[0].shape[1] for each in sums))
    (total,) = call(
        at,
        functools.partial(sum_kernel, tuple(len(each) for each in sums)),
        [(shape, BF16)],
        *terms,
        steps=rows // tile,
        tiles={k: rows_of(v.shape, tile) for k, v in enumerate(terms)},
        out_tiles={0: rows_of(shape, tile)},
        name="add",
    )
    return total


def send_small(at, values):
    total = values[0, 0] + at.flip(values[0, 1], e=1)
    for i in range(1, at.outer):
        total = total + at.push(values[i, 0], i)
        total = total + at.push_beside(values[i, 1], i)
    return total


def order_tokens(at, values):
    seqs, length = values.shape
    view = values.reshape(seqs, 2, 2, length // 4)
    view = pick(at.x, view, view[:, ::-1])
    view = pick(at.c, view, view[:, :, ::-1])
    return jnp.swapaxes(view, 1, 2).reshape(seqs, length)


def body(
    layer_input,
    segment_ids,
    positions,
    ln1_gain,
    ln1_bias,
    qkv_weight,
    qkv_bias,
    out_weight,
    ln2_gain,
    ln2_bias,
    gate_weight,
    up_weight,
    down_weight,
    cotangent,
):
    at = Places()
    width = layer_input.shape[1]
    rows = qkv_weight.shape[0]
    bias_rows = qkv_bias.shape[0]
    length = segment_ids.shape[1]
    heads_here = HEADS // 8
    part = width // 8
    units = gate_weight.shape[1] // 8
    slot = at.b * 4 + at.x * 2 + at.c

    tokens = 2 * length
    count = 2 * at.outer
    near = layer_input.shape[0]

    second = 2 * units // 256 * 128
    first = 2 * units - second
    v = Window()
    padded = (units + 127) // 128 * 128
    thin, wide = (tokens, units), (tokens, 2 * units)

    (v.cotangent,) = to_relative(at, cotangent, [1])
    v.cotangent_near = [at.flip(v.cotangent, x=1), at.flip(v.cotangent, b=1)]
    v.front = at.swap(cut_rows(at, [qkv_weight, out_weight], (3, 1), 4 * part), at.groups)
    v.small = jnp.concatenate([at.after(qkv_bias), ln1_gain, ln1_bias, ln2_gain, ln2_bias])[None]
    v.small = joined(at.c, v.small, at.flip(v.small, c=1), 0)
    v.small = jnp.stack([v.small, at.flip(v.small, e=1)])
    v.small = jnp.stack([v.small] + [at.shift(v.small, i) for i in range(1, at.outer)])
    (v.inputs,) = to_relative(at, layer_input, [1])
    v.first, v.later = split(
        at,
        cut_rows(at, [gate_weight, up_weight, down_weight], (1, 1, 1), 2 * units + padded),
        0,
        (first, second + padded),
    )
    spots = jnp.concatenate([segment_ids, positions[None]], axis=0)[None]
    v.spots = jnp.concatenate([spots, at.flip(spots, b=1)], axis=0)
    v.close(at)

    v.qkv, v.out = split(at, v.front, 0, (3 * part, part))
    del v.front
    v.qkv_across = cross_block(at, v.qkv)
    v.qkv_beside = [at.flip(v.qkv, e=1)]
    v.tokens = spread_tokens(at, v.inputs)
    v.turned = [at.flip(v.tokens[1], c=1)]
    v.small = joined(at.x, v.small, at.flip(v.small, x=1), 2)
    v.small = joined(at.b, v.small, at.flip(v.small, b=1), 2)
    segments_here = order_tokens(at, v.spots[:, 0])
    places = order_tokens(at, v.spots[:, 1])
    index = order_tokens(at, jnp.arange(length)[None])
    v.row = jnp.concatenate([segments_here, index, jnp.zeros((5, length), index.dtype)], axis=0)
    v.row = v.row.astype(F32)
    v.col = jnp.pad(jnp.transpose(v.row), ((0, 0), (0, 120)))
    places = places.reshape(2, 2, length // 2).swapaxes(0, 1).reshape(2 * length)
    v.table = rotary_tables(places)
    v.close(at)

    v.qkv_beside += flip_all(at, v.qkv_across[1:])
    v.turned = [at.flip(v.tokens[0], c=1), *v.turned] + [at.flip(t, c=1) for t in v.tokens[2:]]
    v.out_across = cross_block(at, v.out)
    v.first = at.swap(v.first, at.groups)


    def vector(i):
        start = bias_rows + i * rows
        return v.small[..., start : start + rows].reshape(1, width).astype(F32)

    v.gains = [vector(i) for i in range(4)]
    bias = v.small[..., :bias_rows]
    bias = pick(at.e, bias, bias[:, ::-1])
    bias = jnp.roll(bias, at.a, axis=0)
    bias = bias.reshape(at.outer, 2, 2, 4, bias_rows).swapaxes(1, 2).reshape(3, 8, part)
    bias = lax.dynamic_index_in_dim(bias, slot, 1, keepdims=False)
    v.bias = bias.reshape(1, 3 * part).astype(F32)
    v.close(at)
    v.qkv_blocks = [merge_blocks(v.qkv_across, v.qkv_beside)]
    del v.qkv_across, v.qkv_beside, v.qkv, v.small, v.spots

    v.first_across = cross_block(at, v.first)
    v.first_beside = [at.flip(v.first, e=1)]
    v.out_beside = flip_all(at, v.out_across)
    v.cotangent_near.append(at.flip(v.cotangent_near[1], x=1))
    v.later = at.swap(v.later, at.groups)
    steps = tokens // TILE
    v.normed, v.mixed, v.attended, v.sums = call(
        at,
        functools.partial(attention_kernel, count),
        [
            ((tokens, width), BF16),
            ((tokens, 3 * part), BF16),
            ((tokens, part), BF16),
            ((4 * heads_here, TILE), F32),
        ],
        *v.tokens,
        *v.turned,
        *v.qkv_blocks[0],
        v.gains[0],
        v.gains[1],
        v.bias,
        v.table,
        v.row,
        v.col,
        steps=2 * steps,
        tiles={11 + count: rows_of(v.table.shape, TILE, lambda i: jnp.minimum(i, steps - 1))},
        out_tiles={0: rows_of((tokens, width), TILE, lambda i: jnp.minimum(i, steps - 1))},
        scratch=[pltpu.VMEM((TILE, width), BF16)] * 2,
        name="attention",
    )
    v.out_blocks = [merge_blocks(v.out_across, v.out_beside)]
    v.other = expand(at, v.attended, v.out_blocks, 1, BF16)
    v.close(at)
    del v.out_across, v.out_beside, v.out

    v.other = at.flip(v.other, c=1)
    v.cotangent_far = [at.flip(t, c=1) for t in (v.cotangent, *v.cotangent_near)]
    v.second, v.down = split(at, v.later, 0, (second, padded))
    v.pieces = expand_pieces(at, v.attended, v.out_blocks, v.other)
    v.close(at)
    del v.later

    v.terms = pass_pieces(at, send_pieces(at, v.pieces))
    v.cotangent_all = joined_rows(at, [v.cotangent, *v.cotangent_near, *v.cotangent_far])
    v.second_across = cross_block(at, v.second)
    v.second_beside = [at.flip(v.second, e=1)]
    v.first_beside += flip_all(at, v.first_across[1:])
    v.close(at)
    del v.other, v.pieces, v.cotangent_near, v.cotangent_far

    v.hidden, normed2 = call(
        at,
        hidden_kernel,
        [((near, width), F32), ((near, width), BF16)],
        v.inputs,
        v.gains[2],
        v.gains[3],
        *v.terms,
        name="hidden",
    )
    v.tokens = spread_tokens(at, normed2)
    v.turned = [at.flip(v.tokens[1], c=1)]
    v.down_across = cross_block(at, v.down)
    v.down_beside = [at.flip(v.down, e=1)]
    v.second_beside += flip_all(at, v.second_across[1:])
    v.close(at)
    v.pair_blocks = [
        merge_blocks(v.first_across, v.first_beside),
        merge_blocks(v.second_across, v.second_beside),
    ]
    del v.first_across, v.first_beside, v.second_across, v.second_beside, v.first, v.second

    v.turned = [at.flip(v.tokens[0], c=1), *v.turned] + [at.flip(t, c=1) for t in v.tokens[2:]]
    v.down_beside += flip_all(at, v.down_across[1:])
    v.normed2, v.inner, v.gate_factor, v.up_factor = call(
        at,
        functools.partial(mlp_kernel, count),
        [((tokens, width), BF16), ((tokens, padded), BF16), (thin, F32), (thin, F32)],
        *v.tokens,
        *v.turned,
        *v.pair_blocks[0],
        *v.pair_blocks[1],
        steps=tokens // TILE,
        out_tiles={0: rows_of((tokens, width), TILE)}
        | {1: rows_of((tokens, padded), TILE)}
        | {k: rows_of(thin, TILE) for k in (2, 3)},
        name="mlp",
    )
    v.down_made = grad_beside(at, (v.cotangent_all, v.inner, 0, padded))
    v.close(at)
    v.down_blocks = [merge_blocks(v.down_across, v.down_beside)]
    del v.down_across, v.down_beside, v.down, v.tokens, v.turned

    v.down_sent = flip_all(at, v.down_made[:-1])
    (v.pair_low,) = call(
        at,
        functools.partial(mlp_back_kernel, count),
        [(wide, BF16)],
        v.cotangent_all,
        *v.down_blocks[0],
        v.gate_factor,
        v.up_factor,
        steps=tokens // TILE,
        tiles={
            0: rows_of((tokens, width), TILE),
            1 + count: rows_of(thin, TILE),
            2 + count: rows_of(thin, TILE),
        },
        out_tiles={0: rows_of(wide, TILE)},
        name="mlp_back",
    )
    v.other = expand(at, v.pair_low, v.pair_blocks, 1, BF16)
    v.own = expand(at, v.pair_low, v.pair_blocks, 0, F32)
    v.down_own = grad_own(at, (v.cotangent_all, v.inner, 0, padded))
    v.close(at)

    v.other = at.flip(v.other, c=1)
    v.down_cross = grad_across(at, v.down_sent, (v.cotangent_all, v.inner, 0, padded))
    v.first_made = grad_beside(at, (v.normed2, v.pair_low, first, second))
    v.pieces = add_pieces(at, v.own, v.other)
    v.close(at)

    v.terms = pass_pieces(at, send_pieces(at, v.pieces))
    v.down_far = push_all(at, v.down_cross)
    v.down_sent += flip_all(at, v.down_made[-1:])
    v.first_sent = flip_all(at, v.first_made[:-1])
    v.second_made = grad_beside(at, (v.normed2, v.pair_low, 0, first))
    v.first_own = grad_own(at, (v.normed2, v.pair_low, first, second))
    v.second_own = grad_own(at, (v.normed2, v.pair_low, 0, first))
    v.result_other = expand(at, v.inner, v.down_blocks, 1, BF16)
    v.result_own = expand(at, v.inner, v.down_blocks, 0, F32)
    v.close(at)
    del v.down_cross, v.down_made, v.own, v.other

    v.hidden_grad, branch, v.gain_two_grad, v.shift_two_grad = call(
        at,
        branch_kernel,
        [((near, width), F32), ((near, width), BF16)] + [((1, width), F32)] * 2,
        v.hidden,
        v.cotangent,
        v.gains[2],
        *v.terms,
        name="branch",
    )
    v.tokens = spread_tokens(at, branch)
    v.turned = [at.flip(v.tokens[1], c=1)]
    v.first_far = push_all(at, grad_across(at, v.first_sent, (v.normed2, v.pair_low, first, second)))
    v.first_sent += flip_all(at, v.first_made[-1:])
    v.second_sent = flip_all(at, v.second_made[:-1])
    v.close(at)
    del v.first_made, v.pieces

    v.turned = [at.flip(v.tokens[0], c=1), *v.turned] + [at.flip(t, c=1) for t in v.tokens[2:]]
    v.result_other = at.flip(v.result_other, c=1)
    v.early = add(
        at,
        [v.down_own, v.down_sent[-1], *v.down_far],
        [v.first_own, v.first_sent[-1], *v.first_far],
    )
    v.second_cross = grad_across(at, v.second_sent, (v.normed2, v.pair_low, 0, first))
    v.pieces = add_pieces(at, v.result_own, v.result_other)
    v.branch, v.attended_grad = call(
        at,
        functools.partial(attended_grad_kernel, count),
        [((tokens, width), BF16), ((tokens, part), BF16)],
        *v.tokens,
        *v.turned,
        *v.out_blocks[0],
        steps=tokens // TILE,
        out_tiles={0: rows_of((tokens, width), TILE), 1: rows_of((tokens, part), TILE)},
        name="attended_grad",
    )
    v.close(at)
    del v.first_own, v.first_sent, v.first_far, v.down_own, v.down_sent, v.down_far
    del v.result_own, v.result_other

    v.early = at.swap(v.early, at.groups)
    v.second_far = push_all(at, v.second_cross)
    v.second_sent += flip_all(at, v.second_made[-1:])
    v.result_pieces = [*v.pieces[:3], at.flip(v.pieces[3], x=1)]
    v.out_sent = at.flip(grad_beside(at, (v.branch, v.attended, 0, part), stacked=True), e=1)
    v.mixed_low, v.bias_part = call(
        at,
        attend_back_kernel,
        [((tokens, 3 * part), BF16), ((1, 3 * part), F32)],
        v.attended_grad,
        v.mixed,
        v.sums,
        v.table,
        v.row,
        v.col,
        scratch=[pltpu.VMEM((tokens, part), F32)] * 3,
        name="attend_back",
    )
    v.qkv_made = grad_beside(at, (v.normed, v.mixed_low, 0, 3 * part))
    v.other = expand(at, v.mixed_low, v.qkv_blocks, 1, BF16)
    v.close(at)
    del v.tokens, v.turned, v.second_made, v.second_cross, v.attended_grad

    v.late = at.swap(add(at, [v.second_own, v.second_sent[-1], *v.second_far]), at.groups)
    v.other = at.flip(v.other, c=1)
    v.qkv_sent = flip_all(at, v.qkv_made[:-1])
    v.result_pieces[1] = at.flip(v.result_pieces[1], x=1)
    v.result_terms = pass_pieces(at, v.result_pieces)
    v.out_sent = jnp.split(v.out_sent, at.outer)
    v.out_far = push_all(at, grad_across(at, v.out_sent, (v.branch, v.attended, 0, part)))
    v.qkv_own = grad_own(at, (v.normed, v.mixed_low, 0, 3 * part))
    v.out_own = grad_own(at, (v.branch, v.attended, 0, part))
    v.pieces = expand_pieces(at, v.mixed_low, v.qkv_blocks, v.other)
    v.qkv_cross = grad_across(at, v.qkv_sent, (v.normed, v.mixed_low, 0, 3 * part))
    v.close(at)
    del v.second_own, v.second_sent, v.second_far

    v.qkv_far = push_all(at, v.qkv_cross)
    v.terms = pass_pieces(at, send_pieces(at, v.pieces))
    v.qkv_sent += flip_all(at, v.qkv_made[-1:])
    (v.result,) = call(
        at, result_kernel, [((near, width), BF16)], v.hidden, *v.result_terms, name="result"
    )
    (v.result,) = to_absolute(at, v.result)
    v.gate_grad, v.up_grad = grad_spread(
        at,
        [v.early, v.late],
        (1, 1),
        ((1, 0, first), (0, padded, second)),
        (8 * units,) * 2,
    )
    (v.down_grad,) = grad_spread(at, [v.early], (1,), ((0, 0, units),), (8 * units,))
    bias_part = v.bias_part.reshape(3, 1, part)
    own_slot = (jnp.arange(8) == slot).astype(F32)[None, :, None]
    bias_whole = (bias_part * own_slot).reshape(at.outer, 2, 2, 4, bias_rows).swapaxes(1, 2)
    bias_whole = jnp.roll(bias_whole, -at.a, axis=0)
    bias_whole = pick(at.e, bias_whole, bias_whole[:, ::-1])
    v.small_first = bias_whole.reshape(at.outer, 2, 8, bias_rows)
    v.small_last = jnp.concatenate(
        [g.reshape(at.outer, 2, 8, rows) for g in (v.gain_two_grad, v.shift_two_grad)], axis=-1
    )
    v.close(at)
    del v.other, v.qkv_made, v.pieces

    v.back = at.swap(
        add(
            at,
            [v.qkv_own, v.qkv_sent[-1], *v.qkv_far],
            [v.out_own, v.out_sent[-1], *v.out_far],
        ),
        at.groups,
    )
    v.input_grad, gain_one_grad, shift_one_grad = call(
        at,
        input_kernel,
        [((near, width), F32)] + [((1, width), F32)] * 2,
        v.inputs,
        v.hidden_grad,
        v.gains[0],
        *v.terms,
        name="inputs",
    )
    (input_grad,) = to_absolute(at, v.input_grad)
    v.done = [v.gate_grad, v.up_grad, input_grad]
    grads = [g.reshape(at.outer, 2, 8, rows) for g in (gain_one_grad, shift_one_grad)]
    v.small = jnp.concatenate([v.small_first, *grads, v.small_last], axis=-1)
    v.small = send_small(at, v.small)
    v.close(at)
    gate_wgrad, up_wgrad, input_grad = v.done
    result, down_grad = v.result, v.down_grad
    shares = jnp.sum(at.swap(v.small, at.groups), axis=0)
    qkv_wgrad, out_wgrad = grad_spread(
        at, [v.back], (3, 1), ((0, 0, 4 * part),), (24 * part, 8 * part)
    )

    def share(i):
        return shares[bias_rows + i * rows : bias_rows + (i + 1) * rows]

    return (
        result,
        input_grad,
        share(0),
        share(1),
        qkv_wgrad,
        shares[:bias_rows],
        out_wgrad,
        share(2),
        share(3),
        gate_wgrad,
        up_wgrad,
        down_grad,
    )


def solution(mesh):
    both = ("fsdp", "seq")
    wide = P(both, None)
    flat = P(both)
    return jax.shard_map(
        body,
        mesh=mesh,
        in_specs=(
            wide, P("fsdp", None), P("fsdp"), flat, flat, wide, flat,
            wide, flat, flat, wide, wide, wide, wide,
        ),
        out_specs=(wide, wide, flat, flat, wide, flat, wide, flat, flat, wide, wide, wide),
        check_vma=False,
    )
```

```python
import functools
import math

import jax
import jax.numpy as jnp
from jax import lax
from jax.experimental import pallas as pl
from jax.experimental.pallas import tpu as pltpu
from jax.sharding import PartitionSpec as P

HEADS = 32
HEAD_DIM = 64
AXES = ("fsdp", "seq")
F32 = jnp.float32
BF16 = jnp.bfloat16


def centered_of(values):
    centered = values - jnp.mean(values, axis=-1, keepdims=True)
    spread = jnp.mean(centered * centered, axis=-1, keepdims=True)
    return centered, lax.rsqrt(spread + 1e-05)


def norm_back(values, gain, grad):
    centered, scale = centered_of(values)
    hat = centered * scale
    lifted = grad * gain
    inner = jnp.mean(lifted * hat, axis=-1, keepdims=True)
    pulled = scale * (lifted - jnp.mean(lifted, axis=-1, keepdims=True) - hat * inner)
    return (
        pulled,
        jnp.sum(grad * hat, axis=0, keepdims=True),
        jnp.sum(grad, axis=0, keepdims=True),
    )


def rotary_tables(spots):
    inverse = 10000.0 ** (-jnp.arange(8).astype(F32) / 8.0)
    angle = inverse[:, None] * spots.astype(F32)[None]
    waves = jnp.concatenate([jnp.cos(angle), jnp.sin(angle)], axis=0)
    lane = jnp.arange(2 * HEAD_DIM) % HEAD_DIM
    row = jnp.arange(16)[:, None]
    turn = row - 8
    picks = [
        (row < 8) & (lane < 16) & (lane % 8 == row),
        (lane < 8) & (lane == turn),
        (lane >= 8) & (lane < 16) & (lane - 8 == turn),
    ]
    signs = (1.0, -1.0, 1.0)
    chosen = jnp.concatenate([p.astype(F32) * g for p, g in zip(picks, signs)], axis=1)
    rest = jnp.concatenate([(lane >= 16).astype(F32), jnp.zeros(4 * HEAD_DIM, F32)])
    table = lax.dot_general(
        waves, chosen, (((0,), (0,)), ((), ())), precision=lax.Precision.HIGHEST
    )
    return table + rest


def turned(values, table, sign):
    wide = values.shape[1]
    many = wide // (2 * HEAD_DIM)
    keep, later, earlier = (
        jnp.concatenate([table[:, i * 128 : (i + 1) * 128]] * many, axis=1) for i in range(3)
    )
    partner = pltpu.roll(values, wide - 8, 1) * later + pltpu.roll(values, 8, 1) * earlier
    return values * keep + sign * partner


def dot_rows(left, right, kind=F32):
    return lax.dot_general(
        left, right, (((0,), (0,)), ((), ())), preferred_element_type=F32
    ).astype(kind)


def dot_cols(left, right, kind=F32):
    return lax.dot_general(
        left, right, (((1,), (1,)), ((), ())), preferred_element_type=F32
    ).astype(kind)


def dot(left, right):
    return jnp.dot(left, right, preferred_element_type=F32)


class Places:
    def __init__(self):
        self.fsdp = lax.axis_size("fsdp")
        self.seq = lax.axis_size("seq")
        self.count = self.fsdp * self.seq
        self.outer = self.fsdp // 4
        spot = lax.axis_index("fsdp")
        side = lax.axis_index("seq")
        self.a = spot // 4
        self.b = (spot // 2) % 2
        self.e = spot % 2
        self.x = side // 2
        self.c = side % 2
        self.last = None
        high, low = 2 * self.seq, self.seq
        self.groups = [
            [(a * 4 + e) * low + b * high + i for b in range(2) for i in range(low)]
            for a in range(self.outer)
            for e in range(2)
        ]
        self.sides = [group[c::2] for group in self.groups for c in range(2)]

    def after(self, values):
        if self.last is None:
            return values
        values, self.last = lax.optimization_barrier((values, self.last))
        return values

    def move(self, values, pairs):
        return lax.ppermute(values, AXES, pairs)

    def flip(self, values, c=0, x=0, e=0, b=0):
        mask = c + 2 * x + self.seq * (e + 2 * b)
        return self.move(values, [(i, i ^ mask) for i in range(self.count)])

    def shift(self, values, steps):
        stride = 4 * self.seq * steps
        return self.move(values, [((i + stride) % self.count, i) for i in range(self.count)])

    def push(self, values, steps):
        stride = 4 * self.seq * steps
        return self.move(values, [(i, (i + stride) % self.count) for i in range(self.count)])

    def push_beside(self, values, steps):
        stride = 4 * self.seq * steps
        pairs = [(i, (i + stride) % self.count ^ self.seq) for i in range(self.count)]
        return self.move(values, pairs)

    def swap(self, values, groups):
        parts = len(groups[0])
        view = values.reshape(parts, values.shape[0] // parts, values.shape[1])
        view = lax.all_to_all(view, AXES, 0, 0, axis_index_groups=groups, tiled=True)
        return view.reshape(values.shape)


class Window:
    def close(self, at):
        values, tree = jax.tree.flatten(self.__dict__)
        self.__dict__.update(jax.tree.unflatten(tree, lax.optimization_barrier(values)))
        at.last = None


def pick(bit, first, second):
    return jnp.where(bit == 0, first, second)


def joined(bit, own, other, axis):
    return pick(
        bit, jnp.concatenate([own, other], axis=axis), jnp.concatenate([other, own], axis=axis)
    )


def order_kernel(width, spots_ref, ref, *outs):
    for i in range(ref.shape[1] // width):
        start = pl.multiple_of(spots_ref[i] * width, 128)
        block = ref[:, pl.ds(start, width)]
        for out in outs:
            for k in range(out.shape[0] // ref.shape[0]):
                rows = slice(k * ref.shape[0], (k + 1) * ref.shape[0])
                out[rows, i * width : (i + 1) * width] = block


def reorder(at, spots, values, copies):
    width = values.shape[1] // len(spots)
    if width % 128:
        cols = [lax.dynamic_slice_in_dim(values, spot * width, width, 1) for spot in spots]
        ordered = jnp.concatenate(cols, axis=1)
        return [jnp.concatenate([ordered] * n, axis=0) for n in copies]
    order = jnp.stack(spots).astype(jnp.int32)
    rows, wide = values.shape
    outs = [((n * rows, wide), values.dtype) for n in copies]
    return call(at, functools.partial(order_kernel, width), outs, order, values, name="order")


def to_relative(at, values, copies):
    spots = [
        (((at.a + i) % at.outer) * 2 + k) * 2 + (at.e ^ j)
        for i in range(at.outer)
        for j in range(2)
        for k in range(2)
    ]
    return reorder(at, spots, values, copies)


def to_absolute(at, values):
    spots = [
        (((i - at.a) % at.outer) * 2 + (at.e ^ j)) * 2 + k
        for i in range(at.outer)
        for k in range(2)
        for j in range(2)
    ]
    return reorder(at, spots, values, [1])


def rows_of(shape, rows, index=lambda i: i):
    return pl.BlockSpec((rows, shape[1]), lambda i: (index(i), 0))


def need(args, outs, scratch, tiles, out_tiles):
    total = 6 * 2**20
    for shapes, given in (
        ([(v.shape, v.dtype) for v in args], tiles),
        (list(outs), out_tiles),
        ([(v.shape, v.dtype) for v in scratch], None),
    ):
        for k, (shape, kind) in enumerate(shapes):
            block = given[k].block_shape if given and k in given else shape
            total += math.prod(block) * jnp.dtype(kind).itemsize * (1 + (block is not shape)) * 9 // 8
    return total


def call(at, kernel, outs, *args, steps=1, tiles=None, out_tiles=None, scratch=(), name=None):
    def spec(shape, kind, k, given):
        if given and k in given:
            return given[k]
        if kind == jnp.int32:
            return pl.BlockSpec(memory_space=pltpu.SMEM)
        zeros = (0,) * len(shape)
        return pl.BlockSpec(shape, lambda i: zeros, pipeline_mode=pl.Buffered(1))

    least = min(range(len(args)), key=lambda i: args[i].size)
    in_specs = [spec(v.shape, v.dtype, k, tiles) for k, v in enumerate(args)]
    args = list(args)
    args[least] = at.after(args[least])
    results = pl.pallas_call(
        kernel,
        grid=(steps,),
        out_shape=[jax.ShapeDtypeStruct(shape, kind) for shape, kind in outs],
        in_specs=in_specs,
        out_specs=[spec(shape, kind, k, out_tiles) for k, (shape, kind) in enumerate(outs)],
        scratch_shapes=list(scratch),
        compiler_params=pltpu.CompilerParams(
            vmem_limit_bytes=max(need(args, outs, scratch, tiles, out_tiles), 20 * 2**20)
        ),
        cost_estimate=pl.CostEstimate(flops=0, bytes_accessed=0, transcendentals=0),
        name=name,
    )(*args)
    at.last = min(results, key=lambda v: v.size)
    return results


TILE = 256


def product(values, chunks):
    outs = []
    for blocks in chunks:
        depth = blocks[0].shape[0]
        total = dot(values[:, :depth], blocks[0][...])
        for i, block in enumerate(blocks[1:], 1):
            total = total + dot(values[:, i * depth : (i + 1) * depth], block[...])
        outs.append(total)
    return outs[0] if len(outs) == 1 else jnp.concatenate(outs, axis=1)


def in_chunks(refs, count):
    return [refs[i : i + count] for i in range(0, len(refs), count)]


def transposed_product(values, chunks, j):
    total, col = None, 0
    for blocks in chunks:
        width = blocks[j].shape[1]
        term = dot_cols(values[:, col : col + width], blocks[j][...])
        total = term if total is None else total + term
        col += width
    return total


def tile_of(i):
    return pl.ds(pl.multiple_of(i * TILE, TILE), TILE)


def gathered(pieces, out):
    rows = pieces[0].shape[0]
    for i in range(4):

        @pl.when(pl.program_id(0) == i)
        def _():
            out[:rows, :] = pieces[2 * i][...]
            out[rows:, :] = pieces[2 * i + 1][...]


def attended_grad_kernel(count, *refs):
    pieces, blocks = refs[:8], refs[8:-2]
    whole, grads = refs[-2:]
    gathered(pieces, whole)
    grads[...] = product(whole, in_chunks(blocks, count)).astype(BF16)


def head_of(ref, group, head, start):
    part = ref.shape[1] // 3
    low = group * part + head * HEAD_DIM
    return ref[pl.ds(pl.multiple_of(start, TILE), TILE), low : low + HEAD_DIM]


def both_halves(ref, group, head, start, half):
    return jnp.concatenate(
        [head_of(ref, group, head, start), head_of(ref, group, head, start + half)], axis=0
    )


def allowed_at(row, col, sequence, turn):
    spot = pl.ds(pl.multiple_of(turn * TILE, TILE), TILE)
    ours = jnp.where(sequence == 0, row[0:1, spot], row[1:2, spot])
    theirs = jnp.where(sequence == 0, col[:, 0:1], col[:, 1:2])
    return (theirs == ours) & (col[:, 2:3] <= row[2:3, spot])


def scores_of(key, query, allowed):
    return jnp.where(allowed, dot_cols(key, query), -1e30)


def attention_kernel(count, *refs):
    pieces, blocks = refs[:8], refs[8:-12]
    gain, shift, bias, table, row, col, normed, mixed, attended, sums, tile, low = refs[-12:]
    tiles = pl.num_programs(0) // 2
    half = mixed.shape[0] // 2
    heads = attended.shape[1] // HEAD_DIM
    gathered(pieces, tile)

    @pl.when(pl.program_id(0) < tiles)
    def _():
        centered, scale = centered_of(tile[...].astype(F32))
        low[...] = (centered * scale * gain[...] + shift[...]).astype(BF16)
        normed[...] = low[...]
        turning = mixed.shape[1] * 2 // 3
        values = product(low, in_chunks(blocks, count)) + bias[...]
        both = turned(values[:, :turning], table[...], 1.0).astype(BF16)
        span = tile_of(pl.program_id(0))
        mixed[span, : turning // 2] = both[:, : turning // 2] * 0.125
        mixed[span, turning // 2 : turning] = both[:, turning // 2 :]
        mixed[span, turning:] = values[:, turning:].astype(BF16)

    @pl.when(pl.program_id(0) >= tiles)
    def _():
        i = pl.program_id(0) - tiles
        sequence, turn = i // 2, i % 2
        allowed = allowed_at(row, col, sequence, turn)
        start = turn * half + sequence * TILE
        span = pl.ds(pl.multiple_of(start, TILE), TILE)
        for h in range(heads):
            key = both_halves(mixed, 1, h, sequence * TILE, half)
            value = both_halves(mixed, 2, h, sequence * TILE, half)
            scores = scores_of(key, head_of(mixed, 0, h, start), allowed)
            top = jnp.max(scores, axis=0, keepdims=True)
            expo = jnp.exp(scores - top)
            total = jnp.sum(expo, axis=0, keepdims=True)
            out = jnp.transpose(dot_rows(value, (expo * (1.0 / total)).astype(BF16)))
            attended[span, h * HEAD_DIM : (h + 1) * HEAD_DIM] = out.astype(BF16)
            sums[pl.ds(i * heads + h, 1), :] = top + jnp.log(total)


def attend_back_kernel(
    grads, mixed, sums, table, row, col, low, bias, query_sum, key_sum, value_sum
):
    half = mixed.shape[0] // 2
    part = grads.shape[1]
    heads = part // HEAD_DIM

    for sequence in range(2):
        for turn in range(2):
            i = sequence * 2 + turn
            allowed = allowed_at(row, col, sequence, turn)
            start = turn * half + sequence * TILE
            span = pl.ds(start, TILE)
            for h in range(heads):
                cols = slice(h * HEAD_DIM, (h + 1) * HEAD_DIM)
                query = head_of(mixed, 0, h, start)
                key = both_halves(mixed, 1, h, sequence * TILE, half)
                value = both_halves(mixed, 2, h, sequence * TILE, half)
                grad = grads[span, cols]
                scores = scores_of(key, query, allowed)
                probs = jnp.exp(scores - sums[i * heads + h : i * heads + h + 1, :])
                probs_grad = dot_cols(value, grad)
                value_grad = dot(probs.astype(BF16), grad)
                center = jnp.sum(probs * probs_grad, axis=0, keepdims=True)
                scores_low = (probs * (probs_grad - center)).astype(BF16)
                key_grad = dot(scores_low, query)
                query_sum[span, cols] = jnp.transpose(dot_rows(key, scores_low))
                for k in range(2):
                    keys = pl.ds(k * half + sequence * TILE, TILE)
                    rows = slice(k * TILE, (k + 1) * TILE)
                    if turn == 0:
                        key_sum[keys, cols] = key_grad[rows]
                        value_sum[keys, cols] = value_grad[rows]
                    else:
                        key_sum[keys, cols] += key_grad[rows]
                        value_sum[keys, cols] += value_grad[rows]

    bias[...] = jnp.zeros_like(bias)

    @pl.loop(0, mixed.shape[0] // TILE)
    def _(i):
        span = tile_of(i)
        factors = table[span, :]
        for k, ref in enumerate((query_sum, key_sum, value_sum)):
            values = ref[span, :]
            if k == 0:
                values = values * 0.125
            if k < 2:
                values = turned(values, factors, -1.0)
            values = values.astype(BF16)
            low[span, k * part : (k + 1) * part] = values
            bias[:, k * part : (k + 1) * part] += jnp.sum(
                values.astype(F32), axis=0, keepdims=True
            )


def expand_kernel(count, values, *refs):
    *blocks, out = refs
    chunks = in_chunks(blocks, count)
    width = blocks[0].shape[0]
    for j in range(count):
        total = transposed_product(values, chunks, j)
        out[:, j * width : (j + 1) * width] = total.astype(out.dtype)


def total_of(terms):
    total = terms[0][...].astype(F32)
    for term in terms[1:]:
        total = total + term[...].astype(F32)
    return total


def hidden_kernel(inputs, gain, shift, *refs):
    *terms, hidden, normed = refs
    values = inputs[...].astype(F32) + total_of(terms)
    hidden[...] = values
    centered, scale = centered_of(values)
    normed[...] = (centered * scale * gain[...] + shift[...]).astype(BF16)


def result_kernel(hidden, *refs):
    *terms, out = refs
    out[...] = (hidden[...] + total_of(terms)).astype(BF16)


def branch_kernel(hidden, cotangent, gain, *refs):
    *terms, grad, low, gain_grad, shift_grad = refs
    pulled, gain_grad[...], shift_grad[...] = norm_back(hidden[...], gain[...], total_of(terms))
    values = cotangent[...].astype(F32) + pulled
    grad[...] = values
    low[...] = values.astype(BF16)


def input_kernel(inputs, hidden_grad, gain, *refs):
    *terms, grad, gain_grad, shift_grad = refs
    pulled, gain_grad[...], shift_grad[...] = norm_back(
        inputs[...].astype(F32), gain[...], total_of(terms)
    )
    grad[...] = hidden_grad[...] + pulled


def mlp_kernel(count, *refs):
    pieces, blocks = refs[:8], refs[8:-4]
    normed, inner, gate_factor, up_factor = refs[-4:]
    units = gate_factor.shape[1]
    gathered(pieces, normed)
    values = product(normed, in_chunks(blocks, count))
    gate, up = values[:, :units], values[:, units:]
    sigmoid = 1.0 / (1.0 + jnp.exp(-gate))
    silu = gate * sigmoid
    inner[:, :units] = (silu * up).astype(BF16)
    if inner.shape[1] > units:
        inner[:, units:] = jnp.zeros((inner.shape[0], inner.shape[1] - units), BF16)
    gate_factor[...] = up * sigmoid * (1.0 + gate * (1.0 - sigmoid))
    up_factor[...] = silu


def mlp_back_kernel(count, grads, *refs):
    *blocks, gate_factor, up_factor, pair = refs
    values = product(grads, in_chunks(blocks, count))[:, : gate_factor.shape[1]]
    pair[...] = jnp.concatenate(
        [(values * gate_factor[...]).astype(BF16), (values * up_factor[...]).astype(BF16)],
        axis=1,
    )


def segments(widths, chunks):
    out = []
    at_part = at_chunk = part = chunk = 0
    while part < len(widths):
        size = min(widths[part] - at_part, chunks[chunk] - at_chunk)
        out.append((part, at_part, chunk, at_chunk, size))
        at_part, at_chunk = at_part + size, at_chunk + size
        if at_part == widths[part]:
            part, at_part = part + 1, 0
        if at_chunk == chunks[chunk]:
            chunk, at_chunk = chunk + 1, 0
    return out


def part_list(refs, counts):
    return [
        (ref, p, ref.shape[1] // (8 * count)) for ref, count in zip(refs, counts) for p in range(count)
    ]


def cut_kernel(counts, *refs):
    *weights, out = refs
    rows = weights[0].shape[0]
    col = 0
    for ref, p, width in part_list(weights, counts):
        for j in range(8):
            start = (p * 8 + j) * width
            out[j * rows : (j + 1) * rows, col : col + width] = ref[:, start : start + width]
        col += width
    if col < out.shape[1]:
        out[:, col:] = jnp.zeros((out.shape[0], out.shape[1] - col), BF16)


def spread_kernel(counts, strips, *refs):
    chunks, outs = refs[: -len(counts)], refs[-len(counts) :]
    rows = outs[0].shape[0]
    parts = part_list(outs, counts)
    cuts = segments([width for _, _, width in parts], [width for _, _, width in strips])
    for part, begin, strip, col, size in cuts:
        ref, p, width = parts[part]
        chunk, first, _ = strips[strip]
        for j in range(8):
            start = (p * 8 + j) * width + begin
            piece = chunks[chunk][j * rows : (j + 1) * rows, first + col : first + col + size]
            ref[:, start : start + size] = piece.astype(F32)


def sum_kernel(counts, *refs):
    *terms, out = refs
    col = 0
    for count in counts:
        mine, terms = terms[:count], terms[count:]
        total = mine[0][...].astype(F32)
        for term in mine[1:]:
            total = total + term[...].astype(F32)
        out[:, col : col + total.shape[1]] = total.astype(BF16)
        col += total.shape[1]


def cut_rows(at, weights, counts, wide):
    (out,) = call(
        at,
        functools.partial(cut_kernel, counts),
        [((8 * weights[0].shape[0], wide), BF16)],
        *weights,
        name="cut",
    )
    return out


def split_kernel(col, whole, *outs):
    for out in outs:
        out[...] = whole[:, col : col + out.shape[1]]
        col += out.shape[1]


def split(at, whole, begin, widths):
    outs = [((whole.shape[0], n), BF16) for n in widths]
    return call(at, functools.partial(split_kernel, begin), outs, whole, name="split")


def cross_block(at, block):
    return [block] + [at.shift(block, i) for i in range(1, at.outer)]


def merge_blocks(across, beside):
    return [block for pair in zip(across, beside) for block in pair]


def send_block(at, block):
    return [block] + [at.shift(block, i) for i in range(1, at.outer)]


def grad_kernel(count, ways, *refs):
    many = 2 * len(ways)
    pairs, addends, outs = refs[:many], refs[many : many + count], refs[many + count :]
    each = pl.num_programs(0) // len(outs)
    for k, out in enumerate(outs):

        @pl.when(pl.program_id(0) // each == k)
        def _():
            col = 0
            for i, (begin, size) in enumerate(ways):
                values, grads = pairs[2 * i : 2 * i + 2]
                total = dot_rows(values[...], grads[:, begin : begin + size])
                if k < count:
                    total = total + addends[k][:, col : col + size].astype(F32)
                out[:, col : col + size] = total.astype(out.dtype)
                col += size


def grad_blocks(at, ways, spots, kind, addends=(), stacked=False):
    tokens, wide = ways[0][0].shape
    width = wide // (2 * at.outer)
    tile = min(TILE, width)
    each = width // tile

    def column(i):
        spot = spots[0]
        for k in range(1, len(spots)):
            spot = jnp.where(i // each == k, spots[k], spot)
        return spot * each + i % each

    def row_of(k):
        return lambda i: jnp.clip(i - k * each, 0, each - 1)

    shape = (width, sum(way[3] for way in ways))
    tiles = {2 * i: pl.BlockSpec((tokens, tile), lambda i: (0, column(i))) for i in range(len(ways))}
    for k in range(len(addends)):
        tiles[2 * len(ways) + k] = rows_of(shape, tile, row_of(k))
    kernel = functools.partial(grad_kernel, len(addends), tuple(way[2:] for way in ways))
    if stacked:
        shape = (width * len(spots), shape[1])
        return call(
            at,
            kernel,
            [(shape, kind)],
            *[v for way in ways for v in way[:2]],
            steps=len(spots) * each,
            tiles=tiles,
            out_tiles={0: rows_of(shape, tile)},
            name="grad",
        )[0]
    return call(
        at,
        kernel,
        [(shape, kind)] * len(spots),
        *[v for way in ways for v in way[:2]],
        *addends,
        steps=len(spots) * each,
        tiles=tiles,
        out_tiles={k: rows_of(shape, tile, row_of(k)) for k in range(len(spots))},
        name="grad",
    )


def grad_beside(at, *way, stacked=False):
    order = list(range(1, at.outer)) + [0]
    return grad_blocks(at, way, [2 * i + 1 for i in order], BF16, stacked=stacked)


def grad_own(at, *way):
    return grad_blocks(at, way, [0], F32)[0]


def grad_across(at, sent, *way):
    if at.outer == 1:
        return []
    return grad_blocks(at, way, [2 * i for i in range(1, at.outer)], BF16, sent[: at.outer - 1])


def push_all(at, made):
    return [at.push(v, i) for i, v in enumerate(made, 1)]


def flip_all(at, made):
    return [at.flip(v, e=1) for v in made]


def grad_spread(at, chunks, counts, strips, widths):
    rows = chunks[0].shape[0] // 8
    return call(
        at,
        functools.partial(spread_kernel, counts, strips),
        [((rows, n), F32) for n in widths],
        *chunks,
        name="spread",
    )


def join_kernel(*refs):
    *pieces, out = refs
    rows = pieces[0].shape[0]
    for i, piece in enumerate(pieces):
        out[i * rows : (i + 1) * rows, :] = piece[...]


def joined_rows(at, pieces):
    shape = (8 * pieces[0].shape[0], pieces[0].shape[1])
    (out,) = call(at, join_kernel, [(shape, BF16)], *pieces, name="join")
    return out


def spread_tokens(at, values):
    low = at.flip(values, b=1)
    beside = at.flip(values, x=1)
    return [values, beside, low, at.flip(low, x=1)]


def send_pieces(at, pieces):
    return [pieces[0], at.flip(pieces[1], x=1), pieces[2], at.flip(pieces[3], x=1)]


def pass_pieces(at, pieces):
    return [pieces[0], pieces[1], at.flip(add(at, pieces[2:]), b=1)]


def expand_add_kernel(count, values, *refs):
    blocks, other, outs = refs[:-5], refs[-5], refs[-4:]
    chunks = in_chunks(blocks, count)
    width = blocks[0].shape[0]
    rows = outs[0].shape[0]
    for j in range(count):
        cols = slice(j * width, (j + 1) * width)
        total = transposed_product(values, chunks, j) + other[:, cols].astype(F32)
        total = total.astype(BF16)
        for i in range(2):

            @pl.when(pl.program_id(0) == i)
            def _():
                outs[2 * i][:, cols] = total[:rows]
                outs[2 * i + 1][:, cols] = total[rows:]


def expand_pieces(at, values, chunks, other):
    blocks = [block for chunk in chunks for block in chunk]
    shape = (other.shape[0] // 4, other.shape[1])
    return call(
        at,
        functools.partial(expand_add_kernel, len(chunks[0])),
        [(shape, BF16)] * 4,
        values,
        *blocks,
        other,
        steps=other.shape[0] // TILE,
        tiles={
            0: rows_of(values.shape, TILE),
            1 + len(blocks): rows_of(other.shape, TILE),
        },
        name="expand_add",
    )


def add_pieces_kernel(own, other, *outs):
    rows = outs[0].shape[0]
    for d, out in enumerate(outs):
        span = slice(d * rows, (d + 1) * rows)
        out[...] = (own[span, :] + other[span, :].astype(F32)).astype(BF16)


def add_pieces(at, own, other):
    shape = (own.shape[0] // 4, own.shape[1])
    return call(at, add_pieces_kernel, [(shape, BF16)] * 4, own, other, name="pieces")


def expand(at, values, chunks, side, kind):
    half = values.shape[0] // 2
    blocks = [block for chunk in chunks for block in chunk]
    count = len(chunks[0])
    shape = (half, blocks[0].shape[0] * count)
    steps = half // TILE
    (out,) = call(
        at,
        functools.partial(expand_kernel, count),
        [(shape, kind)],
        values,
        *blocks,
        steps=steps,
        tiles={0: rows_of(values.shape, TILE, lambda i: i + side * steps)},
        out_tiles={0: rows_of(shape, TILE)},
        name="expand",
    )
    return out


def add(at, *sums):
    rows = sums[0][0].shape[0]
    tile = min(TILE, rows)
    terms = [v for each in sums for v in each]
    shape = (rows, sum(each[0].shape[1] for each in sums))
    (total,) = call(
        at,
        functools.partial(sum_kernel, tuple(len(each) for each in sums)),
        [(shape, BF16)],
        *terms,
        steps=rows // tile,
        tiles={k: rows_of(v.shape, tile) for k, v in enumerate(terms)},
        out_tiles={0: rows_of(shape, tile)},
        name="add",
    )
    return total


def send_small(at, values):
    total = values[0, 0] + at.flip(values[0, 1], e=1)
    for i in range(1, at.outer):
        total = total + at.push(values[i, 0], i)
        total = total + at.push_beside(values[i, 1], i)
    return total


def order_tokens(at, values):
    seqs, length = values.shape
    view = values.reshape(seqs, 2, 2, length // 4)
    view = pick(at.x, view, view[:, ::-1])
    view = pick(at.c, view, view[:, :, ::-1])
    return jnp.swapaxes(view, 1, 2).reshape(seqs, length)


def body(
    layer_input,
    segment_ids,
    positions,
    ln1_gain,
    ln1_bias,
    qkv_weight,
    qkv_bias,
    out_weight,
    ln2_gain,
    ln2_bias,
    gate_weight,
    up_weight,
    down_weight,
    cotangent,
):
    at = Places()
    width = layer_input.shape[1]
    rows = qkv_weight.shape[0]
    bias_rows = qkv_bias.shape[0]
    length = segment_ids.shape[1]
    heads_here = HEADS // 8
    part = width // 8
    units = gate_weight.shape[1] // 8
    slot = at.b * 4 + at.x * 2 + at.c

    tokens = 2 * length
    count = 2 * at.outer
    near = layer_input.shape[0]

    second = 2 * units // 256 * 128
    first = 2 * units - second
    v = Window()
    padded = (units + 127) // 128 * 128
    thin, wide = (tokens, units), (tokens, 2 * units)

    (v.cotangent,) = to_relative(at, cotangent, [1])
    v.cotangent_near = [at.flip(v.cotangent, x=1), at.flip(v.cotangent, b=1)]
    v.front = at.swap(cut_rows(at, [qkv_weight, out_weight], (3, 1), 4 * part), at.groups)
    v.small = jnp.concatenate([at.after(qkv_bias), ln1_gain, ln1_bias, ln2_gain, ln2_bias])[None]
    v.small = joined(at.c, v.small, at.flip(v.small, c=1), 0)
    v.small = jnp.stack([v.small, at.flip(v.small, e=1)])
    v.small = jnp.stack([v.small] + [at.shift(v.small, i) for i in range(1, at.outer)])
    (v.inputs,) = to_relative(at, layer_input, [1])
    v.first, v.later = split(
        at,
        cut_rows(at, [gate_weight, up_weight, down_weight], (1, 1, 1), 2 * units + padded),
        0,
        (first, second + padded),
    )
    spots = jnp.concatenate([segment_ids, positions[None]], axis=0)[None]
    v.spots = jnp.concatenate([spots, at.flip(spots, b=1)], axis=0)
    v.close(at)

    v.qkv, v.out = split(at, v.front, 0, (3 * part, part))
    del v.front
    v.qkv_across = cross_block(at, v.qkv)
    v.qkv_beside = [at.flip(v.qkv, e=1)]
    v.tokens = spread_tokens(at, v.inputs)
    v.turned = [at.flip(v.tokens[1], c=1)]
    v.small = joined(at.x, v.small, at.flip(v.small, x=1), 2)
    v.small = joined(at.b, v.small, at.flip(v.small, b=1), 2)
    segments_here = order_tokens(at, v.spots[:, 0])
    places = order_tokens(at, v.spots[:, 1])
    index = order_tokens(at, jnp.arange(length)[None])
    v.row = jnp.concatenate([segments_here, index, jnp.zeros((5, length), index.dtype)], axis=0)
    v.row = v.row.astype(F32)
    v.col = jnp.pad(jnp.transpose(v.row), ((0, 0), (0, 120)))
    places = places.reshape(2, 2, length // 2).swapaxes(0, 1).reshape(2 * length)
    v.table = rotary_tables(places)
    v.close(at)

    v.qkv_beside += flip_all(at, v.qkv_across[1:])
    v.turned = [at.flip(v.tokens[0], c=1), *v.turned] + [at.flip(t, c=1) for t in v.tokens[2:]]
    v.out_across = cross_block(at, v.out)
    v.first = at.swap(v.first, at.groups)


    def vector(i):
        start = bias_rows + i * rows
        return v.small[..., start : start + rows].reshape(1, width).astype(F32)

    v.gains = [vector(i) for i in range(4)]
    bias = v.small[..., :bias_rows]
    bias = pick(at.e, bias, bias[:, ::-1])
    bias = jnp.roll(bias, at.a, axis=0)
    bias = bias.reshape(at.outer, 2, 2, 4, bias_rows).swapaxes(1, 2).reshape(3, 8, part)
    bias = lax.dynamic_index_in_dim(bias, slot, 1, keepdims=False)
    v.bias = bias.reshape(1, 3 * part).astype(F32)
    v.close(at)
    v.qkv_blocks = [merge_blocks(v.qkv_across, v.qkv_beside)]
    del v.qkv_across, v.qkv_beside, v.qkv, v.small, v.spots

    v.first_across = cross_block(at, v.first)
    v.first_beside = [at.flip(v.first, e=1)]
    v.out_beside = flip_all(at, v.out_across)
    v.cotangent_near.append(at.flip(v.cotangent_near[1], x=1))
    v.later = at.swap(v.later, at.groups)
    steps = tokens // TILE
    v.normed, v.mixed, v.attended, v.sums = call(
        at,
        functools.partial(attention_kernel, count),
        [
            ((tokens, width), BF16),
            ((tokens, 3 * part), BF16),
            ((tokens, part), BF16),
            ((4 * heads_here, TILE), F32),
        ],
        *v.tokens,
        *v.turned,
        *v.qkv_blocks[0],
        v.gains[0],
        v.gains[1],
        v.bias,
        v.table,
        v.row,
        v.col,
        steps=2 * steps,
        tiles={11 + count: rows_of(v.table.shape, TILE, lambda i: jnp.minimum(i, steps - 1))},
        out_tiles={0: rows_of((tokens, width), TILE, lambda i: jnp.minimum(i, steps - 1))},
        scratch=[pltpu.VMEM((TILE, width), BF16)] * 2,
        name="attention",
    )
    v.out_blocks = [merge_blocks(v.out_across, v.out_beside)]
    v.other = expand(at, v.attended, v.out_blocks, 1, BF16)
    v.close(at)
    del v.out_across, v.out_beside, v.out

    v.other = at.flip(v.other, c=1)
    v.cotangent_far = [at.flip(t, c=1) for t in (v.cotangent, *v.cotangent_near)]
    v.second, v.down = split(at, v.later, 0, (second, padded))
    v.pieces = expand_pieces(at, v.attended, v.out_blocks, v.other)
    v.close(at)
    del v.later

    v.terms = pass_pieces(at, send_pieces(at, v.pieces))
    v.cotangent_all = joined_rows(at, [v.cotangent, *v.cotangent_near, *v.cotangent_far])
    v.second_across = cross_block(at, v.second)
    v.second_beside = [at.flip(v.second, e=1)]
    v.first_beside += flip_all(at, v.first_across[1:])
    v.close(at)
    del v.other, v.pieces, v.cotangent_near, v.cotangent_far

    v.hidden, normed2 = call(
        at,
        hidden_kernel,
        [((near, width), F32), ((near, width), BF16)],
        v.inputs,
        v.gains[2],
        v.gains[3],
        *v.terms,
        name="hidden",
    )
    v.tokens = spread_tokens(at, normed2)
    v.turned = [at.flip(v.tokens[1], c=1)]
    v.down_across = cross_block(at, v.down)
    v.down_beside = [at.flip(v.down, e=1)]
    v.second_beside += flip_all(at, v.second_across[1:])
    v.close(at)
    v.pair_blocks = [
        merge_blocks(v.first_across, v.first_beside),
        merge_blocks(v.second_across, v.second_beside),
    ]
    del v.first_across, v.first_beside, v.second_across, v.second_beside, v.first, v.second

    v.turned = [at.flip(v.tokens[0], c=1), *v.turned] + [at.flip(t, c=1) for t in v.tokens[2:]]
    v.down_beside += flip_all(at, v.down_across[1:])
    v.normed2, v.inner, v.gate_factor, v.up_factor = call(
        at,
        functools.partial(mlp_kernel, count),
        [((tokens, width), BF16), ((tokens, padded), BF16), (thin, F32), (thin, F32)],
        *v.tokens,
        *v.turned,
        *v.pair_blocks[0],
        *v.pair_blocks[1],
        steps=tokens // TILE,
        out_tiles={0: rows_of((tokens, width), TILE)}
        | {1: rows_of((tokens, padded), TILE)}
        | {k: rows_of(thin, TILE) for k in (2, 3)},
        name="mlp",
    )
    v.down_made = grad_beside(at, (v.cotangent_all, v.inner, 0, padded))
    v.close(at)
    v.down_blocks = [merge_blocks(v.down_across, v.down_beside)]
    del v.down_across, v.down_beside, v.down, v.tokens, v.turned

    v.down_sent = flip_all(at, v.down_made[:-1])
    (v.pair_low,) = call(
        at,
        functools.partial(mlp_back_kernel, count),
        [(wide, BF16)],
        v.cotangent_all,
        *v.down_blocks[0],
        v.gate_factor,
        v.up_factor,
        steps=tokens // TILE,
        tiles={
            0: rows_of((tokens, width), TILE),
            1 + count: rows_of(thin, TILE),
            2 + count: rows_of(thin, TILE),
        },
        out_tiles={0: rows_of(wide, TILE)},
        name="mlp_back",
    )
    v.other = expand(at, v.pair_low, v.pair_blocks, 1, BF16)
    v.own = expand(at, v.pair_low, v.pair_blocks, 0, F32)
    v.down_own = grad_own(at, (v.cotangent_all, v.inner, 0, padded))
    v.close(at)

    v.other = at.flip(v.other, c=1)
    v.down_cross = grad_across(at, v.down_sent, (v.cotangent_all, v.inner, 0, padded))
    v.first_made = grad_beside(at, (v.normed2, v.pair_low, first, second))
    v.pieces = add_pieces(at, v.own, v.other)
    v.close(at)

    v.terms = pass_pieces(at, send_pieces(at, v.pieces))
    v.down_far = push_all(at, v.down_cross)
    v.down_sent += flip_all(at, v.down_made[-1:])
    v.first_sent = flip_all(at, v.first_made[:-1])
    v.second_made = grad_beside(at, (v.normed2, v.pair_low, 0, first))
    v.first_own = grad_own(at, (v.normed2, v.pair_low, first, second))
    v.second_own = grad_own(at, (v.normed2, v.pair_low, 0, first))
    v.result_other = expand(at, v.inner, v.down_blocks, 1, BF16)
    v.result_own = expand(at, v.inner, v.down_blocks, 0, F32)
    v.close(at)
    del v.down_cross, v.down_made, v.own, v.other

    v.hidden_grad, branch, v.gain_two_grad, v.shift_two_grad = call(
        at,
        branch_kernel,
        [((near, width), F32), ((near, width), BF16)] + [((1, width), F32)] * 2,
        v.hidden,
        v.cotangent,
        v.gains[2],
        *v.terms,
        name="branch",
    )
    v.tokens = spread_tokens(at, branch)
    v.turned = [at.flip(v.tokens[1], c=1)]
    v.first_far = push_all(at, grad_across(at, v.first_sent, (v.normed2, v.pair_low, first, second)))
    v.first_sent += flip_all(at, v.first_made[-1:])
    v.second_sent = flip_all(at, v.second_made[:-1])
    v.close(at)
    del v.first_made, v.pieces

    v.turned = [at.flip(v.tokens[0], c=1), *v.turned] + [at.flip(t, c=1) for t in v.tokens[2:]]
    v.result_other = at.flip(v.result_other, c=1)
    v.early = add(
        at,
        [v.down_own, v.down_sent[-1], *v.down_far],
        [v.first_own, v.first_sent[-1], *v.first_far],
    )
    v.second_cross = grad_across(at, v.second_sent, (v.normed2, v.pair_low, 0, first))
    v.pieces = add_pieces(at, v.result_own, v.result_other)
    v.branch, v.attended_grad = call(
        at,
        functools.partial(attended_grad_kernel, count),
        [((tokens, width), BF16), ((tokens, part), BF16)],
        *v.tokens,
        *v.turned,
        *v.out_blocks[0],
        steps=tokens // TILE,
        out_tiles={0: rows_of((tokens, width), TILE), 1: rows_of((tokens, part), TILE)},
        name="attended_grad",
    )
    v.out_made = grad_beside(at, (v.branch, v.attended, 0, part), stacked=True)
    v.close(at)
    del v.first_own, v.first_sent, v.first_far, v.down_own, v.down_sent, v.down_far
    del v.result_own, v.result_other

    v.early = at.swap(v.early, at.groups)
    v.second_far = push_all(at, v.second_cross)
    v.second_sent += flip_all(at, v.second_made[-1:])
    v.result_pieces = [*v.pieces[:3], at.flip(v.pieces[3], x=1)]
    v.out_sent = at.flip(v.out_made, e=1)
    v.mixed_low, v.bias_part = call(
        at,
        attend_back_kernel,
        [((tokens, 3 * part), BF16), ((1, 3 * part), F32)],
        v.attended_grad,
        v.mixed,
        v.sums,
        v.table,
        v.row,
        v.col,
        scratch=[pltpu.VMEM((tokens, part), F32)] * 3,
        name="attend_back",
    )
    v.qkv_made = grad_beside(at, (v.normed, v.mixed_low, 0, 3 * part))
    v.other = expand(at, v.mixed_low, v.qkv_blocks, 1, BF16)
    v.close(at)
    del v.tokens, v.turned, v.second_made, v.second_cross, v.attended_grad

    v.late = at.swap(add(at, [v.second_own, v.second_sent[-1], *v.second_far]), at.groups)
    v.other = at.flip(v.other, c=1)
    v.qkv_sent = flip_all(at, v.qkv_made[:-1])
    v.result_pieces[1] = at.flip(v.result_pieces[1], x=1)
    v.result_terms = pass_pieces(at, v.result_pieces)
    v.out_sent = jnp.split(v.out_sent, at.outer)
    v.out_far = push_all(at, grad_across(at, v.out_sent, (v.branch, v.attended, 0, part)))
    v.qkv_own = grad_own(at, (v.normed, v.mixed_low, 0, 3 * part))
    v.out_own = grad_own(at, (v.branch, v.attended, 0, part))
    v.pieces = expand_pieces(at, v.mixed_low, v.qkv_blocks, v.other)
    v.qkv_cross = grad_across(at, v.qkv_sent, (v.normed, v.mixed_low, 0, 3 * part))
    v.close(at)
    del v.second_own, v.second_sent, v.second_far

    v.qkv_far = push_all(at, v.qkv_cross)
    v.terms = pass_pieces(at, send_pieces(at, v.pieces))
    v.qkv_sent += flip_all(at, v.qkv_made[-1:])
    (v.result,) = call(
        at, result_kernel, [((near, width), BF16)], v.hidden, *v.result_terms, name="result"
    )
    (v.result,) = to_absolute(at, v.result)
    v.gate_grad, v.up_grad = grad_spread(
        at,
        [v.early, v.late],
        (1, 1),
        ((1, 0, first), (0, padded, second)),
        (8 * units,) * 2,
    )
    (v.down_grad,) = grad_spread(at, [v.early], (1,), ((0, 0, units),), (8 * units,))
    bias_part = v.bias_part.reshape(3, 1, part)
    own_slot = (jnp.arange(8) == slot).astype(F32)[None, :, None]
    bias_whole = (bias_part * own_slot).reshape(at.outer, 2, 2, 4, bias_rows).swapaxes(1, 2)
    bias_whole = jnp.roll(bias_whole, -at.a, axis=0)
    bias_whole = pick(at.e, bias_whole, bias_whole[:, ::-1])
    v.small_first = bias_whole.reshape(at.outer, 2, 8, bias_rows)
    v.small_last = jnp.concatenate(
        [g.reshape(at.outer, 2, 8, rows) for g in (v.gain_two_grad, v.shift_two_grad)], axis=-1
    )
    v.close(at)
    del v.other, v.qkv_made, v.pieces

    v.back = at.swap(
        add(
            at,
            [v.qkv_own, v.qkv_sent[-1], *v.qkv_far],
            [v.out_own, v.out_sent[-1], *v.out_far],
        ),
        at.groups,
    )
    v.input_grad, gain_one_grad, shift_one_grad = call(
        at,
        input_kernel,
        [((near, width), F32)] + [((1, width), F32)] * 2,
        v.inputs,
        v.hidden_grad,
        v.gains[0],
        *v.terms,
        name="inputs",
    )
    (input_grad,) = to_absolute(at, v.input_grad)
    v.done = [v.gate_grad, v.up_grad, input_grad]
    grads = [g.reshape(at.outer, 2, 8, rows) for g in (gain_one_grad, shift_one_grad)]
    v.small = jnp.concatenate([v.small_first, *grads, v.small_last], axis=-1)
    v.small = send_small(at, v.small)
    v.close(at)
    gate_wgrad, up_wgrad, input_grad = v.done
    result, down_grad = v.result, v.down_grad
    shares = jnp.sum(at.swap(v.small, at.groups), axis=0)
    qkv_wgrad, out_wgrad = grad_spread(
        at, [v.back], (3, 1), ((0, 0, 4 * part),), (24 * part, 8 * part)
    )

    def share(i):
        return shares[bias_rows + i * rows : bias_rows + (i + 1) * rows]

    return (
        result,
        input_grad,
        share(0),
        share(1),
        qkv_wgrad,
        shares[:bias_rows],
        out_wgrad,
        share(2),
        share(3),
        gate_wgrad,
        up_wgrad,
        down_grad,
    )


def solution(mesh):
    both = ("fsdp", "seq")
    wide = P(both, None)
    flat = P(both)
    return jax.shard_map(
        body,
        mesh=mesh,
        in_specs=(
            wide, P("fsdp", None), P("fsdp"), flat, flat, wide, flat,
            wide, flat, flat, wide, wide, wide, wide,
        ),
        out_specs=(wide, wide, flat, flat, wide, flat, wide, flat, flat, wide, wide, wide),
        check_vma=False,
    )
```
